512 devices in a mesh: exp: 64 (over x, z), rep: 8 (over y, core).
Axes of the slice: x: 4, y: 4, z: 16, core: 2. Of those that a mesh axis runs over, the one named last changes fastest.
Arguments:
- latent: bfloat16 [128, 16, 64], P('exp'), may hold values from -6 to 6
- stem_weight: bfloat16 [144, 1536], replicated, may hold values from -0.5 to 0.5
- norm_gain: float32 [1536], replicated, may hold values from 0.4 to 1.6
- router_weight: bfloat16 [1536, 8], replicated, may hold values from -0.15625 to 0.15625
- routes: int32 [8192, 2], P('exp'), may hold values from 0 to 7, all different within a row; in each aligned block of 128 rows (0 to 127, 128 to 255, ...) at most 40 rows name the same one
- gate_weight: bfloat16 [1536, 24576], P('rep', 'exp'), may hold values from -0.15625 to 0.15625
- up_weight: bfloat16 [1536, 24576], P('rep', 'exp'), may hold values from -0.15625 to 0.15625
- down_weight: bfloat16 [24576, 1536], P('exp', 'rep'), may hold values from -0.109375 to 0.109375
- grad_mixed: bfloat16 [8192, 1536], P('exp'), may hold values from -6 to 6
Outputs:
- mixed: bfloat16 [8192, 1536], P('exp')
- grad_latent: float32 [128, 16, 64], P('exp')
- grad_gate: float32 [1536, 24576], P('rep', 'exp')
- grad_up: float32 [1536, 24576], P('rep', 'exp')
- grad_down: float32 [24576, 1536], P('exp', 'rep')
The draws below stay inside these ranges and needn't reach their ends.
Inputs may be any that keep to these rules, and one draw needn't show every extreme that they name: `routes`: A token's 2 experts differ. Within the 128 tokens of one device, no expert is named more than 40 times, and in every draw some device's tokens name some expert exactly 40 times.
All inputs are finite; a program needn't handle non-finite values.
Results may differ from the reference program's by a relative error of at most 0.023.
Values may be sent and summed in bfloat16 or wider, within the bound.
A program may use at most 64 MiB of HBM per device.

```python
import math
import jax
import jax.numpy as jnp
import numpy as np
from jax import lax

D = 1536
EXPERTS = 8
FF = 3072
TOPK = 2
C_IN = 16
WID = 64
TOK_DEV = 128
CAP = 40
SUB = 5
SHARDS = 8
HID = 384
HGT = 128
TOKENS = 8192
N_EXP = 64
N_REP = 8


def shard_levels(stream_key, shape, shards, least, largest):
    def one(axis_at, shards_of):
        heights = jax.random.uniform(jax.random.fold_in(jax.random.fold_in(stream_key, 6), axis_at), (shards_of,), jnp.float32, least / len(shards), largest / len(shards))
        return jnp.repeat(jnp.exp(heights), shape[axis_at] // shards_of).reshape((-1,) + (1,) * (len(shape) - axis_at - 1))

    loudness = one(*shards[0])
    for cut in shards[1:]:
        loudness = loudness * one(*cut)
    return loudness


def assign_block(stream_key, own, number, rows, amount, top, bound, skew):
    ranking = jax.random.permutation(stream_key, amount)
    packed, ordinary = portions_of(amount, rows * top, bound, skew, True), portions_of(amount, rows * top, bound, skew, False)
    places = jnp.arange(amount)

    def named(tallies, offset_by):
        used = int((tallies > 0).sum())
        fixed = max(1, used // 4)
        passed = fixed + (places - fixed + offset_by * (used - fixed)) % max(1, amount - fixed)
        return jnp.zeros((amount,), jnp.int32).at[ranking[jnp.where(places < fixed, places, passed)]].set(jnp.asarray(tallies, jnp.int32))

    tallies = jnp.where(number % 4 == 0, named(packed, number // 4), named(ordinary, number - number // 4 - 1))
    mixed = jax.random.permutation(jax.random.fold_in(own, 3), amount)
    giver, sink = mixed[0:amount // 2 * 2:2], mixed[1:amount // 2 * 2:2]
    room = jnp.minimum(tallies[giver] - 1, bound - tallies[sink]) // 2
    room = jnp.where((giver == ranking[0]) | (sink == ranking[0]) | (tallies[sink] == 0), 0, jnp.maximum(room, 0))
    passed = jax.random.randint(jax.random.fold_in(own, 4), (amount // 2,), 0, 1 << 20) % (room + 1)
    tallies = tallies.at[giver].add(-passed).at[sink].add(passed)
    labels = jnp.searchsorted(jnp.cumsum(tallies), jnp.arange(rows * top), side="right").astype(jnp.int32)
    listing = labels.reshape(top, rows).T
    listing = listing[jax.random.permutation(jax.random.fold_in(own, 1), rows)]
    offset_by = jax.random.randint(jax.random.fold_in(own, 2), (rows, 1), 0, top)
    return jnp.take_along_axis(listing, (jnp.arange(top)[None, :] + offset_by) % top, axis=1)


def portions_of(count, total, most, lean, full):
    portions = [(1 << 20) // math.isqrt(grade ** lean) + 1 for grade in range(1, count + 1)]
    largest = most if full else min(most, max(-(-total // count), total * portions[0] // sum(portions)))
    least = 1 if total - largest >= count - 1 else 0
    given, spare = [largest] + [least] * (count - 1), total - largest - least * (count - 1)
    while spare > 0:
        movable = [i for i in range(1, count) if given[i] < largest] or [i for i in range(1, count) if given[i] < most]
        mass, remaining = sum([portions[i] for i in movable]), spare
        for i in movable:
            addition = min(most - given[i], max(1, remaining * portions[i] // mass), spare)
            given[i] = given[i] + addition
            spare = spare - addition
    return np.array(given)


def gaussian(rng, shape, spread, reach, shards=(), held_as=jnp.bfloat16):
    array = jax.random.normal(rng, shape, jnp.float32) * spread
    if len(shards) > 0:
        array = shard_levels(rng, shape, shards, -0.22, 0.18) * array
    return jnp.clip(array, min=-reach, max=reach).astype(held_as)


def setup_inputs(seed: int = 0) -> dict:
    key_of = jax.random.split(jax.random.key(seed), 10)
    latent = gaussian(key_of[0], (HGT, C_IN, WID), 1.0, 6.0, ((0, 64),))
    stem_weight = gaussian(key_of[1], (9 * C_IN, D), (9 * C_IN) ** -0.5, 0.5)
    norm_gain = jnp.clip(1.0 + 0.12 * jax.random.normal(key_of[2], (D,), jnp.float32), 0.4, 1.6)
    router_weight = gaussian(key_of[3], (D, EXPERTS), D ** -0.5, 0.15625)
    routes_keys = jax.random.split(jax.random.fold_in(key_of[4], 1), TOKENS // TOK_DEV)
    routes_turns = jax.random.permutation(jax.random.fold_in(key_of[4], 3), TOKENS // TOK_DEV)
    routes = jax.vmap(lambda own, number: assign_block(jax.random.fold_in(key_of[4], 2), own, number, TOK_DEV, EXPERTS, TOPK, CAP, 2))(routes_keys, routes_turns).reshape((TOKENS, TOPK))
    gate_weight = gaussian(key_of[5], (D, EXPERTS * FF), D ** -0.5, 0.15625, ((0, 8), (1, 64)))
    up_weight = gaussian(key_of[6], (D, EXPERTS * FF), D ** -0.5, 0.15625, ((0, 8), (1, 64)))
    down_weight = gaussian(key_of[7], (EXPERTS * FF, D), FF ** -0.5, 0.109375, ((0, 64), (1, 8)))
    grad_mixed = gaussian(key_of[8], (TOKENS, D), 1.0, 6.0, ((0, 64),))
    return dict(latent=latent, stem_weight=stem_weight, norm_gain=norm_gain, router_weight=router_weight, routes=routes, gate_weight=gate_weight, up_weight=up_weight, down_weight=down_weight, grad_mixed=grad_mixed)


def rms_norm(values, gain):
    return values * lax.rsqrt(lax.optimization_barrier(jnp.mean(values * values, axis=-1, keepdims=True)) + 1e-06) * gain

def gating(picked):
    chosen = jax.nn.sigmoid(picked)
    return chosen / lax.optimization_barrier(jnp.sum(chosen, axis=-1, keepdims=True))

def rounded(values):
    return lax.optimization_barrier(values.astype(jnp.bfloat16)).astype(jnp.float32)

def per_expert(items):
    rows, grads, gate_w, up_w, down_w = items
    count = rows.shape[0]
    gate_value = gate_w.astype(jnp.float32)
    up_value = up_w.astype(jnp.float32)
    down_value = down_w.astype(jnp.float32)
    pre_gate = jnp.dot(rows, gate_w, preferred_element_type=jnp.float32)
    pre_up = jnp.dot(rows, up_w, preferred_element_type=jnp.float32)
    sigma = jax.nn.sigmoid(pre_gate)
    hidden = rounded(pre_gate * sigma * pre_up)
    partial_value = jnp.einsum('rsh,shd->rsd', hidden.reshape(count, SHARDS, HID), down_value.reshape(SHARDS, HID, D))
    slot_out = lax.optimization_barrier(jnp.sum(rounded(partial_value), axis=1)).astype(jnp.bfloat16)
    grad_hidden = jnp.dot(grads, down_w.T, preferred_element_type=jnp.float32)
    grad_gate_pre = rounded(grad_hidden * pre_up * sigma * (1.0 + pre_gate * (1.0 - sigma)))
    grad_up_pre = rounded(grad_hidden * pre_gate * sigma)
    back_partial = jnp.einsum('rsh,dsh->rsd', grad_gate_pre.reshape(count, SHARDS, HID), gate_value.reshape(D, SHARDS, HID))
    back_partial = back_partial + jnp.einsum('rsh,dsh->rsd', grad_up_pre.reshape(count, SHARDS, HID), up_value.reshape(D, SHARDS, HID))
    slot_back = lax.optimization_barrier(jnp.sum(rounded(back_partial), axis=1)).astype(jnp.bfloat16)
    rows_grouped = rows.astype(jnp.float32).reshape(N_EXP, N_REP, SUB, D)
    grads_grouped = grads.astype(jnp.float32).reshape(N_EXP, N_REP, SUB, D)
    term_gate = lax.optimization_barrier(jnp.sum(rounded(jnp.einsum('igqd,igqf->gdf', rows_grouped, grad_gate_pre.reshape(N_EXP, N_REP, SUB, FF))), axis=0))
    term_up = lax.optimization_barrier(jnp.sum(rounded(jnp.einsum('igqd,igqf->gdf', rows_grouped, grad_up_pre.reshape(N_EXP, N_REP, SUB, FF))), axis=0))
    term_down = lax.optimization_barrier(jnp.sum(rounded(jnp.einsum('igqf,igqd->gfd', hidden.reshape(N_EXP, N_REP, SUB, FF), grads_grouped)), axis=0))
    return (slot_out, slot_back, term_gate, term_up, term_down)

def reference(latent, stem_weight, norm_gain, router_weight, routes, gate_weight, up_weight, down_weight, grad_mixed):
    padded = jnp.pad(latent, ((1, 1), (0, 0), (1, 1)))
    pieces = jnp.stack([padded[i:i + HGT, :, j:j + WID] for i in range(3) for j in range(3)], axis=0)
    patches = jnp.transpose(pieces, (1, 3, 0, 2)).reshape(TOKENS, 9 * C_IN)
    stem = jnp.dot(patches, stem_weight, preferred_element_type=jnp.float32).astype(jnp.bfloat16)
    stem_value = stem.astype(jnp.float32)
    normed = rms_norm(stem_value, norm_gain).astype(jnp.bfloat16)
    logits = jnp.dot(normed, router_weight, preferred_element_type=jnp.float32)
    picked = jnp.take_along_axis(logits, routes, axis=1)
    gates = gating(picked)
    upstream = grad_mixed.astype(jnp.float32)
    grad_rows = (gates[:, :, None] * upstream[:, None, :]).astype(jnp.bfloat16).reshape(-1, D)
    blocks = routes.reshape(N_EXP, TOK_DEV * TOPK)
    onehot = (blocks[..., None] == jnp.arange(EXPERTS, dtype=jnp.int32)).astype(jnp.int32)
    position = lax.optimization_barrier(jnp.sum(onehot * (jnp.cumsum(onehot, axis=1) - 1), axis=-1))
    source_index = jnp.arange(N_EXP, dtype=jnp.int32)[:, None]
    slot_index = ((blocks * N_EXP + source_index) * CAP + position).reshape(-1).astype(jnp.int32)
    total_slots = EXPERTS * N_EXP * CAP
    per_slots = N_EXP * CAP
    slot_in = jnp.zeros((total_slots, D), jnp.bfloat16).at[slot_index].set(jnp.repeat(normed, TOPK, axis=0))
    slot_grad = jnp.zeros((total_slots, D), jnp.bfloat16).at[slot_index].set(grad_rows)
    slot_in = slot_in.reshape(EXPERTS, per_slots, D)
    slot_grad = slot_grad.reshape(EXPERTS, per_slots, D)
    gate_stack = gate_weight.reshape(D, EXPERTS, FF).transpose(1, 0, 2)
    up_stack = up_weight.reshape(D, EXPERTS, FF).transpose(1, 0, 2)
    down_stack = down_weight.reshape(EXPERTS, FF, D)
    results = lax.map(per_expert, (slot_in, slot_grad, gate_stack, up_stack, down_stack))
    slot_out = results[0].reshape(total_slots, D).astype(jnp.float32)
    slot_back = results[1].reshape(total_slots, D).astype(jnp.float32)
    expert_out = slot_out[slot_index].reshape(TOKENS, TOPK, D)
    expert_back = slot_back[slot_index].reshape(TOKENS, TOPK, D)
    mixed = (stem_value + lax.optimization_barrier(jnp.sum(gates[:, :, None] * expert_out, axis=1))).astype(jnp.bfloat16)
    grad_gates = lax.optimization_barrier(jnp.sum(upstream[:, None, :] * expert_out, axis=-1))
    _, gate_pull = jax.vjp(gating, picked)
    grad_picked = gate_pull(grad_gates)[0]
    selector = (routes[:, :, None] == jnp.arange(EXPERTS, dtype=jnp.int32)).astype(jnp.float32)
    grad_logits = lax.optimization_barrier(jnp.sum(selector * grad_picked[:, :, None], axis=1))
    grad_normed = lax.optimization_barrier(jnp.sum(expert_back, axis=1)) + jnp.dot(grad_logits, router_weight.astype(jnp.float32).T, precision=lax.Precision.HIGHEST)
    _, norm_pull = jax.vjp(lambda values: rms_norm(values, norm_gain), stem_value)
    grad_stem = (upstream + norm_pull(grad_normed)[0]).astype(jnp.bfloat16)
    projected = jnp.dot(grad_stem, stem_weight.T, preferred_element_type=jnp.float32).reshape(HGT, WID, 9, C_IN)
    shifted = jnp.pad(projected, ((1, 1), (1, 1), (0, 0), (0, 0)))
    terms = [shifted[2 - i:2 - i + HGT, 2 - j:2 - j + WID, 3 * i + j, :] for i in range(3) for j in range(3)]
    grad_latent = lax.optimization_barrier(jnp.sum(jnp.stack(terms, axis=0), axis=0)).transpose(0, 2, 1)
    grad_gate = results[2].transpose(1, 0, 2).reshape(D, EXPERTS * FF)
    grad_up = results[3].transpose(1, 0, 2).reshape(D, EXPERTS * FF)
    grad_down = results[4].reshape(EXPERTS * FF, D)
    return (mixed, grad_latent, grad_gate, grad_up, grad_down)
```

```python
import jax
import jax.numpy as jnp
from jax import lax
from jax.sharding import PartitionSpec as P

CAP = 40
F32 = jnp.float32
BF = jnp.bfloat16


def dot32(a, b, dims=None):
    if dims is None:
        return jnp.dot(a, b, preferred_element_type=F32)
    return lax.dot_general(a, b, (dims, ((), ())), preferred_element_type=F32)


def split(v):
    hi = v.astype(BF)
    return hi, (v - hi.astype(F32)).astype(BF)


def halo(cells):
    count = lax.axis_size("exp")
    head, tail = cells[:1], cells[-1:]
    return jnp.concatenate(
        [
            lax.ppermute(tail, "exp", [(i, i + 1) for i in range(count - 1)]),
            cells,
            lax.ppermute(head, "exp", [(i + 1, i) for i in range(count - 1)]),
        ],
        axis=0,
    )


def gating(picked):
    chosen = jax.nn.sigmoid(picked)
    return chosen / jnp.sum(chosen, axis=-1, keepdims=True)


def local(latent, stem_weight, norm_gain, router_weight, routes, gate_weight, up_weight, down_weight, grad_mixed):
    rows_here, channels, width = latent.shape
    taps, model_width = stem_weight.shape
    experts = router_weight.shape[1]
    top = routes.shape[1]
    tok = rows_here * width
    nrep = lax.axis_size("rep")
    nexp = lax.axis_size("exp")
    shards = nexp // experts
    sub = CAP // nrep
    rep = lax.axis_index("rep")
    across = [[e * shards + m for e in range(experts)] for m in range(shards)]
    along = [[e * shards + m for m in range(shards)] for e in range(experts)]

    dsl = model_width // nrep
    s_here = lax.dynamic_slice_in_dim(stem_weight, rep * dsl, dsl, 1)
    gain_here = lax.dynamic_slice_in_dim(norm_gain, rep * dsl, dsl, 0)
    sg_hi, sg_lo = split(s_here.astype(F32) * gain_here)
    w2 = jnp.concatenate([gate_weight, up_weight], axis=1)
    g_full = lax.psum(dot32(sg_hi, w2) + dot32(sg_lo, w2), "rep")
    g_hi, g_lo = split(g_full)
    down = lax.all_gather(down_weight, "rep", axis=1, tiled=True)

    padded = jnp.pad(halo(latent), ((0, 0), (0, 0), (1, 1)))
    pieces = jnp.stack([padded[i : i + rows_here, :, j : j + width] for i in range(3) for j in range(3)], axis=0)
    patches = jnp.transpose(pieces, (1, 3, 0, 2)).reshape(tok, taps)
    stem = dot32(patches, stem_weight).astype(BF)
    sv = stem.astype(F32)
    rstd = lax.rsqrt(jnp.mean(sv * sv, axis=-1, keepdims=True) + 1e-06)
    normed = (sv * rstd * norm_gain).astype(BF)
    logits = dot32(normed, router_weight)
    selector = (routes[:, :, None] == jnp.arange(experts, dtype=jnp.int32)).astype(F32)
    picked = jnp.sum(logits[:, None, :] * selector, axis=-1)
    gates = gating(picked)

    sel_i = selector.astype(jnp.int32)
    both = jnp.sum(sel_i, axis=1)
    before = jnp.cumsum(both, axis=0) - both
    position = jnp.sum(sel_i * before[:, None, :], axis=-1)
    slot = routes * CAP + position
    slot_ids = jnp.arange(experts * CAP, dtype=jnp.int32)
    hot = [(slot[:, k][:, None] == slot_ids[None, :]) for k in range(top)]
    hot_here = [
        lax.dynamic_slice_in_dim(h.reshape(tok, experts, CAP), rep * sub, sub, 2).reshape(tok, experts * sub) for h in hot
    ]
    hot_any = sum(h.astype(BF) for h in hot_here)
    rstd_parts = split(rstd)
    gate_parts = [split(gates[:, k][:, None]) for k in range(top)]
    wide = jnp.concatenate(
        [grad_mixed, patches, rstd_parts[0], rstd_parts[1], jnp.zeros((tok, 110), BF)], axis=1
    )
    send = dot32(hot_any, wide, (((0,), (0,)))).astype(BF)
    send_gate = sum(
        dot32(hot_here[k].astype(BF), jnp.concatenate(gate_parts[k], axis=1), ((0,), (0,))) for k in range(top)
    ).astype(BF)
    send = jnp.concatenate([send[:, : model_width + 146], send_gate, send[:, model_width + 148 :]], axis=1)
    send = send.reshape(experts, sub, -1)
    stage = lax.all_to_all(send, "exp", split_axis=0, concat_axis=0, tiled=True, axis_index_groups=across)
    recv = lax.all_gather(stage, "exp", axis=0, tiled=True, axis_index_groups=along)
    flat = recv.reshape(-1, recv.shape[-1])
    gm = flat[:, :model_width]
    pr = flat[:, model_width : model_width + taps]
    extra = flat[:, model_width + taps : model_width + taps + 4].astype(F32)
    rs = extra[:, 0:1] + extra[:, 1:2]
    gt = extra[:, 2:3] + extra[:, 3:4]

    hid = gate_weight.shape[1]
    pre = rs * (dot32(pr, g_hi) + dot32(pr, g_lo))
    pg, pu = pre[:, :hid], pre[:, hid:]
    sigma = jax.nn.sigmoid(pg)
    hidden = pg * sigma * pu
    hg = (gt * hidden).astype(BF)
    out = dot32(hg, down)
    u = dot32(gm, down, ((1,), (1,)))
    gg = jnp.sum(hidden * u, axis=-1, keepdims=True)
    gu = (rs * gt) * u
    dpre = jnp.concatenate([gu * pu * sigma * (1.0 + pg * (1.0 - sigma)), gu * pg * sigma], axis=1).astype(BF)
    back = dot32(dpre, g_hi, ((1,), (1,))) + dot32(dpre, g_lo, ((1,), (1,)))
    t_part = dot32(pr, dpre, ((0,), (0,)))
    d_part = dot32(gm, hg, ((0,), (0,)))
    gg_hi, gg_lo = split(gg)
    ret = jnp.concatenate(
        [out.astype(BF), back.astype(BF), gg_hi, gg_lo, jnp.zeros((out.shape[0], 110), BF)], axis=1
    ).reshape(shards, experts, sub, -1)
    summed = lax.psum_scatter(ret, "exp", scatter_dimension=0, axis_index_groups=along, tiled=True)[0]
    mine = lax.all_to_all(summed, "exp", split_axis=0, concat_axis=0, tiled=True, axis_index_groups=across)
    slots_back = lax.all_gather(mine, "rep", axis=1, tiled=True).reshape(experts * CAP, -1)

    t_full = lax.psum(t_part, "rep")
    t_hi, t_lo = split(t_full)
    gw = (dot32(s_here, t_hi, ((0,), (0,))) + dot32(s_here, t_lo, ((0,), (0,)))) * gain_here[:, None]
    grad_gate, grad_up = gw[:, :hid], gw[:, hid:]
    grad_down = lax.psum_scatter(d_part.astype(BF), "rep", scatter_dimension=0, tiled=True).astype(F32).T

    hot_sum = sum(h.astype(BF) for h in hot)
    tok_sum = dot32(hot_sum, slots_back)
    mixed = (sv + tok_sum[:, :model_width]).astype(BF)
    ggs = slots_back[:, model_width + taps : model_width + taps + 2]
    grad_gates = jnp.concatenate(
        [jnp.sum(dot32(hot[k].astype(BF), ggs), axis=-1, keepdims=True) for k in range(top)], axis=1
    )
    _, gate_pull = jax.vjp(gating, picked)
    grad_picked = gate_pull(grad_gates)[0]
    grad_logits = jnp.sum(selector * grad_picked[:, :, None], axis=1)
    sg_all = stem_weight.astype(F32) * norm_gain
    rproj = jnp.dot(sg_all, router_weight.astype(F32), precision=lax.Precision.HIGHEST)
    b = tok_sum[:, model_width : model_width + taps] + rstd * jnp.dot(
        grad_logits, rproj.T, precision=lax.Precision.HIGHEST
    )
    c = jnp.sum(patches.astype(F32) * b, axis=-1, keepdims=True) * (rstd * rstd / model_width)
    proj = dot32(grad_mixed, stem_weight, ((1,), (1,))) + b - c * dot32(stem, stem_weight, ((1,), (1,)))
    block = halo(proj.reshape(rows_here, width, taps)).reshape(rows_here + 2, width, 9, channels)
    shifted = jnp.pad(block, ((0, 0), (1, 1), (0, 0), (0, 0)))
    terms = [
        shifted[2 - i : 2 - i + rows_here, 2 - j : 2 - j + width, 3 * i + j, :] for i in range(3) for j in range(3)
    ]
    grad_latent = sum(terms).transpose(0, 2, 1)
    return (mixed, grad_latent, grad_gate, grad_up, grad_down)


def solution(mesh):
    return jax.shard_map(
        local,
        mesh=mesh,
        in_specs=(
            P("exp", None, None),
            P(),
            P(),
            P(),
            P("exp", None),
            P("rep", "exp"),
            P("rep", "exp"),
            P("exp", "rep"),
            P("exp", None),
        ),
        out_specs=(P("exp", None), P("exp", None, None), P("rep", "exp"), P("rep", "exp"), P("exp", "rep")),
        check_vma=False,
    )
```

```python
import jax
import jax.numpy as jnp
from jax import lax
from jax.experimental import pallas as pl
from jax.experimental.pallas import tpu as pltpu
from jax.sharding import PartitionSpec as P

F32 = jnp.float32
BF = jnp.bfloat16
EXP = 8
SH = 8
REP = 8
TILES = 5
ROWS = 8
TAPS = 192
TP = TAPS // REP
MESH = pl.DeviceIdType.MESH
VM = pl.BlockSpec(memory_space=pltpu.VMEM)


def dot32(a, b, dims=None):
    if dims is None:
        return jnp.dot(a, b, preferred_element_type=F32)
    return lax.dot_general(a, b, (dims, ((), ())), preferred_element_type=F32)


def split(v):
    hi = v.astype(BF)
    return hi, (v - hi.astype(F32)).astype(BF)


def rcopy(src, dst, ssem, rsem, exp, rep):
    return pltpu.make_async_remote_copy(
        src_ref=src, dst_ref=dst, send_sem=ssem, recv_sem=rsem, device_id={"exp": exp, "rep": rep}, device_id_type=MESH
    )


class Place:
    def __init__(self):
        self.exp = lax.axis_index("exp")
        self.rep = lax.axis_index("rep")
        self.e = self.exp // SH
        self.m = self.exp % SH
        self.y = self.rep // 2
        self.c = self.rep % 2
        self.tile = self.tile_of(self.rep)
        self.d = 1 - 2 * self.c
        self.fwd = self.rep_at(self.d)
        self.bwd = self.rep_at(-self.d)
        self.partner = self.y * 2 + 1 - self.c

    def rep_at(self, dy):
        return ((self.y + dy + 4) % 4) * 2 + self.c

    def tile_of(self, rep):
        return (rep + 3 * self.e) % 8

    def peers(self):
        return [((self.e + k) % EXP) * SH + self.m for k in range(1, EXP)]

    def enter(self):
        bar = pltpu.get_barrier_semaphore()

        def greet(exp, rep):
            pl.semaphore_signal(bar, inc=1, device_id={"exp": exp, "rep": rep}, device_id_type=MESH)

        for peer in self.peers():
            greet(peer, self.rep)
        for rep in (self.fwd, self.bwd, self.partner):
            greet(self.exp, rep)

        @pl.when(self.m > 0)
        def _():
            greet(self.exp - 1, self.rep)

        @pl.when(self.m < SH - 1)
        def _():
            greet(self.exp + 1, self.rep)

        pl.semaphore_wait(bar, 10 + (self.m > 0).astype(jnp.int32) + (self.m < SH - 1).astype(jnp.int32))


class Gather:
    def __init__(self, pc, src, piece, ssem, rsem, valid=None):
        self.pc, self.src, self.piece, self.ssem, self.rsem = pc, src, piece, ssem, rsem
        self.valid = valid

    def guard(self, rep, fn):
        if self.valid is None:
            fn()
        else:
            pl.when(self.valid(rep))(fn)

    def copy(self, src, rep_of, k, target):
        return rcopy(src, self.piece(rep_of), self.ssem.at[k], self.rsem.at[rep_of], self.pc.exp, target)

    def moves(self):
        pc = self.pc
        far = pc.rep_at(2)
        own, part = pc.rep, pc.partner
        return [
            (self.src, own, 0, pc.fwd),
            (self.src, own, 1, pc.bwd),
            (self.src, own, 2, part),
            (self.piece(pc.bwd), pc.bwd, 3, pc.fwd),
            (self.piece(pc.bwd), pc.bwd, 4, part),
            (self.piece(pc.fwd), pc.fwd, 5, part),
            (self.piece(far), far, 6, part),
        ]

    def start(self):
        def go():
            for mv in self.moves()[:3]:
                self.copy(*mv).start()

        self.guard(self.pc.rep, go)

    def arrive(self, rep):
        self.copy(self.piece(rep), rep, 0, self.pc.partner).wait_recv()

    def relay(self):
        mv = self.moves()

        def near():
            self.arrive(self.pc.bwd)
            self.copy(*mv[3]).start()
            self.copy(*mv[4]).start()

        self.guard(self.pc.bwd, near)

        def other():
            self.arrive(self.pc.fwd)
            self.copy(*mv[5]).start()

        self.guard(self.pc.fwd, other)

    def relay_far(self):
        far = self.pc.rep_at(2)

        def go():
            self.arrive(far)
            self.copy(*self.moves()[6]).start()

        self.guard(far, go)

    def finish(self):
        for dy in range(4):
            rep = ((self.pc.y + dy) % 4) * 2 + 1 - self.pc.c
            self.guard(rep, lambda rep=rep: self.arrive(rep))
        for mv in self.moves():
            self.guard(mv[1], lambda mv=mv: self.copy(*mv).wait_send())


class Scatter:
    def __init__(self, pc, src, got, total, side, ssem, rsem):
        self.pc, self.src, self.got, self.total, self.side, self.ssem, self.rsem = pc, src, got, total, side, ssem, rsem

    def copy(self, k):
        pc = self.pc
        y, d = pc.y, pc.d
        at = lambda dy: self.total.at[(y + dy + 4) % 4]
        src, dst, rep = (
            (self.src.at[1 - pc.c], self.got, pc.partner),
            (at(2), self.side.at[0], pc.fwd),
            (at(-d), self.side.at[1], pc.bwd),
            (at(d), self.side.at[2], pc.fwd),
        )[k]
        return rcopy(src, dst, self.ssem.at[k], self.rsem.at[k], pc.exp, rep)

    def start(self):
        self.copy(0).start()

    def add(self):
        self.copy(0).wait_recv()

        def body(k, _):
            self.total[k] = (self.src[self.pc.c, k].astype(F32) + self.got[k].astype(F32)).astype(self.total.dtype)
            return 0

        lax.fori_loop(0, 4, body, 0)
        self.copy(1).start()
        self.copy(2).start()

    def pass_on(self):
        pc = self.pc
        self.copy(1).wait_recv()
        at = (pc.y + pc.d + 4) % 4
        self.total[at] = (self.total[at].astype(F32) + self.side[0].astype(F32)).astype(self.total.dtype)
        self.copy(3).start()

    def result(self):
        self.copy(2).wait_recv()
        self.copy(3).wait_recv()
        return self.total[self.pc.y].astype(F32) + self.side[1].astype(F32) + self.side[2].astype(F32)

    def finish(self):
        for k in range(4):
            self.copy(k).wait_send()


def scatter_scratch(block, dtype):
    return [
        pltpu.VMEM((4,) + block, dtype),
        pltpu.VMEM((4,) + block, dtype),
        pltpu.VMEM((3,) + block, dtype),
        pltpu.SemaphoreType.DMA((4,)),
        pltpu.SemaphoreType.DMA((4,)),
    ]


def gather_scratch():
    return [pltpu.SemaphoreType.DMA((7,)), pltpu.SemaphoreType.DMA((REP,))]


def dispatch_kernel(
    send, gp, wd, recv, gfull, wfull,
    g_got, g_tot, g_side, g_ss, g_rs, gmine,
    ag_ss, ag_rs, wg_ss, wg_rs,
    st_ss, st_rs, ln_ss, ln_rs, loc,
):
    pc = Place()
    m = pc.m
    pc.enter()

    def stage(k):
        peer = (pc.e + k) % EXP
        return rcopy(send.at[peer], recv.at[m, pc.tile], st_ss.at[k], st_rs.at[pc.tile], peer * SH + m, pc.rep)

    own_copy = pltpu.make_async_copy(send.at[pc.e], recv.at[m, pc.tile], loc.at[0])

    @pl.when(pc.tile < TILES)
    def _():
        for k in (1, 7, 2, 6, 3, 5, 4):
            stage(k).start()
        own_copy.start()

    gather_w = Gather(pc, wd, lambda rep: wfull.at[rep], wg_ss, wg_rs)
    own_w = pltpu.make_async_copy(wd, wfull.at[pc.rep], loc.at[1])
    scatter_g = Scatter(pc, gp, g_got, g_tot, g_side, g_ss, g_rs)
    scatter_g.start()
    gather_w.start()
    own_w.start()
    scatter_g.add()
    scatter_g.pass_on()
    spot = lambda rep: gfull.at[(rep % 2) * 4 + rep // 2]
    gmine[...] = scatter_g.result()
    gather_g = Gather(pc, gmine, spot, ag_ss, ag_rs)
    own_g = pltpu.make_async_copy(gmine, spot(pc.rep), loc.at[2])
    gather_g.start()
    own_g.start()

    @pl.when(pc.tile < TILES)
    def _():
        own_copy.wait()

    def right(i, s):
        return rcopy(
            recv.at[m - s, i], recv.at[m - s, i], ln_ss.at[0, s, i], ln_rs.at[m - s, i], pc.exp + 1, pc.rep
        )

    def left(i, s):
        return rcopy(
            recv.at[m + s, i], recv.at[m + s, i], ln_ss.at[1, s, i], ln_rs.at[m + s, i], pc.exp - 1, pc.rep
        )

    can_right = lambda s: (m < SH - 1) & (m - s >= 0)
    can_left = lambda s: (m > 0) & (m + s < SH)

    def landed(p, i):
        rcopy(recv.at[p, i], recv.at[p, i], ln_ss.at[0, 0, i], ln_rs.at[p, i], pc.exp, pc.partner).wait_recv()

    def first(i, _):
        source = (5 * (pc.rep - i + 8)) % 8

        @pl.when(source != pc.e)
        def _():
            rcopy(recv.at[m, i], recv.at[m, i], st_ss.at[0], st_rs.at[i], pc.exp, pc.partner).wait_recv()

        @pl.when(can_right(0))
        def _():
            right(i, 0).start()

        @pl.when(can_left(0))
        def _():
            left(i, 0).start()

        return 0

    lax.fori_loop(0, TILES, first, 0)
    gather_w.relay()

    def step(n, _):
        s = n // TILES
        i = n % TILES

        @pl.when(m - s >= 0)
        def _():
            landed(m - s, i)

        @pl.when(can_right(s))
        def _():
            right(i, s).start()

        @pl.when(m + s < SH)
        def _():
            landed(m + s, i)

        @pl.when(can_left(s))
        def _():
            left(i, s).start()

        return 0

    lax.fori_loop(TILES, 2 * TILES, step, 0)
    gather_g.relay()
    gather_w.relay_far()
    lax.fori_loop(2 * TILES, 4 * TILES, step, 0)
    gather_g.relay_far()
    lax.fori_loop(4 * TILES, SH * TILES, step, 0)

    gather_w.finish()
    gather_g.finish()
    scatter_g.finish()
    own_w.wait()
    own_g.wait()

    @pl.when(pc.tile < TILES)
    def _():
        for k in range(1, EXP):
            stage(k).wait_send()

    def drain(n, _):
        s = n // TILES
        i = n % TILES

        @pl.when(can_right(s))
        def _():
            right(i, s).wait_send()

        @pl.when(can_left(s))
        def _():
            left(i, s).wait_send()

        return 0

    lax.fori_loop(0, SH * TILES, drain, 0)


def combine_kernel(
    part, dp, tp, slots, gd, tfull,
    acc_l, acc_r, sums,
    d_got, d_tot, d_side, d_ss, d_rs,
    t_got, t_tot, t_side, t_ss, t_rs, tmine,
    tg_ss, tg_rs, sg_ss, sg_rs,
    ln_ss, l_rs, r_rs, st_ss, st_rs, loc,
):
    pc = Place()
    m = pc.m
    pc.enter()
    scatter_d = Scatter(pc, dp, d_got, d_tot, d_side, d_ss, d_rs)
    scatter_t = Scatter(pc, tp, t_got, t_tot, t_side, t_ss, t_rs)

    def right(p, i):
        return rcopy(part.at[p, i], acc_l.at[p, i], ln_ss.at[p, i], l_rs.at[p, i], pc.exp + 1, pc.rep)

    def left(p, i):
        return rcopy(part.at[p, i], acc_r.at[p, i], ln_ss.at[p, i], r_rs.at[p, i], pc.exp - 1, pc.rep)

    def plus(p, i, acc):
        part[p, i] = (part[p, i].astype(F32) + acc[p, i].astype(F32)).astype(BF)

    def step(n, _):
        tau = n // TILES
        i = n % TILES
        p = 7 - tau + m

        @pl.when((tau >= m) & (m > 0))
        def _():
            right_in = rcopy(part.at[p, i], acc_l.at[p, i], ln_ss.at[p, i], l_rs.at[p, i], pc.exp, pc.partner)
            right_in.wait_recv()
            plus(p, i, acc_l)

        @pl.when((tau >= m) & (m < SH - 1))
        def _():
            right(p, i).start()

        q = tau - 7 + m

        @pl.when((q >= 0) & (m < SH - 1))
        def _():
            left_in = rcopy(part.at[q, i], acc_r.at[q, i], ln_ss.at[q, i], r_rs.at[q, i], pc.exp, pc.partner)
            left_in.wait_recv()
            plus(q, i, acc_r)

        @pl.when((q >= 0) & (m > 0))
        def _():
            left(q, i).start()

        return 0

    def steps(lo, hi):
        lax.fori_loop(lo * TILES, hi * TILES, step, 0)

    steps(0, 1)
    scatter_t.start()
    scatter_d.start()
    steps(1, 2)
    scatter_t.add()
    scatter_d.add()
    steps(2, 3)
    scatter_t.pass_on()
    scatter_d.pass_on()
    steps(3, 4)
    tmine[...] = scatter_t.result()
    spot = lambda rep: tfull.at[(rep % 2) * 4 + rep // 2]
    gather_t = Gather(pc, tmine, spot, tg_ss, tg_rs)
    own_t = pltpu.make_async_copy(tmine, spot(pc.rep), loc.at[0])
    gather_t.start()
    own_t.start()
    steps(4, 5)
    gd[...] = scatter_d.result()
    steps(5, 6)
    gather_t.relay()
    steps(6, 7)

    def give(i):
        source = (5 * (pc.rep - i + 8)) % 8
        return source, rcopy(
            sums.at[i], slots.at[i, pc.e], st_ss.at[i], st_rs.at[pc.e], source * SH + m, pc.rep
        )

    def keep(i):
        return pltpu.make_async_copy(sums.at[i], slots.at[i, pc.e], loc.at[1])

    def last(i, _):
        sums[i] = part[m, i]

        @pl.when(m > 0)
        def _():
            rcopy(part.at[m, i], acc_l.at[m, i], ln_ss.at[m, i], l_rs.at[m, i], pc.exp, pc.partner).wait_recv()
            sums[i] = (sums[i].astype(F32) + acc_l[m, i].astype(F32)).astype(BF)

        @pl.when(m < SH - 1)
        def _():
            rcopy(part.at[m, i], acc_r.at[m, i], ln_ss.at[m, i], r_rs.at[m, i], pc.exp, pc.partner).wait_recv()
            sums[i] = (sums[i].astype(F32) + acc_r[m, i].astype(F32)).astype(BF)

        source, copy = give(i)

        @pl.when(source != pc.e)
        def _():
            copy.start()

        @pl.when(source == pc.e)
        def _():
            keep(i).start()

        return 0

    lax.fori_loop(0, TILES, last, 0)
    gather_t.relay_far()

    @pl.when(pc.tile < TILES)
    def _():
        keep(pc.tile).wait()
        for k in range(1, EXP):
            e = (pc.e + k) % EXP
            rcopy(
                slots.at[pc.tile, e], slots.at[pc.tile, e], st_ss.at[0], st_rs.at[e], pc.exp, pc.partner
            ).wait_recv()

    def has_rows(rep):
        return pc.tile_of(rep) < TILES

    gather_s = Gather(
        pc, slots.at[pc.tile % TILES], lambda rep: slots.at[pc.tile_of(rep) % TILES], sg_ss, sg_rs, has_rows
    )
    gather_s.start()
    gather_s.relay()
    gather_s.relay_far()
    gather_t.finish()
    scatter_t.finish()
    scatter_d.finish()
    own_t.wait()

    def drain(n, _):
        p = n // TILES
        i = n % TILES

        @pl.when((p > m) & (m < SH - 1))
        def _():
            right(p, i).wait_send()

        @pl.when((p < m) & (m > 0))
        def _():
            left(p, i).wait_send()

        return 0

    lax.fori_loop(0, SH * TILES, drain, 0)

    def drain_last(i, _):
        source, copy = give(i)

        @pl.when(source != pc.e)
        def _():
            copy.wait_send()

        return 0

    lax.fori_loop(0, TILES, drain_last, 0)
    gather_s.finish()


def dispatch(send, gp, wd):
    width = send.shape[-1]
    return pl.pallas_call(
        dispatch_kernel,
        out_shape=(
            jax.ShapeDtypeStruct((SH, TILES, ROWS, width), BF),
            jax.ShapeDtypeStruct((REP,) + gp.shape[2:], F32),
            jax.ShapeDtypeStruct((REP,) + wd.shape, BF),
        ),
        in_specs=[VM] * 3,
        out_specs=(VM,) * 3,
        scratch_shapes=scatter_scratch(gp.shape[2:], F32)
        + [pltpu.VMEM(gp.shape[2:], F32)]
        + gather_scratch()
        + gather_scratch()
        + [
            pltpu.SemaphoreType.DMA((EXP,)),
            pltpu.SemaphoreType.DMA((TILES,)),
            pltpu.SemaphoreType.DMA((2, SH, TILES)),
            pltpu.SemaphoreType.DMA((SH, TILES)),
            pltpu.SemaphoreType.DMA((3,)),
        ],
        compiler_params=pltpu.CompilerParams(collective_id=0, has_side_effects=True),
        name="dispatch",
    )(send, gp, wd)


def combine(part, dp, tp):
    width = part.shape[-1]
    shape = part.shape
    return pl.pallas_call(
        combine_kernel,
        out_shape=(
            jax.ShapeDtypeStruct((TILES, EXP, ROWS, width), BF),
            jax.ShapeDtypeStruct(dp.shape[2:], F32),
            jax.ShapeDtypeStruct((REP,) + tp.shape[2:], F32),
        ),
        in_specs=[VM] * 3,
        out_specs=(VM,) * 3,
        scratch_shapes=[pltpu.VMEM(shape, BF), pltpu.VMEM(shape, BF), pltpu.VMEM(shape[1:], BF)]
        + scatter_scratch(dp.shape[2:], BF)
        + scatter_scratch(tp.shape[2:], F32)
        + [pltpu.VMEM(tp.shape[2:], F32)]
        + gather_scratch()
        + gather_scratch()
        + [
            pltpu.SemaphoreType.DMA((SH, TILES)),
            pltpu.SemaphoreType.DMA((SH, TILES)),
            pltpu.SemaphoreType.DMA((SH, TILES)),
            pltpu.SemaphoreType.DMA((TILES,)),
            pltpu.SemaphoreType.DMA((EXP,)),
            pltpu.SemaphoreType.DMA((2,)),
        ],
        compiler_params=pltpu.CompilerParams(collective_id=1, has_side_effects=True),
        name="combine",
    )(part, dp, tp)


def halo(cells):
    count = lax.axis_size("exp")
    head, tail = cells[:1], cells[-1:]
    return jnp.concatenate(
        [
            lax.ppermute(tail, "exp", [(i, i + 1) for i in range(count - 1)]),
            cells,
            lax.ppermute(head, "exp", [(i + 1, i) for i in range(count - 1)]),
        ],
        axis=0,
    )


def gating(picked):
    chosen = jax.nn.sigmoid(picked)
    return chosen / jnp.sum(chosen, axis=-1, keepdims=True)


def local(latent, stem_weight, norm_gain, router_weight, routes, gate_weight, up_weight, down_weight, grad_mixed):
    rows_here, channels, width = latent.shape
    taps, model_width = stem_weight.shape
    experts = router_weight.shape[1]
    top = routes.shape[1]
    tok = rows_here * width
    rep = lax.axis_index("rep")
    expert_here = lax.axis_index("exp") // SH
    tile = (rep + 3 * expert_here) % 8
    hid = gate_weight.shape[1]
    extra = TAPS - taps

    dsl = model_width // REP
    s_here = lax.dynamic_slice_in_dim(stem_weight, rep * dsl, dsl, 1)
    gain_here = lax.dynamic_slice_in_dim(norm_gain, rep * dsl, dsl, 0)
    sg_hi, sg_lo = split(jnp.pad(s_here.astype(F32) * gain_here, ((0, extra), (0, 0))))
    w2 = jnp.concatenate([gate_weight, up_weight], axis=1)
    gp = (dot32(sg_hi, w2) + dot32(sg_lo, w2)).reshape(2, 4, TP, 2 * hid)

    padded = jnp.pad(halo(latent), ((0, 0), (0, 0), (1, 1)))
    pieces = jnp.stack([padded[i : i + rows_here, :, j : j + width] for i in range(3) for j in range(3)], axis=0)
    patches = jnp.transpose(pieces, (1, 3, 0, 2)).reshape(tok, taps)
    stem = dot32(patches, stem_weight).astype(BF)
    sv = stem.astype(F32)
    rstd = lax.rsqrt(jnp.mean(sv * sv, axis=-1, keepdims=True) + 1e-06)
    normed = (sv * rstd * norm_gain).astype(BF)
    logits = dot32(normed, router_weight)
    selector = (routes[:, :, None] == jnp.arange(experts, dtype=jnp.int32)).astype(F32)
    picked = jnp.sum(logits[:, None, :] * selector, axis=-1)
    gates = gating(picked)

    both = jnp.sum(selector, axis=1)
    earlier = (jnp.arange(tok)[:, None] > jnp.arange(tok)[None, :]).astype(BF)
    before = dot32(earlier, both.astype(BF))
    position = jnp.sum(selector * before[:, None, :], axis=-1).astype(jnp.int32)
    in_tile = position - ROWS * tile
    here = jnp.where((in_tile >= 0) & (in_tile < ROWS), routes * ROWS + in_tile, -1)
    here_ids = jnp.arange(experts * ROWS, dtype=jnp.int32)
    hot_here = [(here[:, k][:, None] == here_ids).astype(BF) for k in range(top)]
    full = (position // ROWS) * (experts * ROWS) + routes * ROWS + position % ROWS
    full_ids = jnp.arange(TILES * experts * ROWS, dtype=jnp.int32)
    hot = [(full[:, k][:, None] == full_ids).astype(BF) for k in range(top)]

    r_hi, r_lo = split(rstd)
    side = jnp.concatenate([jnp.pad(patches, ((0, 0), (0, extra))), r_hi, r_lo], axis=1)
    send_gm = dot32(hot_here[0] + hot_here[1], grad_mixed, ((0,), (0,))).astype(BF)
    send_side = dot32(hot_here[0] + hot_here[1], side, ((0,), (0,))).astype(BF)
    send_gate = sum(
        dot32(hot_here[k], jnp.concatenate(split(gates[:, k : k + 1]), axis=1), ((0,), (0,))) for k in range(top)
    ).astype(BF)
    send = jnp.concatenate([send_gm, send_side, send_gate, jnp.zeros((experts * ROWS, 60), BF)], axis=1)
    recv, g_full, w_full = dispatch(
        send.reshape(experts, ROWS, -1), gp, down_weight.T
    )
    flat = recv.reshape(-1, recv.shape[-1])
    gm = flat[:, :model_width]
    pr = flat[:, model_width : model_width + TAPS]
    more = flat[:, model_width + TAPS : model_width + TAPS + 4].astype(F32)
    rs = more[:, 0:1] + more[:, 1:2]
    gt = more[:, 2:3] + more[:, 3:4]
    g_hi, g_lo = split(g_full.reshape(TAPS, 2 * hid))
    down_t = w_full.reshape(model_width, hid)

    pre = rs * (dot32(pr, g_hi) + dot32(pr, g_lo))
    pg, pu = pre[:, :hid], pre[:, hid:]
    sigma = jax.nn.sigmoid(pg)
    hidden = pg * sigma * pu
    hg = (gt * hidden).astype(BF)
    out = dot32(hg, down_t, ((1,), (1,)))
    u = dot32(gm, down_t)
    gg = jnp.sum(hidden * u, axis=-1, keepdims=True)
    gu = (rs * gt) * u
    dpre = jnp.concatenate([gu * pu * sigma * (1.0 + pg * (1.0 - sigma)), gu * pg * sigma], axis=1).astype(BF)
    back = dot32(dpre, g_hi, ((1,), (1,))) + dot32(dpre, g_lo, ((1,), (1,)))
    t_part = dot32(pr, dpre, ((0,), (0,))).reshape(2, 4, TP, 2 * hid)
    d_part = dot32(gm, hg, ((0,), (0,))).astype(BF)
    d_part = d_part.reshape(4, 2, dsl, hid).transpose(1, 0, 2, 3)
    gg_hi, gg_lo = split(gg)
    part = jnp.concatenate(
        [out.astype(BF), back.astype(BF), gg_hi, gg_lo, jnp.zeros((out.shape[0], 62), BF)], axis=1
    ).reshape(recv.shape)
    slots_back, gd, t_full = combine(part, d_part, t_part)
    slots_back = slots_back.reshape(TILES * experts * ROWS, -1)

    t_hi, t_lo = split(t_full.reshape(TAPS, 2 * hid)[:taps])
    gw = (dot32(s_here, t_hi, ((0,), (0,))) + dot32(s_here, t_lo, ((0,), (0,)))) * gain_here[:, None]
    grad_gate, grad_up = gw[:, :hid], gw[:, hid:]
    grad_down = gd.T

    tok_sum = dot32(hot[0] + hot[1], slots_back)
    mixed = (sv + tok_sum[:, :model_width]).astype(BF)
    ggs = slots_back[:, model_width + TAPS : model_width + TAPS + 2]
    grad_gates = jnp.concatenate(
        [jnp.sum(dot32(hot[k], ggs), axis=-1, keepdims=True) for k in range(top)], axis=1
    )
    _, gate_pull = jax.vjp(gating, picked)
    grad_picked = gate_pull(grad_gates)[0]
    grad_logits = jnp.sum(selector * grad_picked[:, :, None], axis=1)
    sg_all = stem_weight.astype(F32) * norm_gain
    rproj = jnp.dot(sg_all, router_weight.astype(F32), precision=lax.Precision.HIGHEST)
    b = tok_sum[:, model_width : model_width + taps] + rstd * jnp.dot(
        grad_logits, rproj.T, precision=lax.Precision.HIGHEST
    )
    c = jnp.sum(patches.astype(F32) * b, axis=-1, keepdims=True) * (rstd * rstd / model_width)
    proj = dot32(grad_mixed, stem_weight, ((1,), (1,))) + b - c * dot32(stem, stem_weight, ((1,), (1,)))
    block = halo(proj.reshape(rows_here, width, taps)).reshape(rows_here + 2, width, 9, channels)
    shifted = jnp.pad(block, ((0, 0), (1, 1), (0, 0), (0, 0)))
    terms = [
        shifted[2 - i : 2 - i + rows_here, 2 - j : 2 - j + width, 3 * i + j, :] for i in range(3) for j in range(3)
    ]
    grad_latent = sum(terms).transpose(0, 2, 1)
    return (mixed, grad_latent, grad_gate, grad_up, grad_down)


def solution(mesh):
    return jax.shard_map(
        local,
        mesh=mesh,
        in_specs=(
            P("exp", None, None),
            P(),
            P(),
            P(),
            P("exp", None),
            P("rep", "exp"),
            P("rep", "exp"),
            P("exp", "rep"),
            P("exp", None),
        ),
        out_specs=(P("exp", None), P("exp", None, None), P("rep", "exp"), P("rep", "exp"), P("exp", "rep")),
        check_vma=False,
    )
```

```python
import jax
import jax.numpy as jnp
from jax import lax
from jax.experimental import pallas as pl
from jax.experimental.pallas import tpu as pltpu
from jax.sharding import PartitionSpec as P

F32 = jnp.float32
BF = jnp.bfloat16
I32 = jnp.int32
EXP = 8
SH = 8
REP = 8
TILES = 5
ROWS = 8
PIECE = TILES * ROWS
CHUNKS = ((0, 2), (2, 2), (4, 1))
TAPS = 192
TP = TAPS // REP
SIDE = 256
MESH = pl.DeviceIdType.MESH
VM = pl.BlockSpec(memory_space=pltpu.VMEM)


def dot32(a, b, dims=None):
    if dims is None:
        return jnp.dot(a, b, preferred_element_type=F32)
    return lax.dot_general(a, b, (dims, ((), ())), preferred_element_type=F32)


NT = ((1,), (1,))
TN = ((0,), (0,))


def split(v):
    hi = v.astype(BF)
    return hi, (v - hi.astype(F32)).astype(BF)


def iota(shape, dim):
    return lax.broadcasted_iota(I32, shape, dim)


def rcopy(src, dst, ssem, rsem, exp, rep):
    return pltpu.make_async_remote_copy(
        src_ref=src, dst_ref=dst, send_sem=ssem, recv_sem=rsem, device_id={"exp": exp, "rep": rep}, device_id_type=MESH
    )


class Place:
    def __init__(self):
        self.exp = lax.axis_index("exp")
        self.rep = lax.axis_index("rep")
        self.e = self.exp // SH
        self.m = self.exp % SH
        self.y = self.rep // 2
        self.c = self.rep % 2
        self.tile = self.tile_of(self.rep)
        self.d = 1 - 2 * self.c
        self.fwd = self.rep_at(self.d)
        self.bwd = self.rep_at(-self.d)
        self.partner = self.y * 2 + 1 - self.c

    def rep_at(self, dy):
        return ((self.y + dy + 4) % 4) * 2 + self.c

    def tile_of(self, rep):
        return (rep + 3 * self.e) % 8

    def peers(self):
        return [((self.e + k) % EXP) * SH + self.m for k in range(1, EXP)]

    def enter(self):
        bar = pltpu.get_barrier_semaphore()

        def greet(exp, rep):
            pl.semaphore_signal(bar, inc=1, device_id={"exp": exp, "rep": rep}, device_id_type=MESH)

        for peer in self.peers():
            greet(peer, self.rep)
        for rep in (self.fwd, self.bwd, self.partner):
            greet(self.exp, rep)

        @pl.when(self.exp > 0)
        def _():
            greet(self.exp - 1, self.rep)

        @pl.when(self.exp < EXP * SH - 1)
        def _():
            greet(self.exp + 1, self.rep)

        pl.semaphore_wait(bar, 10 + (self.exp > 0).astype(jnp.int32) + (self.exp < EXP * SH - 1).astype(jnp.int32))


class Gather:
    def __init__(self, pc, src, piece, ssem, rsem, valid=None):
        self.pc, self.src, self.piece, self.ssem, self.rsem = pc, src, piece, ssem, rsem
        self.valid = valid

    def guard(self, rep, fn):
        if self.valid is None:
            fn()
        else:
            pl.when(self.valid(rep))(fn)

    def copy(self, src, rep_of, k, target):
        return rcopy(src, self.piece(rep_of), self.ssem.at[k], self.rsem.at[rep_of], self.pc.exp, target)

    def moves(self):
        pc = self.pc
        far = pc.rep_at(2)
        own, part = pc.rep, pc.partner
        return [
            (self.src, own, 0, pc.fwd),
            (self.src, own, 1, pc.bwd),
            (self.src, own, 2, part),
            (self.piece(pc.bwd), pc.bwd, 3, pc.fwd),
            (self.piece(pc.bwd), pc.bwd, 4, part),
            (self.piece(pc.fwd), pc.fwd, 5, part),
            (self.piece(far), far, 6, part),
        ]

    def start(self):
        def go():
            for mv in self.moves()[:3]:
                self.copy(*mv).start()

        self.guard(self.pc.rep, go)

    def arrive(self, rep):
        self.copy(self.piece(rep), rep, 0, self.pc.partner).wait_recv()

    def relay(self):
        mv = self.moves()

        def near():
            self.arrive(self.pc.bwd)
            self.copy(*mv[3]).start()
            self.copy(*mv[4]).start()

        self.guard(self.pc.bwd, near)

        def other():
            self.arrive(self.pc.fwd)
            self.copy(*mv[5]).start()

        self.guard(self.pc.fwd, other)

    def relay_far(self):
        far = self.pc.rep_at(2)

        def go():
            self.arrive(far)
            self.copy(*self.moves()[6]).start()

        self.guard(far, go)

    def finish(self):
        for dy in range(4):
            rep = ((self.pc.y + dy) % 4) * 2 + 1 - self.pc.c
            self.guard(rep, lambda rep=rep: self.arrive(rep))
        for mv in self.moves():
            self.guard(mv[1], lambda mv=mv: self.copy(*mv).wait_send())


class Scatter:
    def __init__(self, pc, src, got, total, side, ssem, rsem):
        self.pc, self.src, self.got, self.total, self.side, self.ssem, self.rsem = pc, src, got, total, side, ssem, rsem

    def copy(self, k):
        pc = self.pc
        y, d = pc.y, pc.d
        at = lambda dy: self.total.at[(y + dy + 4) % 4]
        src, dst, rep = (
            (self.src.at[1 - pc.c], self.got, pc.partner),
            (at(2), self.side.at[0], pc.fwd),
            (at(-d), self.side.at[1], pc.bwd),
            (at(d), self.side.at[2], pc.fwd),
        )[k]
        return rcopy(src, dst, self.ssem.at[k], self.rsem.at[k], pc.exp, rep)

    def start(self):
        self.copy(0).start()

    def add(self):
        self.copy(0).wait_recv()

        def body(k, _):
            self.total[k] = (self.src[self.pc.c, k].astype(F32) + self.got[k].astype(F32)).astype(self.total.dtype)
            return 0

        lax.fori_loop(0, 4, body, 0)
        self.copy(1).start()
        self.copy(2).start()

    def pass_on(self):
        pc = self.pc
        self.copy(1).wait_recv()
        at = (pc.y + pc.d + 4) % 4
        self.total[at] = (self.total[at].astype(F32) + self.side[0].astype(F32)).astype(self.total.dtype)
        self.copy(3).start()

    def result(self):
        self.copy(2).wait_recv()
        self.copy(3).wait_recv()
        return self.total[self.pc.y].astype(F32) + self.side[1].astype(F32) + self.side[2].astype(F32)

    def finish(self):
        for k in range(4):
            self.copy(k).wait_send()


def scatter_scratch(block, dtype):
    return [
        pltpu.VMEM((4,) + block, dtype),
        pltpu.VMEM((4,) + block, dtype),
        pltpu.VMEM((3,) + block, dtype),
        pltpu.SemaphoreType.DMA((4,)),
        pltpu.SemaphoreType.DMA((4,)),
    ]


def gather_scratch():
    return [pltpu.SemaphoreType.DMA((7,)), pltpu.SemaphoreType.DMA((REP,))]


def layer_kernel(
    latent, s_ref, gain_ref, wr_ref, routes_ref, routes_t_ref, wg_ref, wu_ref, wd_ref, gm_ref,
    mixed_ref, glat_ref, ggate_ref, gup_ref, gdown_ref,
    send, send_side, recv, recv_side, w_own, wfull, gp, gmine, gfull,
    h_prev, h_next, lat4, ptx, stem_ref, sg_hi, sg_lo,
    row32, gm_all, hg_ref, dpre_ref,
    part, acc_l, acc_r, sums, ret32, slots, dp, tp, tmine, tfull, a_out, a_prev, a_next,
    *sems
):
    (g_got, g_tot, g_side, g_ss, g_rs, d_got, d_tot, d_side, d_ss, d_rs, t_got, t_tot, t_side, t_ss, t_rs,
     ag_ss, ag_rs, wg_ss, wg_rs, tg_ss, tg_rs, sg_ss, sg_rs,
     st_ss, st_rs, sd_ss, sd_rs, ln_ss, ln_rs, sl_ss, sl_rs, ca_ss, cl_rs, cr_rs, ct_ss, ct_rs,
     ha_ss, ha_rs, hb_ss, hb_rs, loc) = sems
    pc = Place()
    m = pc.m
    tok, dm = gm_ref.shape
    hid = wg_ref.shape[1]
    taps = s_ref.shape[0]
    wide = tok // 2
    top = routes_ref.shape[1]
    has_rows = pc.tile < TILES

    upper = (iota((tok, tok), 0) < iota((tok, tok), 1)).astype(BF)
    lower = (iota((tok, tok), 0) > iota((tok, tok), 1)).astype(BF)
    r_row = [routes_t_ref[k : k + 1, :] for k in range(top)]
    r_col = [routes_ref[:, k : k + 1] for k in range(top)]
    sel_row = [(iota((EXP, tok), 0) == r).astype(F32) for r in r_row]
    sel_col = [(iota((tok, EXP), 1) == r).astype(F32) for r in r_col]
    before_row = dot32((sel_row[0] + sel_row[1]).astype(BF), upper)
    before_col = dot32(lower, (sel_col[0] + sel_col[1]).astype(BF))
    pos_row = [jnp.sum(s * before_row, axis=0, keepdims=True).astype(I32) for s in sel_row]
    pos_col = [jnp.sum(s * before_col, axis=1, keepdims=True).astype(I32) for s in sel_col]

    def here_id(pos, r):
        q = pos - ROWS * pc.tile
        return jnp.where((q >= 0) & (q < ROWS), r * ROWS + q, -1)

    def full_id(pos, r):
        t = lax.shift_right_logical(pos, 3)
        return t * (EXP * ROWS) + r * ROWS + (pos - t * ROWS)

    hot_here = [(iota((EXP * ROWS, tok), 0) == here_id(p, r)).astype(F32) for p, r in zip(pos_row, r_row)]
    hot_here_b = [h.astype(BF) for h in hot_here]
    picked_rows = dot32(hot_here_b[0] + hot_here_b[1], gm_ref[...])
    for e in range(EXP):
        send[e] = picked_rows[e * ROWS : (e + 1) * ROWS].astype(BF)
    eye = (iota((hid, hid), 0) == iota((hid, hid), 1)).astype(BF)
    w_own[...] = dot32(wd_ref[...], eye, TN).astype(BF)

    pc.enter()

    ha = (
        rcopy(latent.at[1], h_prev, ha_ss.at[0], ha_rs.at[0], pc.exp + 1, pc.rep),
        rcopy(latent.at[0], h_next, ha_ss.at[1], ha_rs.at[1], pc.exp - 1, pc.rep),
    )
    first_row, last_row = pc.exp == 0, pc.exp == EXP * SH - 1
    pl.when(jnp.logical_not(last_row))(lambda: ha[0].start())
    pl.when(jnp.logical_not(first_row))(lambda: ha[1].start())

    def stage(k, side):
        peer = (pc.e + k) % EXP
        src, dst, ss, rs = (send_side, recv_side, sd_ss, sd_rs) if side else (send, recv, st_ss, st_rs)
        return rcopy(src.at[peer], dst.at[m, pc.tile], ss.at[k], rs.at[pc.tile], peer * SH + m, pc.rep)

    keep_gm = pltpu.make_async_copy(send.at[pc.e], recv.at[m, pc.tile], loc.at[0])
    keep_side = pltpu.make_async_copy(send_side.at[pc.e], recv_side.at[m, pc.tile], loc.at[1])

    @pl.when(has_rows)
    def _():
        for k in (1, 7, 2, 6, 3, 5, 4):
            stage(k, False).start()
        keep_gm.start()

    gather_w = Gather(pc, w_own, lambda rep: wfull.at[rep], wg_ss, wg_rs)
    own_w = pltpu.make_async_copy(w_own, wfull.at[pc.rep], loc.at[2])
    gather_w.start()
    own_w.start()

    dsl = wg_ref.shape[0]
    sg = s_ref[...].astype(F32) * gain_ref[...]
    hi, lo = split(sg)
    pick = (iota((dm, dsl), 0) == iota((dm, dsl), 1) + pc.rep * dsl).astype(BF)
    s_hi = dot32(hi, pick).astype(BF)
    s_lo = dot32(lo, pick).astype(BF)
    sg_hi[...] = s_hi
    sg_lo[...] = s_lo
    zero_taps = jnp.zeros((TAPS - taps, 2 * hid), F32)
    share = jnp.concatenate(
        [dot32(s_hi, w[...]) + dot32(s_lo, w[...]) for w in (wg_ref, wu_ref)], axis=1
    )
    share = jnp.concatenate([share, zero_taps], axis=0)
    for k in range(REP):
        gp[k // 4, k % 4] = share[k * TP : (k + 1) * TP]
    rproj = dot32(hi, wr_ref[...], NT) + dot32(lo, wr_ref[...], NT)
    scatter_g = Scatter(pc, gp, g_got, g_tot, g_side, g_ss, g_rs)
    scatter_g.start()

    @pl.when(jnp.logical_not(first_row))
    def _():
        rcopy(latent.at[1], h_prev, ha_ss.at[0], ha_rs.at[0], pc.exp, pc.partner).wait_recv()
        lat4[0] = h_prev[...].astype(F32)

    @pl.when(first_row)
    def _():
        lat4[0] = jnp.zeros(lat4.shape[1:], F32)

    @pl.when(jnp.logical_not(last_row))
    def _():
        rcopy(latent.at[0], h_next, ha_ss.at[1], ha_rs.at[1], pc.exp, pc.partner).wait_recv()
        lat4[3] = h_next[...].astype(F32)

    @pl.when(last_row)
    def _():
        lat4[3] = jnp.zeros(lat4.shape[1:], F32)

    lat4[1] = latent[0].astype(F32)
    lat4[2] = latent[1].astype(F32)
    chan = lat4.shape[1]
    col = iota((chan, tok), 1)
    col = jnp.where(col >= wide, col - wide, col)

    def shifted(v, by):
        if by == 0:
            return v
        rolled = pltpu.roll(v, (-by) % tok, 1)
        return jnp.where(col == (0 if by < 0 else wide - 1), 0.0, rolled)

    for i in range(3):
        two = jnp.concatenate([lat4[i], lat4[i + 1]], axis=1)
        for j in range(3):
            ptx[pl.ds((3 * i + j) * chan, chan), :] = shifted(two, j - 1)
    ptx[pl.ds(taps, SIDE - taps), :] = jnp.zeros((SIDE - taps, tok), F32)
    pt = ptx[pl.ds(0, taps), :]
    stem = dot32(pt.astype(BF), s_ref[...], TN).astype(BF)
    stem_ref[...] = stem
    sv = stem.astype(F32)
    rstd = lax.rsqrt(jnp.mean(sv * sv, axis=-1, keepdims=True) + 1e-06)
    rstd_row = jnp.transpose(jnp.broadcast_to(rstd, (tok, tok)))[0:1, :]
    normed = (sv * rstd * gain_ref[...]).astype(BF)
    logits = dot32(wr_ref[...], normed, NT)
    picked = [jnp.sum(s * logits, axis=0, keepdims=True) for s in sel_row]
    chosen = [jax.nn.sigmoid(p) for p in picked]
    total = chosen[0] + chosen[1]
    gates = [c / total for c in chosen]
    r_hi, r_lo = split(rstd_row)
    ptx[pl.ds(TAPS, 1), :] = r_hi.astype(F32)
    ptx[pl.ds(TAPS + 1, 1), :] = r_lo.astype(F32)
    side = jnp.zeros((EXP * ROWS, SIDE), F32)
    for k in range(top):
        k_hi, k_lo = split(gates[k])
        ptx[pl.ds(TAPS + 2, 1), :] = k_hi.astype(F32)
        ptx[pl.ds(TAPS + 3, 1), :] = k_lo.astype(F32)
        side = side + dot32(hot_here_b[k], ptx[...].astype(BF), NT)
    for e in range(EXP):
        send_side[e] = side[e * ROWS : (e + 1) * ROWS].astype(BF)

    @pl.when(has_rows)
    def _():
        for k in (1, 7, 2, 6, 3, 5, 4):
            stage(k, True).start()
        keep_side.start()

    ends = (m < SH - 1, m > 0)

    def hop(way, p, c, s):
        at = pl.ds(CHUNKS[c][0], CHUNKS[c][1])
        ref = recv.at[p, at]
        return rcopy(ref, ref, ln_ss.at[way, s, c], ln_rs.at[p, c], pc.exp + 1 - 2 * way, pc.rep)

    def hop_side(way, p, s):
        ref = recv_side.at[p]
        return rcopy(ref, ref, sl_ss.at[way, s], sl_rs.at[p], pc.exp + 1 - 2 * way, pc.rep)

    def arrived(i, side):
        source = (5 * (pc.rep - i + 8)) % 8
        ref, ss, rs = (recv_side, sd_ss, sd_rs) if side else (recv, st_ss, st_rs)

        @pl.when(source != pc.e)
        def _():
            rcopy(ref.at[m, i], ref.at[m, i], ss.at[0], rs.at[i], pc.exp, pc.partner).wait_recv()

    def step(s, _):
        for c in range(len(CHUNKS)):
            for way, p in ((0, m - s), (1, m + s)):
                ok = (p >= 0) if way == 0 else (p < SH)

                @pl.when(ok)
                def _():
                    hop(way, p, c, s).wait_recv()

                    @pl.when(ends[way])
                    def _():
                        hop(way, p, c, s).start()

        return 0

    def step_side(s, _):
        for way, p in ((0, m - s), (1, m + s)):
            ok = (p >= 0) if way == 0 else (p < SH)

            @pl.when(ok)
            def _():
                hop_side(way, p, s).wait_recv()

                @pl.when(ends[way])
                def _():
                    hop_side(way, p, s).start()

        return 0

    scatter_g.add()

    @pl.when(has_rows)
    def _():
        keep_gm.wait()

    for c, (at, count) in enumerate(CHUNKS):
        for i in range(at, at + count):
            arrived(i, False)
        for way in range(2):
            pl.when(ends[way])(lambda way=way, c=c: hop(way, m, c, 0).start())
    scatter_g.pass_on()
    gather_w.relay()
    lax.fori_loop(1, 2, step, 0)
    gmine[...] = scatter_g.result()
    spot = lambda ref: lambda rep: ref.at[(rep % 2) * 4 + rep // 2]
    gather_g = Gather(pc, gmine, spot(gfull), ag_ss, ag_rs)
    own_g = pltpu.make_async_copy(gmine, spot(gfull)(pc.rep), loc.at[3])
    gather_g.start()
    own_g.start()

    @pl.when(has_rows)
    def _():
        keep_side.wait()

    for i in range(TILES):
        arrived(i, True)
    for way in range(2):
        pl.when(ends[way])(lambda way=way: hop_side(way, m, 0).start())
    gather_w.relay_far()
    lax.fori_loop(2, 3, step, 0)
    gather_g.relay()
    lax.fori_loop(1, 3, step_side, 0)
    lax.fori_loop(3, 4, step, 0)
    gather_g.relay_far()
    lax.fori_loop(3, 5, step_side, 0)
    lax.fori_loop(4, 5, step, 0)
    lax.fori_loop(5, 7, step_side, 0)
    lax.fori_loop(5, 6, step, 0)
    lax.fori_loop(7, 8, step_side, 0)
    lax.fori_loop(6, 7, step, 0)
    gather_g.finish()
    gather_w.finish()
    scatter_g.finish()
    own_w.wait()
    own_g.wait()

    def widen(ref, n):
        def body(k, _):
            for i in range(TILES):
                row32[pl.ds(k * PIECE + i * ROWS, ROWS), pl.ds(0, n)] = ref[k, i].astype(F32)
            return 0

        lax.fori_loop(0, SH, body, 0)

    widen(recv_side, SIDE)
    more = row32[:, pl.ds(0, SIDE)]
    pr = more[:, :TAPS].astype(BF)
    rs = more[:, TAPS : TAPS + 1] + more[:, TAPS + 1 : TAPS + 2]
    gt = more[:, TAPS + 2 : TAPS + 3] + more[:, TAPS + 3 : TAPS + 4]
    g_hi, g_lo = split(gfull[...].reshape(TAPS, 2 * hid))
    pre = rs * (dot32(pr, g_hi) + dot32(pr, g_lo))
    pg, pu = pre[:, :hid], pre[:, hid:]
    sigma = jax.nn.sigmoid(pg)
    silu = pg * sigma
    hidden = silu * pu
    slope = pu * sigma * (1.0 + pg * (1.0 - sigma))
    hg = (gt * hidden).astype(BF)
    down_t = wfull[...].reshape(dm, hid)
    ret32[:, pl.ds(0, dm)] = dot32(hg, down_t, NT)
    lax.fori_loop(7, 8, step, 0)
    widen(recv, dm)
    gm_all[...] = row32[...].astype(BF)
    u = dot32(gm_all[...], down_t)
    gg = jnp.sum(hidden * u, axis=-1, keepdims=True)
    gu = (rs * gt) * u
    dpre = jnp.concatenate([gu * slope, gu * silu], axis=1).astype(BF)
    dpre_ref[...] = dpre
    hg_ref[...] = hg
    back = dot32(dpre, g_hi, NT) + dot32(dpre, g_lo, NT)
    gg_hi = gg.astype(BF).astype(F32)
    lane = iota((SH * PIECE, SIDE - TAPS), 1)
    tail = jnp.where(lane == 0, gg_hi, jnp.where(lane == 1, gg - gg_hi, 0.0))
    ret32[:, pl.ds(dm, SIDE)] = jnp.concatenate([back, tail], axis=1)

    def narrow(k, _):
        for i in range(TILES):
            part[k, i] = ret32[pl.ds(k * PIECE + i * ROWS, ROWS), :].astype(BF)
        return 0

    lax.fori_loop(0, SH, narrow, 0)

    def give(way, p, c):
        at = pl.ds(CHUNKS[c][0], CHUNKS[c][1])
        dst, rsem = ((acc_l, cl_rs), (acc_r, cr_rs))[way]
        return rcopy(
            part.at[p, at], dst.at[p, at], ca_ss.at[p, c], rsem.at[p, c], pc.exp + 1 - 2 * way, pc.rep
        )

    def step_sum(tau, _):
        for c, (at, count) in enumerate(CHUNKS):
            for way, p in ((0, 7 - tau + m), (1, tau - 7 + m)):
                ok = (tau >= m) if way == 0 else (p >= 0)
                acc = (acc_l, acc_r)[way]

                @pl.when(ok & ends[1 - way])
                def _():
                    give(way, p, c).wait_recv()
                    for i in range(at, at + count):
                        part[p, i] = (part[p, i].astype(F32) + acc[p, i].astype(F32)).astype(BF)

                pl.when(ok & ends[way])(lambda: give(way, p, c).start())

        return 0

    def steps(at, to):
        lax.fori_loop(at, to, step_sum, 0)

    steps(0, 1)
    t_share = dot32(pr, dpre_ref[...], TN)
    for k in range(REP):
        tp[k // 4, k % 4] = t_share[k * TP : (k + 1) * TP]
    scatter_t = Scatter(pc, tp, t_got, t_tot, t_side, t_ss, t_rs)
    scatter_t.start()
    d_share = dot32(hg_ref[...], gm_all[...], TN)
    for k in range(REP):
        dp[k % 2, k // 2] = d_share[:, k * dsl : (k + 1) * dsl].astype(BF)
    scatter_d = Scatter(pc, dp, d_got, d_tot, d_side, d_ss, d_rs)
    scatter_d.start()
    steps(1, 2)
    scatter_t.add()
    scatter_d.add()
    steps(2, 3)
    scatter_t.pass_on()
    scatter_d.pass_on()
    steps(3, 4)
    tmine[...] = scatter_t.result()
    gather_t = Gather(pc, tmine, spot(tfull), tg_ss, tg_rs)
    own_t = pltpu.make_async_copy(tmine, spot(tfull)(pc.rep), loc.at[4])
    gather_t.start()
    own_t.start()
    gdown_ref[...] = scatter_d.result()
    steps(4, 5)
    gather_t.relay()
    steps(5, 6)
    gather_t.relay_far()
    steps(6, 7)

    def home(i):
        source = (5 * (pc.rep - i + 8)) % 8
        return source, rcopy(
            sums.at[i], slots.at[i, pc.e], ct_ss.at[i], ct_rs.at[pc.e], source * SH + m, pc.rep
        )

    keep_out = lambda i: pltpu.make_async_copy(sums.at[i], slots.at[i, pc.e], loc.at[5])
    for c, (at, count) in enumerate(CHUNKS):
        for way in range(2):
            pl.when(ends[1 - way])(lambda way=way, c=c: give(way, m, c).wait_recv())
        for i in range(at, at + count):
            sums[i] = part[m, i]
            for way in range(2):

                @pl.when(ends[1 - way])
                def _():
                    acc = (acc_l, acc_r)[way]
                    sums[i] = (sums[i].astype(F32) + acc[m, i].astype(F32)).astype(BF)

            source, copy = home(i)
            pl.when(source != pc.e)(lambda copy=copy: copy.start())
            pl.when(source == pc.e)(lambda i=i: keep_out(i).start())

    gather_t.finish()
    own_t.wait()
    t_hi, t_lo = split(tfull[...].reshape(TAPS, 2 * hid)[:taps])
    gw = dot32(sg_hi[...], t_hi, TN) + dot32(sg_hi[...], t_lo, TN) + dot32(sg_lo[...], t_hi, TN)
    ggate_ref[...] = gw[:, :hid]
    gup_ref[...] = gw[:, hid:]
    proj0 = dot32(s_ref[...], gm_ref[...], NT)
    proj1 = dot32(s_ref[...], stem_ref[...], NT)

    @pl.when(has_rows)
    def _():
        keep_out(pc.tile).wait()
        for k in range(1, EXP):
            e = (pc.e + k) % EXP
            rcopy(
                slots.at[pc.tile, e], slots.at[pc.tile, e], ct_ss.at[0], ct_rs.at[e], pc.exp, pc.partner
            ).wait_recv()

    gather_s = Gather(
        pc,
        slots.at[pc.tile % TILES],
        lambda rep: slots.at[pc.tile_of(rep) % TILES],
        sg_ss,
        sg_rs,
        lambda rep: pc.tile_of(rep) < TILES,
    )
    gather_s.start()
    gather_s.relay()
    gather_s.relay_far()
    scatter_t.finish()
    scatter_d.finish()
    gather_s.finish()

    def collect(k, _):
        for i in range(EXP):
            ret32[pl.ds(k * EXP * ROWS + i * ROWS, ROWS), :] = slots[k, i].astype(F32)
        return 0

    lax.fori_loop(0, TILES, collect, 0)
    count = TILES * EXP * ROWS
    hot_row = [(iota((count, tok), 0) == full_id(p, r)).astype(F32) for p, r in zip(pos_row, r_row)]
    hot_col = sum((iota((tok, count), 1) == full_id(p, r)).astype(F32) for p, r in zip(pos_col, r_col)).astype(BF)
    tail = ret32[:, pl.ds(dm, SIDE)]
    gg_slot = tail[:, TAPS : TAPS + 1] + tail[:, TAPS + 1 : TAPS + 2]
    gg_row = [jnp.sum(h * gg_slot, axis=0, keepdims=True) for h in hot_row]
    b = dot32(tail.astype(BF), (hot_row[0] + hot_row[1]).astype(BF), TN)[:taps]
    mean = gg_row[0] * gates[0] + gg_row[1] * gates[1]
    grad_picked = [(g - mean) / total * (c * (1.0 - c)) for g, c in zip(gg_row, chosen)]
    grad_logits = sel_row[0] * grad_picked[0] + sel_row[1] * grad_picked[1]
    b = b + rstd_row * jnp.dot(rproj, grad_logits, precision=lax.Precision.HIGHEST, preferred_element_type=F32)
    c_row = jnp.sum(pt * b, axis=0, keepdims=True) * (rstd_row * rstd_row * (1.0 / dm))
    proj = proj0 + b - c_row * proj1
    rows3 = []
    for i in range(3):
        rows3.append(
            sum(shifted(proj[(3 * i + j) * chan : (3 * i + j + 1) * chan], 1 - j) for j in range(3))
        )
    a_out[0] = rows3[0][:, :wide]
    a_out[1] = rows3[2][:, wide:]
    hb = (
        rcopy(a_out.at[0], a_next, hb_ss.at[0], hb_rs.at[0], pc.exp - 1, pc.rep),
        rcopy(a_out.at[1], a_prev, hb_ss.at[1], hb_rs.at[1], pc.exp + 1, pc.rep),
    )
    pl.when(jnp.logical_not(first_row))(lambda: hb[0].start())
    pl.when(jnp.logical_not(last_row))(lambda: hb[1].start())
    out = dot32(hot_col, ret32[:, pl.ds(0, dm)].astype(BF))
    mixed_ref[...] = (stem_ref[...].astype(F32) + out).astype(BF)
    glat_ref[0] = rows3[0][:, wide:] + rows3[1][:, :wide]
    glat_ref[1] = rows3[1][:, wide:] + rows3[2][:, :wide]

    @pl.when(jnp.logical_not(last_row))
    def _():
        rcopy(a_out.at[0], a_next, hb_ss.at[0], hb_rs.at[0], pc.exp, pc.partner).wait_recv()
        glat_ref[1] = glat_ref[1] + a_next[...]

    @pl.when(jnp.logical_not(first_row))
    def _():
        rcopy(a_out.at[1], a_prev, hb_ss.at[1], hb_rs.at[1], pc.exp, pc.partner).wait_recv()
        glat_ref[0] = glat_ref[0] + a_prev[...]

    for copy in (ha[1], hb[0]):
        pl.when(jnp.logical_not(first_row))(copy.wait_send)
    for copy in (ha[0], hb[1]):
        pl.when(jnp.logical_not(last_row))(copy.wait_send)

    @pl.when(has_rows)
    def _():
        for k in range(1, EXP):
            stage(k, False).wait_send()
            stage(k, True).wait_send()

    def drain(s, _):
        for way, p in ((0, m - s), (1, m + s)):

            @pl.when(((p >= 0) if way == 0 else (p < SH)) & ends[way])
            def _():
                hop_side(way, p, s).wait_send()
                for c in range(len(CHUNKS)):
                    hop(way, p, c, s).wait_send()

        for way, ok in ((0, s > m), (1, s < m)):

            @pl.when(ok & ends[way])
            def _():
                for c in range(len(CHUNKS)):
                    give(way, s, c).wait_send()

        return 0

    lax.fori_loop(0, SH, drain, 0)
    for i in range(TILES):
        source, copy = home(i)
        pl.when(source != pc.e)(lambda copy=copy: copy.wait_send())


def local(latent, stem_weight, norm_gain, router_weight, routes, gate_weight, up_weight, down_weight, grad_mixed):
    tok, dm = grad_mixed.shape
    dsl, hid = gate_weight.shape
    rows_here, chan, wide = latent.shape
    taps = stem_weight.shape[0]
    full = dm + SIDE
    dma = pltpu.SemaphoreType.DMA
    chunks = len(CHUNKS)
    v = pltpu.VMEM
    return pl.pallas_call(
        layer_kernel,
        out_shape=(
            jax.ShapeDtypeStruct((tok, dm), BF),
            jax.ShapeDtypeStruct((rows_here, chan, wide), F32),
            jax.ShapeDtypeStruct((dsl, hid), F32),
            jax.ShapeDtypeStruct((dsl, hid), F32),
            jax.ShapeDtypeStruct((hid, dsl), F32),
        ),
        in_specs=[VM] * 10,
        out_specs=(VM,) * 5,
        scratch_shapes=[
            v((EXP, ROWS, dm), BF),
            v((EXP, ROWS, SIDE), BF),
            v((SH, TILES, ROWS, dm), BF),
            v((SH, TILES, ROWS, SIDE), BF),
            v((dsl, hid), BF),
            v((REP, dsl, hid), BF),
            v((2, 4, TP, 2 * hid), F32),
            v((TP, 2 * hid), F32),
            v((REP, TP, 2 * hid), F32),
            v((chan, wide), BF),
            v((chan, wide), BF),
            v((4, chan, wide), F32),
            v((SIDE, tok), F32),
            v((tok, dm), BF),
            v((taps, dsl), BF),
            v((taps, dsl), BF),
            v((SH * PIECE, dm), F32),
            v((SH * PIECE, dm), BF),
            v((SH * PIECE, hid), BF),
            v((SH * PIECE, 2 * hid), BF),
            v((SH, TILES, ROWS, full), BF),
            v((SH, TILES, ROWS, full), BF),
            v((SH, TILES, ROWS, full), BF),
            v((TILES, ROWS, full), BF),
            v((SH * PIECE, full), F32),
            v((TILES, EXP, ROWS, full), BF),
            v((2, 4, hid, dsl), BF),
            v((2, 4, TP, 2 * hid), F32),
            v((TP, 2 * hid), F32),
            v((REP, TP, 2 * hid), F32),
            v((2, chan, wide), F32),
            v((chan, wide), F32),
            v((chan, wide), F32),
        ]
        + scatter_scratch((TP, 2 * hid), F32)
        + scatter_scratch((hid, dsl), BF)
        + scatter_scratch((TP, 2 * hid), F32)
        + gather_scratch() * 4
        + [
            dma((EXP,)),
            dma((TILES,)),
            dma((EXP,)),
            dma((TILES,)),
            dma((2, SH, chunks)),
            dma((SH, chunks)),
            dma((2, SH)),
            dma((SH,)),
            dma((SH, chunks)),
            dma((SH, chunks)),
            dma((SH, chunks)),
            dma((TILES,)),
            dma((EXP,)),
            dma((2,)),
            dma((2,)),
            dma((2,)),
            dma((2,)),
            dma((6,)),
        ],
        compiler_params=pltpu.CompilerParams(collective_id=0, has_side_effects=True),
        name="layer",
    )(
        latent, stem_weight, norm_gain.reshape(1, -1), router_weight.T, routes, routes.T,
        gate_weight, up_weight, down_weight, grad_mixed,
    )


def solution(mesh):
    return jax.shard_map(
        local,
        mesh=mesh,
        in_specs=(
            P("exp", None, None),
            P(),
            P(),
            P(),
            P("exp", None),
            P("rep", "exp"),
            P("rep", "exp"),
            P("exp", "rep"),
            P("exp", None),
        ),
        out_specs=(P("exp", None), P("exp", None, None), P("rep", "exp"), P("rep", "exp"), P("exp", "rep")),
        check_vma=False,
    )
```

```python
import jax
import jax.numpy as jnp
from jax import lax
from jax.experimental import pallas as pl
from jax.experimental.pallas import tpu as pltpu
from jax.sharding import PartitionSpec as P

F32 = jnp.float32
BF = jnp.bfloat16
I32 = jnp.int32
EXP = 8
SH = 8
REP = 8
TILES = 5
ROWS = 8
PIECE = TILES * ROWS
CHUNKS = ((0, 2), (2, 2), (4, 1))
TAPS = 192
TP = TAPS // REP
SIDE = 256
MESH = pl.DeviceIdType.MESH
VM = pl.BlockSpec(memory_space=pltpu.VMEM)


def dot32(a, b, dims=None):
    if dims is None:
        return jnp.dot(a, b, preferred_element_type=F32)
    return lax.dot_general(a, b, (dims, ((), ())), preferred_element_type=F32)


NT = ((1,), (1,))
TN = ((0,), (0,))


def split(v):
    hi = v.astype(BF)
    return hi, (v - hi.astype(F32)).astype(BF)


def iota(shape, dim):
    return lax.broadcasted_iota(I32, shape, dim)


def rcopy(src, dst, ssem, rsem, exp, rep):
    return pltpu.make_async_remote_copy(
        src_ref=src, dst_ref=dst, send_sem=ssem, recv_sem=rsem, device_id={"exp": exp, "rep": rep}, device_id_type=MESH
    )


class Place:
    def __init__(self):
        self.exp = lax.axis_index("exp")
        self.rep = lax.axis_index("rep")
        self.e = self.exp // SH
        self.half = self.e % 2
        self.x = self.e // 2
        self.m = self.exp % SH
        self.y = self.rep // 2
        self.c = self.rep % 2
        self.tile = self.tile_of(self.rep)
        self.d = 1 - 2 * self.c
        self.fwd = self.rep_at(self.d)
        self.bwd = self.rep_at(-self.d)
        self.partner = self.y * 2 + 1 - self.c

    def rep_at(self, dy):
        return ((self.y + dy + 4) % 4) * 2 + self.c

    def tile_of(self, rep):
        return (rep + 3 * self.e) % 8

    def greet(self):
        bar = pltpu.get_barrier_semaphore()

        def hello(exp, rep):
            pl.semaphore_signal(bar, inc=1, device_id={"exp": exp, "rep": rep}, device_id_type=MESH)

        for rep in (self.fwd, self.bwd, self.partner):
            hello(self.exp, rep)

        def body(n, _):
            hello((self.exp + n) % (EXP * SH), self.rep)
            return 0

        lax.fori_loop(1, EXP * SH, body, 0)

    def enter(self):
        pl.semaphore_wait(pltpu.get_barrier_semaphore(), EXP * SH + 2)


class Gather:
    def __init__(self, pc, src, piece, ssem, rsem, valid=None):
        self.pc, self.src, self.piece, self.ssem, self.rsem = pc, src, piece, ssem, rsem
        self.valid = valid

    def guard(self, rep, fn):
        if self.valid is None:
            fn()
        else:
            pl.when(self.valid(rep))(fn)

    def copy(self, src, rep_of, k, target):
        return rcopy(src, self.piece(rep_of), self.ssem.at[k], self.rsem.at[rep_of], self.pc.exp, target)

    def moves(self):
        pc = self.pc
        far = pc.rep_at(2)
        own, part = pc.rep, pc.partner
        return [
            (self.src, own, 0, pc.fwd),
            (self.src, own, 1, pc.bwd),
            (self.src, own, 2, part),
            (self.piece(pc.bwd), pc.bwd, 3, pc.fwd),
            (self.piece(pc.bwd), pc.bwd, 4, part),
            (self.piece(pc.fwd), pc.fwd, 5, part),
            (self.piece(far), far, 6, part),
        ]

    def start(self):
        def go():
            for mv in self.moves()[:3]:
                self.copy(*mv).start()

        self.guard(self.pc.rep, go)

    def arrive(self, rep):
        self.copy(self.piece(rep), rep, 0, self.pc.partner).wait_recv()

    def relay(self):
        mv = self.moves()

        def near():
            self.arrive(self.pc.bwd)
            self.copy(*mv[3]).start()
            self.copy(*mv[4]).start()

        self.guard(self.pc.bwd, near)

        def other():
            self.arrive(self.pc.fwd)
            self.copy(*mv[5]).start()

        self.guard(self.pc.fwd, other)

    def relay_far(self):
        far = self.pc.rep_at(2)

        def go():
            self.arrive(far)
            self.copy(*self.moves()[6]).start()

        self.guard(far, go)

    def finish(self):
        for dy in range(4):
            rep = ((self.pc.y + dy) % 4) * 2 + 1 - self.pc.c
            self.guard(rep, lambda rep=rep: self.arrive(rep))
        for mv in self.moves():
            self.guard(mv[1], lambda mv=mv: self.copy(*mv).wait_send())


class Scatter:
    def __init__(self, pc, src, got, total, side, ssem, rsem):
        self.pc, self.src, self.got, self.total, self.side, self.ssem, self.rsem = pc, src, got, total, side, ssem, rsem

    def copy(self, k):
        pc = self.pc
        y, d = pc.y, pc.d
        at = lambda dy: self.total.at[(y + dy + 4) % 4]
        src, dst, rep = (
            (self.src.at[1 - pc.c], self.got, pc.partner),
            (at(2), self.side.at[0], pc.fwd),
            (at(-d), self.side.at[1], pc.bwd),
            (at(d), self.side.at[2], pc.fwd),
        )[k]
        return rcopy(src, dst, self.ssem.at[k], self.rsem.at[k], pc.exp, rep)

    def start(self):
        self.copy(0).start()

    def add(self):
        self.copy(0).wait_recv()

        def body(k, _):
            self.total[k] = (self.src[self.pc.c, k].astype(F32) + self.got[k].astype(F32)).astype(self.total.dtype)
            return 0

        lax.fori_loop(0, 4, body, 0)
        self.copy(1).start()
        self.copy(2).start()

    def pass_on(self):
        pc = self.pc
        self.copy(1).wait_recv()
        at = (pc.y + pc.d + 4) % 4
        self.total[at] = (self.total[at].astype(F32) + self.side[0].astype(F32)).astype(self.total.dtype)
        self.copy(3).start()

    def result(self):
        self.copy(2).wait_recv()
        self.copy(3).wait_recv()
        return self.total[self.pc.y].astype(F32) + self.side[1].astype(F32) + self.side[2].astype(F32)

    def finish(self):
        for k in range(4):
            self.copy(k).wait_send()


def scatter_scratch(block, dtype):
    return [
        pltpu.VMEM((4,) + block, dtype),
        pltpu.VMEM((4,) + block, dtype),
        pltpu.VMEM((3,) + block, dtype),
        pltpu.SemaphoreType.DMA((4,)),
        pltpu.SemaphoreType.DMA((4,)),
    ]


def gather_scratch():
    return [pltpu.SemaphoreType.DMA((7,)), pltpu.SemaphoreType.DMA((REP,))]


def layer_kernel(
    latent, s_ref, gain_ref, wr_ref, routes_ref, wg_ref, wu_ref, wd_ref, gm_ref,
    mixed_ref, glat_ref, ggate_ref, gup_ref, gdown_ref,
    send, send_side, recv, recv_side, wfull, gp, gmine, gfull,
    h_prev, h_next, lat4, ptx, stem_ref, sg_hi, sg_lo,
    row32, side32, gm_all, hg_ref, dpre_ref,
    part, acc_l, acc_r, sums, ret32, send_back, back_in, bsum, back_all, slots, dp, tp, tmine, tfull, a_out, a_prev, a_next,
    *sems
):
    (g_got, g_tot, g_side, g_ss, g_rs, d_got, d_tot, d_side, d_ss, d_rs, t_got, t_tot, t_side, t_ss, t_rs,
     ag_ss, ag_rs, wg_ss, wg_rs, tg_ss, tg_rs, bg_ss, bg_rs, s0_ss, s0_rs, s1_ss, s1_rs,
     st_ss, st_rs, sd_ss, sd_rs, ln_ss, ln_rs, ca_ss, cl_rs, cr_rs, ct_ss, ct_rs, bk_ss, bo_ss, bk_rs,
     ha_ss, ha_rs, hb_ss, hb_rs, loc) = sems
    pc = Place()
    m = pc.m
    tok, dm = gm_ref.shape
    hid = wg_ref.shape[1]
    taps = s_ref.shape[0]
    wide = tok // 2
    top = routes_ref.shape[0]
    has_rows = pc.tile < TILES

    pc.greet()

    upper = (iota((tok, tok), 0) < iota((tok, tok), 1)).astype(BF)
    r_row = [routes_ref[k : k + 1, :] for k in range(top)]
    sel_row = [(iota((EXP, tok), 0) == r).astype(F32) for r in r_row]
    before_row = dot32((sel_row[0] + sel_row[1]).astype(BF), upper)
    pos_row = [jnp.sum(s * before_row, axis=0, keepdims=True).astype(I32) for s in sel_row]

    def here_id(pos, r):
        q = pos - ROWS * pc.tile
        return jnp.where((q >= 0) & (q < ROWS), r * ROWS + q, -1)

    def full_id(pos, r):
        t = lax.shift_right_logical(pos, 3)
        place = (r & 1) * (EXP // 2) + lax.shift_right_logical(r, 1)
        return t * (EXP * ROWS) + place * ROWS + (pos - t * ROWS)

    hot_here = [(iota((EXP * ROWS, tok), 0) == here_id(p, r)).astype(F32) for p, r in zip(pos_row, r_row)]
    hot_here_b = [h.astype(BF) for h in hot_here]
    picked_rows = dot32(hot_here_b[0] + hot_here_b[1], gm_ref[...])
    for e in range(EXP):
        send[e] = picked_rows[e * ROWS : (e + 1) * ROWS].astype(BF)

    pc.enter()

    ha = (
        rcopy(latent.at[1], h_prev, ha_ss.at[0], ha_rs.at[0], pc.exp + 1, pc.rep),
        rcopy(latent.at[0], h_next, ha_ss.at[1], ha_rs.at[1], pc.exp - 1, pc.rep),
    )
    first_row, last_row = pc.exp == 0, pc.exp == EXP * SH - 1
    pl.when(jnp.logical_not(last_row))(lambda: ha[0].start())
    pl.when(jnp.logical_not(first_row))(lambda: ha[1].start())

    def stage(k):
        peer = (pc.e + k) % EXP
        return rcopy(send.at[peer], recv.at[m, pc.tile], st_ss.at[k], st_rs.at[pc.tile], peer * SH + m, pc.rep)

    keep_gm = pltpu.make_async_copy(send.at[pc.e], recv.at[m, pc.tile], loc.at[0])

    @pl.when(has_rows)
    def _():
        for k in (1, 7, 2, 6, 3, 5, 4):
            stage(k).start()
        keep_gm.start()

    gather_w = Gather(pc, wd_ref, lambda rep: wfull.at[rep], wg_ss, wg_rs)
    own_w = pltpu.make_async_copy(wd_ref, wfull.at[pc.rep], loc.at[2])
    gather_w.start()
    own_w.start()

    gain = gain_ref[...].reshape(1, dm)
    dsl = wg_ref.shape[0]
    sg = s_ref[...].astype(F32) * gain
    hi, lo = split(sg)
    pick = (iota((dm, dsl), 0) == iota((dm, dsl), 1) + pc.rep * dsl).astype(BF)
    s_hi = dot32(hi, pick).astype(BF)
    s_lo = dot32(lo, pick).astype(BF)
    sg_hi[...] = s_hi
    sg_lo[...] = s_lo
    zero_taps = jnp.zeros((TAPS - taps, 2 * hid), F32)
    share = jnp.concatenate(
        [dot32(s_hi, w[...]) + dot32(s_lo, w[...]) for w in (wg_ref, wu_ref)], axis=1
    )
    share = jnp.concatenate([share, zero_taps], axis=0)
    for k in range(REP):
        gp[k // 4, k % 4] = share[k * TP : (k + 1) * TP]
    rproj = dot32(hi, wr_ref[...], NT) + dot32(lo, wr_ref[...], NT)
    scatter_g = Scatter(pc, gp, g_got, g_tot, g_side, g_ss, g_rs)
    scatter_g.start()

    @pl.when(jnp.logical_not(first_row))
    def _():
        rcopy(latent.at[1], h_prev, ha_ss.at[0], ha_rs.at[0], pc.exp, pc.partner).wait_recv()
        lat4[0] = h_prev[...].astype(F32)

    @pl.when(first_row)
    def _():
        lat4[0] = jnp.zeros(lat4.shape[1:], F32)

    @pl.when(jnp.logical_not(last_row))
    def _():
        rcopy(latent.at[0], h_next, ha_ss.at[1], ha_rs.at[1], pc.exp, pc.partner).wait_recv()
        lat4[3] = h_next[...].astype(F32)

    @pl.when(last_row)
    def _():
        lat4[3] = jnp.zeros(lat4.shape[1:], F32)

    lat4[1] = latent[0].astype(F32)
    lat4[2] = latent[1].astype(F32)
    chan = lat4.shape[1]
    col = iota((chan, tok), 1)
    col = jnp.where(col >= wide, col - wide, col)

    def shifted(v, by):
        if by == 0:
            return v
        rolled = pltpu.roll(v, (-by) % tok, 1)
        return jnp.where(col == (0 if by < 0 else wide - 1), 0.0, rolled)

    for i in range(3):
        two = jnp.concatenate([lat4[i], lat4[i + 1]], axis=1)
        for j in range(3):
            ptx[pl.ds((3 * i + j) * chan, chan), :] = shifted(two, j - 1)
    ptx[pl.ds(taps, SIDE - taps), :] = jnp.zeros((SIDE - taps, tok), F32)
    pt = ptx[pl.ds(0, taps), :]
    stem = dot32(pt.astype(BF), s_ref[...], TN).astype(BF)
    stem_ref[...] = stem
    sv = stem.astype(F32)
    rstd = lax.rsqrt(jnp.mean(sv * sv, axis=-1, keepdims=True) + 1e-06)
    rstd_row = jnp.transpose(jnp.broadcast_to(rstd, (tok, tok)))[0:1, :]
    normed = (sv * rstd * gain).astype(BF)
    logits = dot32(wr_ref[...], normed, NT)
    picked = [jnp.sum(s * logits, axis=0, keepdims=True) for s in sel_row]
    chosen = [jax.nn.sigmoid(p) for p in picked]
    total = chosen[0] + chosen[1]
    gates = [c / total for c in chosen]
    r_hi, r_lo = split(rstd_row)
    ptx[pl.ds(TAPS, 1), :] = r_hi.astype(F32)
    ptx[pl.ds(TAPS + 1, 1), :] = r_lo.astype(F32)
    side = jnp.zeros((EXP * ROWS, SIDE), F32)
    for k in range(top):
        k_hi, k_lo = split(gates[k])
        ptx[pl.ds(TAPS + 2, 1), :] = k_hi.astype(F32)
        ptx[pl.ds(TAPS + 3, 1), :] = k_lo.astype(F32)
        side = side + dot32(hot_here_b[k], ptx[...].astype(BF), NT)
    for e in range(EXP):
        send_side[e] = side[e * ROWS : (e + 1) * ROWS].astype(BF)

    def to_all(n):
        dest = (pc.exp + n) % (EXP * SH)
        e = dest // SH
        return rcopy(send_side.at[e], recv_side.at[m, pc.tile], sd_ss.at[e], sd_rs.at[m], dest, pc.rep)

    @pl.when(has_rows)
    def _():
        def body(n, _):
            to_all(n).start()
            return 0

        lax.fori_loop(1, EXP * SH, body, 0)
        pltpu.make_async_copy(send_side.at[pc.e], recv_side.at[m, pc.tile], sd_rs.at[m]).start()

    ends = (m < SH - 1, m > 0)

    def hop(way, p, c, s):
        at = pl.ds(CHUNKS[c][0], CHUNKS[c][1])
        ref = recv.at[p, at]
        return rcopy(ref, ref, ln_ss.at[way, s], ln_rs.at[p, c], pc.exp + 1 - 2 * way, pc.rep)

    def arrived(i):
        source = (5 * (pc.rep - i + 8)) % 8

        @pl.when(source != pc.e)
        def _():
            rcopy(recv.at[m, i], recv.at[m, i], st_ss.at[0], st_rs.at[i], pc.exp, pc.partner).wait_recv()

    def widen(p):
        for i in range(TILES):
            row32[pl.ds(pl.multiple_of(p * PIECE + i * ROWS, ROWS), ROWS), :] = recv[p, i].astype(F32)

    def step(s, _):
        for c in range(len(CHUNKS)):
            for way, p in ((0, m - s), (1, m + s)):
                ok = (p >= 0) if way == 0 else (p < SH)

                @pl.when(ok)
                def _():
                    hop(way, p, c, s).wait_recv()

                    @pl.when(ends[way])
                    def _():
                        hop(way, p, c, s).start()

        for way, p in ((0, m - s), (1, m + s)):
            pl.when((p >= 0) if way == 0 else (p < SH))(lambda p=p: widen(p))
        return 0

    scatter_g.add()

    @pl.when(has_rows)
    def _():
        keep_gm.wait()

    for c, (at, count) in enumerate(CHUNKS):
        for i in range(at, at + count):
            arrived(i)
        for way in range(2):
            pl.when(ends[way])(lambda way=way, c=c: hop(way, m, c, 0).start())
    widen(m)
    scatter_g.pass_on()
    gather_w.relay()
    lax.fori_loop(1, 2, step, 0)
    gmine[...] = scatter_g.result()
    spot = lambda ref: lambda rep: ref.at[(rep % 2) * 4 + rep // 2]
    gather_g = Gather(pc, gmine, spot(gfull), ag_ss, ag_rs)
    own_g = pltpu.make_async_copy(gmine, spot(gfull)(pc.rep), loc.at[3])
    gather_g.start()
    own_g.start()
    gather_w.relay_far()
    lax.fori_loop(2, 3, step, 0)
    gather_g.relay()
    lax.fori_loop(3, 4, step, 0)
    gather_g.relay_far()
    lax.fori_loop(4, 7, step, 0)
    gather_g.finish()
    gather_w.finish()
    scatter_g.finish()
    own_w.wait()
    own_g.wait()

    def widen_side(p, _):
        pltpu.make_async_copy(recv_side.at[p], recv_side.at[p], sd_rs.at[p]).wait()
        for i in range(TILES):
            side32[pl.ds(pl.multiple_of(p * PIECE + i * ROWS, ROWS), ROWS), :] = recv_side[p, i].astype(F32)
        return 0

    lax.fori_loop(0, SH, widen_side, 0)
    more = side32[...]
    pr = more[:, :TAPS].astype(BF)
    rs = more[:, TAPS : TAPS + 1] + more[:, TAPS + 1 : TAPS + 2]
    gt = more[:, TAPS + 2 : TAPS + 3] + more[:, TAPS + 3 : TAPS + 4]
    g_hi, g_lo = split(gfull[...].reshape(TAPS, 2 * hid))
    pre = rs * (dot32(pr, g_hi) + dot32(pr, g_lo))
    pg, pu = pre[:, :hid], pre[:, hid:]
    sigma = jax.nn.sigmoid(pg)
    silu = pg * sigma
    hidden = silu * pu
    slope = pu * sigma * (1.0 + pg * (1.0 - sigma))
    hg = (gt * hidden).astype(BF)
    down_t = wfull[...].reshape(dm, hid)
    ret32[...] = dot32(hg, down_t, NT)
    hg_ref[...] = hg

    def give(way, p, c):
        at = pl.ds(CHUNKS[c][0], CHUNKS[c][1])
        dst, rsem = ((acc_l, cl_rs), (acc_r, cr_rs))[way]
        return rcopy(
            part.at[p, at], dst.at[p, at], ca_ss.at[p], rsem.at[p, c], pc.exp + 1 - 2 * way, pc.rep
        )

    def mine(p, i):
        return ret32[pl.ds(pl.multiple_of(p * PIECE + i * ROWS, ROWS), ROWS), :]

    def step_sum(tau, _):
        for c, (at, count) in enumerate(CHUNKS):
            for way, p in ((0, 7 - tau + m), (1, tau - 7 + m)):
                ok = (tau >= m) if way == 0 else (p >= 0)
                acc = (acc_l, acc_r)[way]

                @pl.when(ok & ends[1 - way])
                def _():
                    give(way, p, c).wait_recv()
                    for i in range(at, at + count):
                        part[p, i] = (mine(p, i) + acc[p, i].astype(F32)).astype(BF)

                @pl.when(ok & jnp.logical_not(ends[1 - way]))
                def _():
                    for i in range(at, at + count):
                        part[p, i] = mine(p, i).astype(BF)

                pl.when(ok & ends[way])(lambda: give(way, p, c).start())

        return 0

    def steps(at, to):
        lax.fori_loop(at, to, step_sum, 0)

    steps(0, 1)
    lax.fori_loop(7, 8, step, 0)

    gm_all[...] = row32[...].astype(BF)
    u = dot32(gm_all[...], down_t)
    gg = jnp.sum(hidden * u, axis=-1, keepdims=True)
    gu = (rs * gt) * u
    dpre = jnp.concatenate([gu * slope, gu * silu], axis=1).astype(BF)
    dpre_ref[...] = dpre
    back = dot32(dpre, g_hi, NT) + dot32(dpre, g_lo, NT)
    gg_hi = gg.astype(BF).astype(F32)
    lane = iota((SH * PIECE, SIDE - TAPS), 1)
    tail = jnp.where(lane == 0, gg_hi, jnp.where(lane == 1, gg - gg_hi, 0.0))
    side32[...] = jnp.concatenate([back, tail], axis=1)
    place = pc.half * (EXP // 2) + pc.x

    def source_of(i):
        return (5 * (pc.rep - i + 8)) % 8

    def reply(p, i, sem):
        return rcopy(send_back.at[p, i], back_in.at[m, place], sem, bk_rs.at[0], source_of(i) * SH + p, pc.rep)

    def narrow(n, _):
        p = (m + n) % SH
        for i in range(TILES):
            send_back[p, i] = side32[pl.ds(pl.multiple_of(p * PIECE + i * ROWS, ROWS), ROWS), :].astype(BF)
        for i in range(TILES):
            pl.when(p != m)(lambda i=i: reply(p, i, bk_ss.at[p]).start())

            @pl.when((p == m) & (source_of(i) != pc.e))
            def _():
                reply(p, i, bo_ss.at[i]).start()

            @pl.when((p == m) & (source_of(i) == pc.e))
            def _():
                pltpu.make_async_copy(send_back.at[p, i], back_in.at[m, place], bk_rs.at[0]).start()

        return 0

    lax.fori_loop(0, SH, narrow, 0)
    steps(1, 2)
    t_share = dot32(pr, dpre_ref[...], TN)
    for k in range(REP):
        tp[k // 4, k % 4] = t_share[k * TP : (k + 1) * TP]
    scatter_t = Scatter(pc, tp, t_got, t_tot, t_side, t_ss, t_rs)
    scatter_t.start()
    d_share = dot32(gm_all[...], hg_ref[...], TN)
    for k in range(REP):
        dp[k % 2, k // 2] = d_share[k * dsl : (k + 1) * dsl].astype(BF)
    scatter_d = Scatter(pc, dp, d_got, d_tot, d_side, d_ss, d_rs)
    scatter_d.start()
    steps(2, 3)
    scatter_t.add()
    scatter_d.add()
    steps(3, 4)
    scatter_t.pass_on()
    scatter_d.pass_on()
    steps(4, 5)
    tmine[...] = scatter_t.result()
    gather_t = Gather(pc, tmine, spot(tfull), tg_ss, tg_rs)
    own_t = pltpu.make_async_copy(tmine, spot(tfull)(pc.rep), loc.at[4])
    gather_t.start()
    own_t.start()
    with_rows = lambda rep: pc.tile_of(rep) < TILES
    tile_at = lambda rep: pc.tile_of(rep) % TILES
    gather_b = Gather(pc, bsum, lambda rep: back_all.at[tile_at(rep)], bg_ss, bg_rs, with_rows)
    own_b = pltpu.make_async_copy(bsum, back_all.at[pc.tile % TILES], loc.at[1])

    @pl.when(has_rows)
    def _():
        pltpu.make_async_copy(back_in, back_in, bk_rs.at[0]).wait()
        for k in range(EXP):
            bsum[k] = sum(back_in[j, k].astype(F32) for j in range(SH)).astype(BF)
        own_b.start()

    gather_b.start()
    gdown_ref[...] = scatter_d.result()
    steps(5, 6)
    gather_t.relay()
    gather_b.relay()
    steps(6, 7)

    def home(i):
        source = source_of(i)
        return source, rcopy(
            sums.at[i], slots.at[i, pc.half, pc.x], ct_ss.at[i], ct_rs.at[pc.half], source * SH + m, pc.rep
        )

    keep_out = lambda i: pltpu.make_async_copy(sums.at[i], slots.at[i, pc.half, pc.x], ct_rs.at[pc.half])
    for c, (at, count) in enumerate(CHUNKS):
        for way in range(2):
            pl.when(ends[1 - way])(lambda way=way, c=c: give(way, m, c).wait_recv())
        for i in range(at, at + count):
            @pl.when(m == 0)
            def _():
                sums[i] = (mine(m, i) + acc_r[m, i].astype(F32)).astype(BF)

            @pl.when(m == SH - 1)
            def _():
                sums[i] = (mine(m, i) + acc_l[m, i].astype(F32)).astype(BF)

            @pl.when(ends[0] & ends[1])
            def _():
                sums[i] = (mine(m, i) + acc_l[m, i].astype(F32) + acc_r[m, i].astype(F32)).astype(BF)

            source, copy = home(i)
            pl.when(source != pc.e)(lambda copy=copy: copy.start())
            pl.when(source == pc.e)(lambda i=i: keep_out(i).start())

    def out_gather(h, ss, rs):
        half = (pc.half + h) % 2
        ready = slots.at[pc.tile % TILES, half]
        gather = Gather(pc, ready, lambda rep: slots.at[tile_at(rep), half], ss, rs, with_rows)
        wait = pltpu.make_async_copy(ready, ready, ct_rs.at[half])
        return gather, wait

    (near, near_wait), (away, away_wait) = out_gather(0, s0_ss, s0_rs), out_gather(1, s1_ss, s1_rs)
    gather_t.relay_far()
    gather_b.relay_far()
    pl.when(has_rows)(near_wait.wait)
    near.start()
    gather_t.finish()
    own_t.wait()
    t_hi, t_lo = split(tfull[...].reshape(TAPS, 2 * hid)[:taps])
    gw = dot32(sg_hi[...], t_hi, TN) + dot32(sg_hi[...], t_lo, TN) + dot32(sg_lo[...], t_hi, TN)
    ggate_ref[...] = gw[:, :hid]
    gup_ref[...] = gw[:, hid:]
    pl.when(has_rows)(away_wait.wait)
    away.start()
    near.relay()
    pl.when(has_rows)(own_b.wait)
    gather_b.finish()

    for t in range(TILES):
        for k in range(EXP):
            side32[pl.ds((t * EXP + k) * ROWS, ROWS), :] = back_all[t, k].astype(F32)
    count = TILES * EXP * ROWS
    full_row = [full_id(p, r) for p, r in zip(pos_row, r_row)]
    hot_row = [(iota((count, tok), 0) == f).astype(F32) for f in full_row]
    tail = side32[...]
    gg_slot = tail[:, TAPS : TAPS + 1] + tail[:, TAPS + 1 : TAPS + 2]
    gg_row = [jnp.sum(h * gg_slot, axis=0, keepdims=True) for h in hot_row]
    b = dot32(tail.astype(BF), (hot_row[0] + hot_row[1]).astype(BF), TN)[:taps]
    mean = gg_row[0] * gates[0] + gg_row[1] * gates[1]
    grad_picked = [(g - mean) / total * (c * (1.0 - c)) for g, c in zip(gg_row, chosen)]
    grad_logits = sel_row[0] * grad_picked[0] + sel_row[1] * grad_picked[1]
    b = b + rstd_row * jnp.dot(rproj, grad_logits, precision=lax.Precision.HIGHEST, preferred_element_type=F32)
    c_row = jnp.sum(pt * b, axis=0, keepdims=True) * (rstd_row * rstd_row * (1.0 / dm))
    proj0 = dot32(s_ref[...], gm_ref[...], NT)
    proj1 = dot32(s_ref[...], stem_ref[...], NT)
    proj = proj0 + b - c_row * proj1
    away.relay()
    near.relay_far()
    rows3 = []
    for i in range(3):
        rows3.append(
            sum(shifted(proj[(3 * i + j) * chan : (3 * i + j + 1) * chan], 1 - j) for j in range(3))
        )
    a_out[0] = rows3[0][:, :wide]
    a_out[1] = rows3[2][:, wide:]
    hb = (
        rcopy(a_out.at[0], a_next, hb_ss.at[0], hb_rs.at[0], pc.exp - 1, pc.rep),
        rcopy(a_out.at[1], a_prev, hb_ss.at[1], hb_rs.at[1], pc.exp + 1, pc.rep),
    )
    pl.when(jnp.logical_not(first_row))(lambda: hb[0].start())
    pl.when(jnp.logical_not(last_row))(lambda: hb[1].start())
    glat_ref[0] = rows3[0][:, wide:] + rows3[1][:, :wide]
    glat_ref[1] = rows3[1][:, wide:] + rows3[2][:, :wide]

    @pl.when(jnp.logical_not(last_row))
    def _():
        rcopy(a_out.at[0], a_next, hb_ss.at[0], hb_rs.at[0], pc.exp, pc.partner).wait_recv()
        glat_ref[1] = glat_ref[1] + a_next[...]

    @pl.when(jnp.logical_not(first_row))
    def _():
        rcopy(a_out.at[1], a_prev, hb_ss.at[1], hb_rs.at[1], pc.exp, pc.partner).wait_recv()
        glat_ref[0] = glat_ref[0] + a_prev[...]

    away.relay_far()
    square = [jnp.transpose(jnp.broadcast_to(f.astype(F32), (tok, tok)))[:, :1].astype(I32) for f in full_row]
    hot_col = sum((iota((tok, count), 1) == f).astype(F32) for f in square).astype(BF)

    for copy in (ha[1], hb[0]):
        pl.when(jnp.logical_not(first_row))(copy.wait_send)
    for copy in (ha[0], hb[1]):
        pl.when(jnp.logical_not(last_row))(copy.wait_send)
    scatter_t.finish()
    scatter_d.finish()

    @pl.when(has_rows)
    def _():
        for k in range(1, EXP):
            stage(k).wait_send()

        def body(k, _):
            rcopy(send_side, send_side, sd_ss.at[(pc.e + k) % EXP], sd_rs.at[0], pc.exp, pc.partner).wait_send()
            return 0

        lax.fori_loop(1, EXP, body, 0)
        seven = send_side.at[pl.ds(0, EXP - 1)]
        rcopy(seven, seven, sd_ss.at[pc.e], sd_rs.at[0], pc.exp, pc.partner).wait_send()

    def drain(s, _):
        for way, p in ((0, m - s), (1, m + s)):

            @pl.when(((p >= 0) if way == 0 else (p < SH)) & ends[way])
            def _():
                rcopy(recv.at[p], recv.at[p], ln_ss.at[way, s], ln_rs.at[p, 0], pc.exp, pc.partner).wait_send()

        for way, ok in ((0, s > m), (1, s < m)):

            @pl.when(ok & ends[way])
            def _():
                rcopy(part.at[s], acc_l.at[s], ca_ss.at[s], cl_rs.at[s, 0], pc.exp, pc.partner).wait_send()

        @pl.when(s != m)
        def _():
            rcopy(send_back.at[s], send_back.at[s], bk_ss.at[s], bk_rs.at[0], pc.exp, pc.partner).wait_send()

        return 0

    lax.fori_loop(0, SH, drain, 0)
    for i in range(TILES):

        @pl.when(source_of(i) != pc.e)
        def _():
            home(i)[1].wait_send()
            reply(m, i, bo_ss.at[i]).wait_send()

    near.finish()
    away.finish()

    def collect(k, _):
        for i in range(EXP):
            at = pl.multiple_of(k * EXP * ROWS + i * ROWS, ROWS)
            ret32[pl.ds(at, ROWS), :] = slots[k, i // 4, i % 4].astype(F32)
        return 0

    lax.fori_loop(0, TILES, collect, 0)
    out = dot32(hot_col, ret32[...].astype(BF))
    mixed_ref[...] = (stem_ref[...].astype(F32) + out).astype(BF)


def local(latent, stem_weight, norm_gain, router_weight, routes, gate_weight, up_weight, down_weight, grad_mixed):
    tok, dm = grad_mixed.shape
    dsl, hid = gate_weight.shape
    rows_here, chan, wide = latent.shape
    taps = stem_weight.shape[0]
    dma = pltpu.SemaphoreType.DMA
    chunks = len(CHUNKS)
    v = pltpu.VMEM
    outs = pl.pallas_call(
        layer_kernel,
        out_shape=(
            jax.ShapeDtypeStruct((tok, dm), BF),
            jax.ShapeDtypeStruct((rows_here, chan, wide), F32),
            jax.ShapeDtypeStruct((dsl, hid), F32),
            jax.ShapeDtypeStruct((dsl, hid), F32),
            jax.ShapeDtypeStruct((dsl, hid), F32),
        ),
        in_specs=[VM] * 9,
        out_specs=(VM,) * 5,
        scratch_shapes=[
            v((EXP, ROWS, dm), BF),
            v((EXP, ROWS, SIDE), BF),
            v((SH, TILES, ROWS, dm), BF),
            v((SH, TILES, ROWS, SIDE), BF),
            v((REP, dsl, hid), BF),
            v((2, 4, TP, 2 * hid), F32),
            v((TP, 2 * hid), F32),
            v((REP, TP, 2 * hid), F32),
            v((chan, wide), BF),
            v((chan, wide), BF),
            v((4, chan, wide), F32),
            v((SIDE, tok), F32),
            v((tok, dm), BF),
            v((taps, dsl), BF),
            v((taps, dsl), BF),
            v((SH * PIECE, dm), F32),
            v((SH * PIECE, SIDE), F32),
            v((SH * PIECE, dm), BF),
            v((SH * PIECE, hid), BF),
            v((SH * PIECE, 2 * hid), BF),
            v((SH, TILES, ROWS, dm), BF),
            v((SH, TILES, ROWS, dm), BF),
            v((SH, TILES, ROWS, dm), BF),
            v((TILES, ROWS, dm), BF),
            v((SH * PIECE, dm), F32),
            v((SH, TILES, ROWS, SIDE), BF),
            v((SH, EXP, ROWS, SIDE), BF),
            v((EXP, ROWS, SIDE), BF),
            v((TILES, EXP, ROWS, SIDE), BF),
            v((TILES, 2, EXP // 2, ROWS, dm), BF),
            v((2, 4, dsl, hid), BF),
            v((2, 4, TP, 2 * hid), F32),
            v((TP, 2 * hid), F32),
            v((REP, TP, 2 * hid), F32),
            v((2, chan, wide), F32),
            v((chan, wide), F32),
            v((chan, wide), F32),
        ]
        + scatter_scratch((TP, 2 * hid), F32)
        + scatter_scratch((dsl, hid), BF)
        + scatter_scratch((TP, 2 * hid), F32)
        + gather_scratch() * 6
        + [
            dma((EXP,)),
            dma((TILES,)),
            dma((EXP,)),
            dma((SH,)),
            dma((2, SH)),
            dma((SH, chunks)),
            dma((SH,)),
            dma((SH, chunks)),
            dma((SH, chunks)),
            dma((TILES,)),
            dma((2,)),
            dma((SH,)),
            dma((TILES,)),
            dma((1,)),
            dma((2,)),
            dma((2,)),
            dma((2,)),
            dma((2,)),
            dma((6,)),
        ],
        compiler_params=pltpu.CompilerParams(collective_id=0, has_side_effects=True),
        name="layer",
    )(
        latent, stem_weight, norm_gain, router_weight.T, routes.T,
        gate_weight, up_weight, down_weight.T, grad_mixed,
    )
    return outs[:4] + (outs[4].T,)


def solution(mesh):
    return jax.shard_map(
        local,
        mesh=mesh,
        in_specs=(
            P("exp", None, None),
            P(),
            P(),
            P(),
            P("exp", None),
            P("rep", "exp"),
            P("rep", "exp"),
            P("exp", "rep"),
            P("exp", None),
        ),
        out_specs=(P("exp", None), P("exp", None, None), P("rep", "exp"), P("rep", "exp"), P("exp", "rep")),
        check_vma=False,
    )
```

```python
import jax
import jax.numpy as jnp
from jax import lax
from jax.experimental import pallas as pl
from jax.experimental.pallas import tpu as pltpu
from jax.sharding import PartitionSpec as P

F32 = jnp.float32
BF = jnp.bfloat16
I32 = jnp.int32
EXP = 8
SH = 8
REP = 8
TILES = 5
ROWS = 8
PIECE = TILES * ROWS
CHUNKS = ((0, 2), (2, 2), (4, 1))
TAPS = 192
TP = TAPS // REP
SIDE = 256
MESH = pl.DeviceIdType.MESH
VM = pl.BlockSpec(memory_space=pltpu.VMEM)


def dot32(a, b, dims=None):
    if dims is None:
        return jnp.dot(a, b, preferred_element_type=F32)
    return lax.dot_general(a, b, (dims, ((), ())), preferred_element_type=F32)


NT = ((1,), (1,))
TN = ((0,), (0,))


def split(v):
    hi = v.astype(BF)
    return hi, (v - hi.astype(F32)).astype(BF)


def iota(shape, dim):
    return lax.broadcasted_iota(I32, shape, dim)


def rcopy(src, dst, ssem, rsem, exp, rep):
    return pltpu.make_async_remote_copy(
        src_ref=src, dst_ref=dst, send_sem=ssem, recv_sem=rsem, device_id={"exp": exp, "rep": rep}, device_id_type=MESH
    )


class Place:
    def __init__(self):
        self.exp = lax.axis_index("exp")
        self.rep = lax.axis_index("rep")
        self.e = self.exp // SH
        self.half = self.e % 2
        self.x = self.e // 2
        self.m = self.exp % SH
        self.y = self.rep // 2
        self.c = self.rep % 2
        self.tile = self.tile_of(self.rep)
        self.d = 1 - 2 * self.c
        self.fwd = self.rep_at(self.d)
        self.bwd = self.rep_at(-self.d)
        self.partner = self.y * 2 + 1 - self.c

    def rep_at(self, dy):
        return ((self.y + dy + 4) % 4) * 2 + self.c

    def tile_of(self, rep):
        return (rep + 3 * self.e) % 8

    def greet(self):
        bar = pltpu.get_barrier_semaphore()

        def hello(exp, rep):
            pl.semaphore_signal(bar, inc=1, device_id={"exp": exp, "rep": rep}, device_id_type=MESH)

        for rep in (self.fwd, self.bwd, self.rep_at(2), self.partner):
            hello(self.exp, rep)

        def body(n, _):
            hello((self.exp + n) % (EXP * SH), self.rep)
            return 0

        lax.fori_loop(1, EXP * SH, body, 0)

    def enter(self):
        pl.semaphore_wait(pltpu.get_barrier_semaphore(), EXP * SH + 3)


class Gather:
    def __init__(self, pc, src, piece, ssem, rsem, valid=None):
        self.pc, self.src, self.piece, self.ssem, self.rsem = pc, src, piece, ssem, rsem
        self.valid = valid

    def guard(self, rep, fn):
        if self.valid is None:
            fn()
        else:
            pl.when(self.valid(rep))(fn)

    def copy(self, src, rep_of, k, target):
        return rcopy(src, self.piece(rep_of), self.ssem.at[k], self.rsem.at[rep_of], self.pc.exp, target)

    def moves(self):
        pc = self.pc
        far = pc.rep_at(2)
        own, part = pc.rep, pc.partner
        return [
            (self.src, own, 0, pc.fwd),
            (self.src, own, 1, pc.bwd),
            (self.src, own, 2, part),
            (self.src, own, 3, far),
            (self.piece(pc.bwd), pc.bwd, 4, part),
            (self.piece(pc.fwd), pc.fwd, 5, part),
            (self.piece(far), far, 6, part),
        ]

    def start(self):
        def go():
            mv = self.moves()
            for k in (3, 0, 1, 2):
                self.copy(*mv[k]).start()

        self.guard(self.pc.rep, go)

    def arrive(self, rep):
        self.copy(self.piece(rep), rep, 0, self.pc.partner).wait_recv()

    def relay(self):
        mv = self.moves()

        def near():
            self.arrive(self.pc.bwd)
            self.copy(*mv[4]).start()

        self.guard(self.pc.bwd, near)

        def other():
            self.arrive(self.pc.fwd)
            self.copy(*mv[5]).start()

        self.guard(self.pc.fwd, other)

    def relay_far(self):
        far = self.pc.rep_at(2)

        def go():
            self.arrive(far)
            self.copy(*self.moves()[6]).start()

        self.guard(far, go)

    def finish(self):
        for dy in range(4):
            rep = ((self.pc.y + dy) % 4) * 2 + 1 - self.pc.c
            self.guard(rep, lambda rep=rep: self.arrive(rep))
        for mv in self.moves():
            self.guard(mv[1], lambda mv=mv: self.copy(*mv).wait_send())


class Scatter:
    def __init__(self, pc, src, got, total, side, ssem, rsem):
        self.pc, self.src, self.got, self.total, self.side, self.ssem, self.rsem = pc, src, got, total, side, ssem, rsem

    def copy(self, k):
        pc = self.pc
        y, d = pc.y, pc.d
        at = lambda dy: self.total.at[(y + dy + 4) % 4]
        src, dst, rep = (
            (self.src.at[1 - pc.c], self.got, pc.partner),
            (at(2), self.side.at[0], pc.rep_at(2)),
            (at(-d), self.side.at[1], pc.bwd),
            (at(d), self.side.at[2], pc.fwd),
        )[k]
        return rcopy(src, dst, self.ssem.at[k], self.rsem.at[k], pc.exp, rep)

    def start(self):
        self.copy(0).start()

    def add(self):
        self.copy(0).wait_recv()

        def body(k, _):
            self.total[k] = (self.src[self.pc.c, k].astype(F32) + self.got[k].astype(F32)).astype(self.total.dtype)
            return 0

        lax.fori_loop(0, 4, body, 0)
        for k in (1, 2, 3):
            self.copy(k).start()

    def result(self):
        for k in (1, 2, 3):
            self.copy(k).wait_recv()
        return self.total[self.pc.y].astype(F32) + sum(self.side[k].astype(F32) for k in range(3))

    def finish(self):
        for k in range(4):
            self.copy(k).wait_send()


def scatter_scratch(block, dtype):
    return [
        pltpu.VMEM((4,) + block, dtype),
        pltpu.VMEM((4,) + block, dtype),
        pltpu.VMEM((3,) + block, dtype),
        pltpu.SemaphoreType.DMA((4,)),
        pltpu.SemaphoreType.DMA((4,)),
    ]


def gather_scratch():
    return [pltpu.SemaphoreType.DMA((7,)), pltpu.SemaphoreType.DMA((REP,))]


def layer_kernel(
    latent, s_ref, gain_ref, wr_ref, routes_ref, wg_ref, wu_ref, wd_ref, gm_ref,
    mixed_ref, glat_ref, ggate_ref, gup_ref, gdown_ref,
    send, send_side, recv, recv_side, wfull, gp, gmine, gfull,
    h_prev, h_next, lat4, ptx, stem_ref, sg_hi, sg_lo,
    row32, side32, gm_all, hg_ref, dpre_ref,
    part, acc_l, acc_r, sums, ret32, send_back, back_in, bsum, back_all, slots, dp, tp, tmine, tfull, a_out, a_prev, a_next,
    *sems
):
    (g_got, g_tot, g_side, g_ss, g_rs, d_got, d_tot, d_side, d_ss, d_rs, t_got, t_tot, t_side, t_ss, t_rs,
     ag_ss, ag_rs, wg_ss, wg_rs, tg_ss, tg_rs, bg_ss, bg_rs, s0_ss, s0_rs, s1_ss, s1_rs,
     st_ss, st_rs, sd_ss, sd_rs, ln_ss, ln_rs, ca_ss, cl_rs, cr_rs, ct_ss, ct_rs, bk_ss, bo_ss, bk_rs,
     ha_ss, ha_rs, hb_ss, hb_rs, loc) = sems
    pc = Place()
    m = pc.m
    tok, dm = gm_ref.shape
    hid = wg_ref.shape[1]
    taps = s_ref.shape[0]
    wide = tok // 2
    top = routes_ref.shape[0]
    has_rows = pc.tile < TILES

    pc.greet()

    upper = (iota((tok, tok), 0) < iota((tok, tok), 1)).astype(BF)
    r_row = [routes_ref[k : k + 1, :] for k in range(top)]
    sel_row = [(iota((EXP, tok), 0) == r).astype(F32) for r in r_row]
    before_row = dot32((sel_row[0] + sel_row[1]).astype(BF), upper)
    pos_row = [jnp.sum(s * before_row, axis=0, keepdims=True).astype(I32) for s in sel_row]

    def here_id(pos, r):
        q = pos - ROWS * pc.tile
        return jnp.where((q >= 0) & (q < ROWS), r * ROWS + q, -1)

    def full_id(pos, r):
        t = lax.shift_right_logical(pos, 3)
        place = (r & 1) * (EXP // 2) + lax.shift_right_logical(r, 1)
        return t * (EXP * ROWS) + place * ROWS + (pos - t * ROWS)

    hot_here = [(iota((EXP * ROWS, tok), 0) == here_id(p, r)).astype(F32) for p, r in zip(pos_row, r_row)]
    hot_here_b = [h.astype(BF) for h in hot_here]
    picked_rows = dot32(hot_here_b[0] + hot_here_b[1], gm_ref[...])
    for e in range(EXP):
        send[e] = picked_rows[e * ROWS : (e + 1) * ROWS].astype(BF)

    gain = gain_ref[...].reshape(1, dm)
    dsl = wg_ref.shape[0]
    sg = s_ref[...].astype(F32) * gain
    hi, lo = split(sg)
    pick = (iota((dm, dsl), 0) == iota((dm, dsl), 1) + pc.rep * dsl).astype(BF)
    s_hi = dot32(hi, pick).astype(BF)
    s_lo = dot32(lo, pick).astype(BF)
    sg_hi[...] = s_hi
    sg_lo[...] = s_lo
    zero_taps = jnp.zeros((TAPS - taps, 2 * hid), F32)
    share = jnp.concatenate(
        [dot32(s_hi, w[...]) + dot32(s_lo, w[...]) for w in (wg_ref, wu_ref)], axis=1
    )
    share = jnp.concatenate([share, zero_taps], axis=0)
    for k in range(REP):
        gp[k // 4, k % 4] = share[k * TP : (k + 1) * TP]
    rproj = dot32(hi, wr_ref[...], NT) + dot32(lo, wr_ref[...], NT)

    pc.enter()

    ha = (
        rcopy(latent.at[1], h_prev, ha_ss.at[0], ha_rs.at[0], pc.exp + 1, pc.rep),
        rcopy(latent.at[0], h_next, ha_ss.at[1], ha_rs.at[1], pc.exp - 1, pc.rep),
    )
    first_row, last_row = pc.exp == 0, pc.exp == EXP * SH - 1
    pl.when(jnp.logical_not(last_row))(lambda: ha[0].start())
    pl.when(jnp.logical_not(first_row))(lambda: ha[1].start())

    def stage(k):
        peer = (pc.e + k) % EXP
        return rcopy(send.at[peer], recv.at[m, pc.tile], st_ss.at[k], st_rs.at[pc.tile], peer * SH + m, pc.rep)

    keep_gm = pltpu.make_async_copy(send.at[pc.e], recv.at[m, pc.tile], loc.at[0])

    @pl.when(has_rows)
    def _():
        for k in (1, 7, 2, 6, 3, 5, 4):
            stage(k).start()
        keep_gm.start()

    gather_w = Gather(pc, wd_ref, lambda rep: wfull.at[rep], wg_ss, wg_rs)
    own_w = pltpu.make_async_copy(wd_ref, wfull.at[pc.rep], loc.at[2])
    gather_w.start()
    own_w.start()

    scatter_g = Scatter(pc, gp, g_got, g_tot, g_side, g_ss, g_rs)
    scatter_g.start()

    @pl.when(jnp.logical_not(first_row))
    def _():
        rcopy(latent.at[1], h_prev, ha_ss.at[0], ha_rs.at[0], pc.exp, pc.partner).wait_recv()
        lat4[0] = h_prev[...].astype(F32)

    @pl.when(first_row)
    def _():
        lat4[0] = jnp.zeros(lat4.shape[1:], F32)

    @pl.when(jnp.logical_not(last_row))
    def _():
        rcopy(latent.at[0], h_next, ha_ss.at[1], ha_rs.at[1], pc.exp, pc.partner).wait_recv()
        lat4[3] = h_next[...].astype(F32)

    @pl.when(last_row)
    def _():
        lat4[3] = jnp.zeros(lat4.shape[1:], F32)

    lat4[1] = latent[0].astype(F32)
    lat4[2] = latent[1].astype(F32)
    chan = lat4.shape[1]
    col = iota((chan, tok), 1)
    col = jnp.where(col >= wide, col - wide, col)

    def shifted(v, by):
        if by == 0:
            return v
        rolled = pltpu.roll(v, (-by) % tok, 1)
        return jnp.where(col == (0 if by < 0 else wide - 1), 0.0, rolled)

    for i in range(3):
        two = jnp.concatenate([lat4[i], lat4[i + 1]], axis=1)
        for j in range(3):
            ptx[pl.ds((3 * i + j) * chan, chan), :] = shifted(two, j - 1)
    ptx[pl.ds(taps, SIDE - taps), :] = jnp.zeros((SIDE - taps, tok), F32)
    pt = ptx[pl.ds(0, taps), :]
    stem = dot32(pt.astype(BF), s_ref[...], TN).astype(BF)
    stem_ref[...] = stem
    sv = stem.astype(F32)
    rstd = lax.rsqrt(jnp.mean(sv * sv, axis=-1, keepdims=True) + 1e-06)
    rstd_row = jnp.transpose(jnp.broadcast_to(rstd, (tok, tok)))[0:1, :]
    normed = (sv * rstd * gain).astype(BF)
    logits = dot32(wr_ref[...], normed, NT)
    picked = [jnp.sum(s * logits, axis=0, keepdims=True) for s in sel_row]
    chosen = [jax.nn.sigmoid(p) for p in picked]
    total = chosen[0] + chosen[1]
    gates = [c / total for c in chosen]
    r_hi, r_lo = split(rstd_row)
    ptx[pl.ds(TAPS, 1), :] = r_hi.astype(F32)
    ptx[pl.ds(TAPS + 1, 1), :] = r_lo.astype(F32)
    side = jnp.zeros((EXP * ROWS, SIDE), F32)
    for k in range(top):
        k_hi, k_lo = split(gates[k])
        ptx[pl.ds(TAPS + 2, 1), :] = k_hi.astype(F32)
        ptx[pl.ds(TAPS + 3, 1), :] = k_lo.astype(F32)
        side = side + dot32(hot_here_b[k], ptx[...].astype(BF), NT)
    for e in range(EXP):
        send_side[e] = side[e * ROWS : (e + 1) * ROWS].astype(BF)

    scatter_g.add()

    def to_all(n):
        dest = (pc.exp + n) % (EXP * SH)
        e = dest // SH
        return rcopy(send_side.at[e], recv_side.at[m, pc.tile], sd_ss.at[e], sd_rs.at[m], dest, pc.rep)

    @pl.when(has_rows)
    def _():
        def body(n, _):
            to_all(n).start()
            return 0

        lax.fori_loop(1, EXP * SH, body, 0)
        pltpu.make_async_copy(send_side.at[pc.e], recv_side.at[m, pc.tile], sd_rs.at[m]).start()

    ends = (m < SH - 1, m > 0)

    def hop(way, p, c, s):
        at = pl.ds(CHUNKS[c][0], CHUNKS[c][1])
        ref = recv.at[p, at]
        return rcopy(ref, ref, ln_ss.at[way, s], ln_rs.at[p, c], pc.exp + 1 - 2 * way, pc.rep)

    def arrived(i):
        source = (5 * (pc.rep - i + 8)) % 8

        @pl.when(source != pc.e)
        def _():
            rcopy(recv.at[m, i], recv.at[m, i], st_ss.at[0], st_rs.at[i], pc.exp, pc.partner).wait_recv()

    def widen(p):
        for i in range(TILES):
            row32[pl.ds(pl.multiple_of(p * PIECE + i * ROWS, ROWS), ROWS), :] = recv[p, i].astype(F32)

    def step(s, _):
        for c in range(len(CHUNKS)):
            for way, p in ((0, m - s), (1, m + s)):
                ok = (p >= 0) if way == 0 else (p < SH)

                @pl.when(ok)
                def _():
                    hop(way, p, c, s).wait_recv()

                    @pl.when(ends[way])
                    def _():
                        hop(way, p, c, s).start()

        for way, p in ((0, m - s), (1, m + s)):
            pl.when((p >= 0) if way == 0 else (p < SH))(lambda p=p: widen(p))
        return 0

    @pl.when(has_rows)
    def _():
        keep_gm.wait()

    for c, (at, count) in enumerate(CHUNKS):
        for i in range(at, at + count):
            arrived(i)
        for way in range(2):
            pl.when(ends[way])(lambda way=way, c=c: hop(way, m, c, 0).start())
    gmine[...] = scatter_g.result()
    spot = lambda ref: lambda rep: ref.at[(rep % 2) * 4 + rep // 2]
    gather_g = Gather(pc, gmine, spot(gfull), ag_ss, ag_rs)
    own_g = pltpu.make_async_copy(gmine, spot(gfull)(pc.rep), loc.at[3])
    gather_g.start()
    own_g.start()
    widen(m)
    gather_w.relay()
    lax.fori_loop(1, 2, step, 0)
    gather_w.relay_far()
    gather_g.relay()
    lax.fori_loop(2, 3, step, 0)
    gather_g.relay_far()
    lax.fori_loop(3, 4, step, 0)
    gather_g.finish()
    gather_w.finish()
    scatter_g.finish()
    own_w.wait()
    own_g.wait()

    def widen_side(p, _):
        pltpu.make_async_copy(recv_side.at[p], recv_side.at[p], sd_rs.at[p]).wait()
        for i in range(TILES):
            side32[pl.ds(pl.multiple_of(p * PIECE + i * ROWS, ROWS), ROWS), :] = recv_side[p, i].astype(F32)
        return 0

    lax.fori_loop(0, SH, widen_side, 0)
    more = side32[...]
    pr = more[:, :TAPS].astype(BF)
    rs = more[:, TAPS : TAPS + 1] + more[:, TAPS + 1 : TAPS + 2]
    gt = more[:, TAPS + 2 : TAPS + 3] + more[:, TAPS + 3 : TAPS + 4]
    g_hi, g_lo = split(gfull[...].reshape(TAPS, 2 * hid))
    pre = rs * (dot32(pr, g_hi) + dot32(pr, g_lo))
    pg, pu = pre[:, :hid], pre[:, hid:]
    sigma = jax.nn.sigmoid(pg)
    silu = pg * sigma
    hidden = silu * pu
    slope = pu * sigma * (1.0 + pg * (1.0 - sigma))
    hg = (gt * hidden).astype(BF)
    down_t = wfull[...].reshape(dm, hid)
    ret32[...] = dot32(hg, down_t, NT)
    hg_ref[...] = hg

    def give(way, p, c):
        at = pl.ds(CHUNKS[c][0], CHUNKS[c][1])
        dst, rsem = ((acc_l, cl_rs), (acc_r, cr_rs))[way]
        return rcopy(
            part.at[p, at], dst.at[p, at], ca_ss.at[p], rsem.at[p, c], pc.exp + 1 - 2 * way, pc.rep
        )

    def mine(p, i):
        return ret32[pl.ds(pl.multiple_of(p * PIECE + i * ROWS, ROWS), ROWS), :]

    def step_sum(tau, _):
        for c, (at, count) in enumerate(CHUNKS):
            for way, p in ((0, 7 - tau + m), (1, tau - 7 + m)):
                ok = (tau >= m) if way == 0 else (p >= 0)
                acc = (acc_l, acc_r)[way]

                @pl.when(ok & ends[1 - way])
                def _():
                    give(way, p, c).wait_recv()
                    for i in range(at, at + count):
                        part[p, i] = (mine(p, i) + acc[p, i].astype(F32)).astype(BF)

                @pl.when(ok & jnp.logical_not(ends[1 - way]))
                def _():
                    for i in range(at, at + count):
                        part[p, i] = mine(p, i).astype(BF)

                pl.when(ok & ends[way])(lambda: give(way, p, c).start())

        return 0

    def steps(at, to):
        lax.fori_loop(at, to, step_sum, 0)

    for n in range(4):
        steps(n, n + 1)
        lax.fori_loop(4 + n, 5 + n, step, 0)

    gm_all[...] = row32[...].astype(BF)
    u = dot32(gm_all[...], down_t)
    gg = jnp.sum(hidden * u, axis=-1, keepdims=True)
    gu = (rs * gt) * u
    dpre = jnp.concatenate([gu * slope, gu * silu], axis=1).astype(BF)
    dpre_ref[...] = dpre
    back = dot32(dpre, g_hi, NT) + dot32(dpre, g_lo, NT)
    gg_hi = gg.astype(BF).astype(F32)
    lane = iota((SH * PIECE, SIDE - TAPS), 1)
    tail = jnp.where(lane == 0, gg_hi, jnp.where(lane == 1, gg - gg_hi, 0.0))
    side32[...] = jnp.concatenate([back, tail], axis=1)
    place = pc.half * (EXP // 2) + pc.x

    def source_of(i):
        return (5 * (pc.rep - i + 8)) % 8

    def reply(p, i, sem):
        return rcopy(send_back.at[p, i], back_in.at[m, place], sem, bk_rs.at[0], source_of(i) * SH + p, pc.rep)

    def narrow(n, _):
        p = (m + n) % SH
        for i in range(TILES):
            send_back[p, i] = side32[pl.ds(pl.multiple_of(p * PIECE + i * ROWS, ROWS), ROWS), :].astype(BF)
        for i in range(TILES):
            pl.when(p != m)(lambda i=i: reply(p, i, bk_ss.at[p]).start())

            @pl.when((p == m) & (source_of(i) != pc.e))
            def _():
                reply(p, i, bo_ss.at[i]).start()

            @pl.when((p == m) & (source_of(i) == pc.e))
            def _():
                pltpu.make_async_copy(send_back.at[p, i], back_in.at[m, place], bk_rs.at[0]).start()

        return 0

    lax.fori_loop(0, SH, narrow, 0)
    steps(4, 5)
    t_share = dot32(pr, dpre_ref[...], TN)
    for k in range(REP):
        tp[k // 4, k % 4] = t_share[k * TP : (k + 1) * TP]
    scatter_t = Scatter(pc, tp, t_got, t_tot, t_side, t_ss, t_rs)
    scatter_t.start()
    d_share = dot32(gm_all[...], hg_ref[...], TN)
    for k in range(REP):
        dp[k % 2, k // 2] = d_share[k * dsl : (k + 1) * dsl].astype(BF)
    scatter_d = Scatter(pc, dp, d_got, d_tot, d_side, d_ss, d_rs)
    scatter_d.start()
    steps(5, 6)
    scatter_t.add()
    scatter_d.add()
    steps(6, 7)
    gather_t = Gather(pc, tmine, spot(tfull), tg_ss, tg_rs)
    own_t = pltpu.make_async_copy(tmine, spot(tfull)(pc.rep), loc.at[4])
    with_rows = lambda rep: pc.tile_of(rep) < TILES
    tile_at = lambda rep: pc.tile_of(rep) % TILES
    gather_b = Gather(pc, bsum, lambda rep: back_all.at[tile_at(rep)], bg_ss, bg_rs, with_rows)
    own_b = pltpu.make_async_copy(bsum, back_all.at[pc.tile % TILES], loc.at[1])

    def home(i):
        source = source_of(i)
        return source, rcopy(
            sums.at[i], slots.at[pc.half, i, pc.x], ct_ss.at[i], ct_rs.at[pc.half], source * SH + m, pc.rep
        )

    keep_out = lambda i: pltpu.make_async_copy(sums.at[i], slots.at[pc.half, i, pc.x], ct_rs.at[pc.half])
    for c, (at, count) in enumerate(CHUNKS):
        for way in range(2):
            pl.when(ends[1 - way])(lambda way=way, c=c: give(way, m, c).wait_recv())
        for i in range(at, at + count):
            @pl.when(m == 0)
            def _():
                sums[i] = (mine(m, i) + acc_r[m, i].astype(F32)).astype(BF)

            @pl.when(m == SH - 1)
            def _():
                sums[i] = (mine(m, i) + acc_l[m, i].astype(F32)).astype(BF)

            @pl.when(ends[0] & ends[1])
            def _():
                sums[i] = (mine(m, i) + acc_l[m, i].astype(F32) + acc_r[m, i].astype(F32)).astype(BF)

            source, copy = home(i)
            pl.when(source != pc.e)(lambda copy=copy: copy.start())
            pl.when(source == pc.e)(lambda i=i: keep_out(i).start())

    def out_gather(h, ss, rs):
        half = (pc.half + h) % 2
        ready = slots.at[half, pc.tile % TILES]
        gather = Gather(pc, ready, lambda rep: slots.at[half, tile_at(rep)], ss, rs, with_rows)
        wait = pltpu.make_async_copy(ready, ready, ct_rs.at[half])
        return half, gather, wait

    near_half, near, near_wait = out_gather(0, s0_ss, s0_rs)
    away_half, away, away_wait = out_gather(1, s1_ss, s1_rs)

    @pl.when(has_rows)
    def _():
        pltpu.make_async_copy(back_in, back_in, bk_rs.at[0]).wait()
        for k in range(EXP):
            bsum[k] = sum(back_in[j, k].astype(F32) for j in range(SH)).astype(BF)
        own_b.start()

    gather_b.start()
    tmine[...] = scatter_t.result()
    gather_t.start()
    own_t.start()
    pl.when(has_rows)(near_wait.wait)
    near.start()
    gather_b.relay()
    gather_t.relay()
    gather_b.relay_far()
    near.relay()
    gather_t.relay_far()
    near.relay_far()
    pl.when(has_rows)(away_wait.wait)
    away.start()
    gdown_ref[...] = scatter_d.result()
    pl.when(has_rows)(own_b.wait)
    gather_b.finish()

    for t in range(TILES):
        for k in range(EXP):
            side32[pl.ds((t * EXP + k) * ROWS, ROWS), :] = back_all[t, k].astype(F32)
    count = TILES * EXP * ROWS
    full_row = [full_id(p, r) for p, r in zip(pos_row, r_row)]
    hot_row = [(iota((count, tok), 0) == f).astype(F32) for f in full_row]
    tail = side32[...]
    gg_slot = tail[:, TAPS : TAPS + 1] + tail[:, TAPS + 1 : TAPS + 2]
    gg_row = [jnp.sum(h * gg_slot, axis=0, keepdims=True) for h in hot_row]
    b = dot32(tail.astype(BF), (hot_row[0] + hot_row[1]).astype(BF), TN)[:taps]
    mean = gg_row[0] * gates[0] + gg_row[1] * gates[1]
    grad_picked = [(g - mean) / total * (c * (1.0 - c)) for g, c in zip(gg_row, chosen)]
    grad_logits = sel_row[0] * grad_picked[0] + sel_row[1] * grad_picked[1]
    b = b + rstd_row * jnp.dot(rproj, grad_logits, precision=lax.Precision.HIGHEST, preferred_element_type=F32)
    c_row = jnp.sum(pt * b, axis=0, keepdims=True) * (rstd_row * rstd_row * (1.0 / dm))
    proj0 = dot32(s_ref[...], gm_ref[...], NT)
    proj1 = dot32(s_ref[...], stem_ref[...], NT)
    proj = proj0 + b - c_row * proj1
    rows3 = []
    for i in range(3):
        rows3.append(
            sum(shifted(proj[(3 * i + j) * chan : (3 * i + j + 1) * chan], 1 - j) for j in range(3))
        )
    a_out[0] = rows3[0][:, :wide]
    a_out[1] = rows3[2][:, wide:]
    hb = (
        rcopy(a_out.at[0], a_next, hb_ss.at[0], hb_rs.at[0], pc.exp - 1, pc.rep),
        rcopy(a_out.at[1], a_prev, hb_ss.at[1], hb_rs.at[1], pc.exp + 1, pc.rep),
    )
    pl.when(jnp.logical_not(first_row))(lambda: hb[0].start())
    pl.when(jnp.logical_not(last_row))(lambda: hb[1].start())
    glat_ref[0] = rows3[0][:, wide:] + rows3[1][:, :wide]
    glat_ref[1] = rows3[1][:, wide:] + rows3[2][:, :wide]

    @pl.when(jnp.logical_not(last_row))
    def _():
        rcopy(a_out.at[0], a_next, hb_ss.at[0], hb_rs.at[0], pc.exp, pc.partner).wait_recv()
        glat_ref[1] = glat_ref[1] + a_next[...]

    @pl.when(jnp.logical_not(first_row))
    def _():
        rcopy(a_out.at[1], a_prev, hb_ss.at[1], hb_rs.at[1], pc.exp, pc.partner).wait_recv()
        glat_ref[0] = glat_ref[0] + a_prev[...]

    away.relay()
    away.relay_far()
    gather_t.finish()
    own_t.wait()
    t_hi, t_lo = split(tfull[...].reshape(TAPS, 2 * hid)[:taps])
    gw = dot32(sg_hi[...], t_hi, TN) + dot32(sg_hi[...], t_lo, TN) + dot32(sg_lo[...], t_hi, TN)
    ggate_ref[...] = gw[:, :hid]
    gup_ref[...] = gw[:, hid:]
    square = [jnp.transpose(jnp.broadcast_to(f.astype(F32), (tok, tok)))[:, :1].astype(I32) for f in full_row]
    span = count // 2

    def out_of(half, gather):
        hot = jnp.zeros((tok, span), F32)
        for f in square:
            t = lax.shift_right_logical(f, 6)
            own = (lax.shift_right_logical(f, 5) & 1) == half
            at = jnp.where(own, t * (EXP // 2 * ROWS) + (f & 31), -1)
            hot = hot + (iota((tok, span), 1) == at).astype(F32)
        gather.finish()
        for t in range(TILES):
            for x in range(EXP // 2):
                ret32[pl.ds((t * (EXP // 2) + x) * ROWS, ROWS), :] = slots[half, t, x].astype(F32)
        return dot32(hot.astype(BF), ret32[pl.ds(0, span), :].astype(BF))

    sv_out = stem_ref[...].astype(F32) + out_of(near_half, near)

    for copy in (ha[1], hb[0]):
        pl.when(jnp.logical_not(first_row))(copy.wait_send)
    for copy in (ha[0], hb[1]):
        pl.when(jnp.logical_not(last_row))(copy.wait_send)
    scatter_t.finish()
    scatter_d.finish()

    @pl.when(has_rows)
    def _():
        for k in range(1, EXP):
            stage(k).wait_send()

        def body(k, _):
            rcopy(send_side, send_side, sd_ss.at[(pc.e + k) % EXP], sd_rs.at[0], pc.exp, pc.partner).wait_send()
            return 0

        lax.fori_loop(1, EXP, body, 0)
        seven = send_side.at[pl.ds(0, EXP - 1)]
        rcopy(seven, seven, sd_ss.at[pc.e], sd_rs.at[0], pc.exp, pc.partner).wait_send()

    def drain(s, _):
        for way, p in ((0, m - s), (1, m + s)):

            @pl.when(((p >= 0) if way == 0 else (p < SH)) & ends[way])
            def _():
                rcopy(recv.at[p], recv.at[p], ln_ss.at[way, s], ln_rs.at[p, 0], pc.exp, pc.partner).wait_send()

        for way, ok in ((0, s > m), (1, s < m)):

            @pl.when(ok & ends[way])
            def _():
                rcopy(part.at[s], acc_l.at[s], ca_ss.at[s], cl_rs.at[s, 0], pc.exp, pc.partner).wait_send()

        @pl.when(s != m)
        def _():
            rcopy(send_back.at[s], send_back.at[s], bk_ss.at[s], bk_rs.at[0], pc.exp, pc.partner).wait_send()

        return 0

    lax.fori_loop(0, SH, drain, 0)
    for i in range(TILES):

        @pl.when(source_of(i) != pc.e)
        def _():
            home(i)[1].wait_send()
            reply(m, i, bo_ss.at[i]).wait_send()

    mixed_ref[...] = (sv_out + out_of(away_half, away)).astype(BF)


def local(latent, stem_weight, norm_gain, router_weight, routes, gate_weight, up_weight, down_weight, grad_mixed):
    tok, dm = grad_mixed.shape
    dsl, hid = gate_weight.shape
    rows_here, chan, wide = latent.shape
    taps = stem_weight.shape[0]
    dma = pltpu.SemaphoreType.DMA
    chunks = len(CHUNKS)
    v = pltpu.VMEM
    outs = pl.pallas_call(
        layer_kernel,
        out_shape=(
            jax.ShapeDtypeStruct((tok, dm), BF),
            jax.ShapeDtypeStruct((rows_here, chan, wide), F32),
            jax.ShapeDtypeStruct((dsl, hid), F32),
            jax.ShapeDtypeStruct((dsl, hid), F32),
            jax.ShapeDtypeStruct((dsl, hid), F32),
        ),
        in_specs=[VM] * 9,
        out_specs=(VM,) * 5,
        scratch_shapes=[
            v((EXP, ROWS, dm), BF),
            v((EXP, ROWS, SIDE), BF),
            v((SH, TILES, ROWS, dm), BF),
            v((SH, TILES, ROWS, SIDE), BF),
            v((REP, dsl, hid), BF),
            v((2, 4, TP, 2 * hid), F32),
            v((TP, 2 * hid), F32),
            v((REP, TP, 2 * hid), F32),
            v((chan, wide), BF),
            v((chan, wide), BF),
            v((4, chan, wide), F32),
            v((SIDE, tok), F32),
            v((tok, dm), BF),
            v((taps, dsl), BF),
            v((taps, dsl), BF),
            v((SH * PIECE, dm), F32),
            v((SH * PIECE, SIDE), F32),
            v((SH * PIECE, dm), BF),
            v((SH * PIECE, hid), BF),
            v((SH * PIECE, 2 * hid), BF),
            v((SH, TILES, ROWS, dm), BF),
            v((SH, TILES, ROWS, dm), BF),
            v((SH, TILES, ROWS, dm), BF),
            v((TILES, ROWS, dm), BF),
            v((SH * PIECE, dm), F32),
            v((SH, TILES, ROWS, SIDE), BF),
            v((SH, EXP, ROWS, SIDE), BF),
            v((EXP, ROWS, SIDE), BF),
            v((TILES, EXP, ROWS, SIDE), BF),
            v((2, TILES, EXP // 2, ROWS, dm), BF),
            v((2, 4, dsl, hid), BF),
            v((2, 4, TP, 2 * hid), F32),
            v((TP, 2 * hid), F32),
            v((REP, TP, 2 * hid), F32),
            v((2, chan, wide), F32),
            v((chan, wide), F32),
            v((chan, wide), F32),
        ]
        + scatter_scratch((TP, 2 * hid), F32)
        + scatter_scratch((dsl, hid), BF)
        + scatter_scratch((TP, 2 * hid), F32)
        + gather_scratch() * 6
        + [
            dma((EXP,)),
            dma((TILES,)),
            dma((EXP,)),
            dma((SH,)),
            dma((2, SH)),
            dma((SH, chunks)),
            dma((SH,)),
            dma((SH, chunks)),
            dma((SH, chunks)),
            dma((TILES,)),
            dma((2,)),
            dma((SH,)),
            dma((TILES,)),
            dma((1,)),
            dma((2,)),
            dma((2,)),
            dma((2,)),
            dma((2,)),
            dma((6,)),
        ],
        compiler_params=pltpu.CompilerParams(collective_id=0, has_side_effects=True),
        name="layer",
    )(
        latent, stem_weight, norm_gain, router_weight.T, routes.T,
        gate_weight, up_weight, down_weight.T, grad_mixed,
    )
    return outs[:4] + (outs[4].T,)


def solution(mesh):
    return jax.shard_map(
        local,
        mesh=mesh,
        in_specs=(
            P("exp", None, None),
            P(),
            P(),
            P(),
            P("exp", None),
            P("rep", "exp"),
            P("rep", "exp"),
            P("exp", "rep"),
            P("exp", None),
        ),
        out_specs=(P("exp", None), P("exp", None, None), P("rep", "exp"), P("rep", "exp"), P("exp", "rep")),
        check_vma=False,
    )
```

```python
import jax
import jax.numpy as jnp
from jax import lax
from jax.experimental import pallas as pl
from jax.experimental.pallas import tpu as pltpu
from jax.sharding import PartitionSpec as P

F32 = jnp.float32
BF = jnp.bfloat16
I32 = jnp.int32
EXP = 8
SH = 8
REP = 8
TILES = 5
ROWS = 8
PIECE = TILES * ROWS
CHUNKS = ((0, 2), (2, 2), (4, 1))
TAPS = 192
TP = TAPS // REP
SIDE = 256
MESH = pl.DeviceIdType.MESH
VM = pl.BlockSpec(memory_space=pltpu.VMEM)


def dot32(a, b, dims=None):
    if dims is None:
        return jnp.dot(a, b, preferred_element_type=F32)
    return lax.dot_general(a, b, (dims, ((), ())), preferred_element_type=F32)


NT = ((1,), (1,))
TN = ((0,), (0,))


def split(v):
    hi = v.astype(BF)
    return hi, (v - hi.astype(F32)).astype(BF)


def iota(shape, dim):
    return lax.broadcasted_iota(I32, shape, dim)


def rcopy(src, dst, ssem, rsem, exp, rep):
    return pltpu.make_async_remote_copy(
        src_ref=src, dst_ref=dst, send_sem=ssem, recv_sem=rsem, device_id={"exp": exp, "rep": rep}, device_id_type=MESH
    )


class Place:
    def __init__(self):
        self.exp = lax.axis_index("exp")
        self.rep = lax.axis_index("rep")
        self.e = self.exp // SH
        self.half = self.e % 2
        self.x = self.e // 2
        self.m = self.exp % SH
        self.y = self.rep // 2
        self.c = self.rep % 2
        self.tile = self.tile_of(self.rep)
        self.d = 1 - 2 * self.c
        self.fwd = self.rep_at(self.d)
        self.bwd = self.rep_at(-self.d)
        self.partner = self.y * 2 + 1 - self.c

    def rep_at(self, dy):
        return ((self.y + dy + 4) % 4) * 2 + self.c

    def tile_of(self, rep):
        return (rep + 3 * self.e) % 8

    def greet(self):
        bar = pltpu.get_barrier_semaphore()

        def hello(exp, rep):
            pl.semaphore_signal(bar, inc=1, device_id={"exp": exp, "rep": rep}, device_id_type=MESH)

        for rep in (self.fwd, self.bwd, self.rep_at(2), self.partner):
            hello(self.exp, rep)

        def body(n, _):
            hello((self.exp + n) % (EXP * SH), self.rep)
            return 0

        lax.fori_loop(1, EXP * SH, body, 0)

    def enter(self):
        pl.semaphore_wait(pltpu.get_barrier_semaphore(), EXP * SH + 3)


class Gather:
    def __init__(self, pc, src, piece, ssem, rsem, valid=None):
        self.pc, self.src, self.piece, self.ssem, self.rsem = pc, src, piece, ssem, rsem
        self.valid = valid

    def guard(self, rep, fn):
        if self.valid is None:
            fn()
        else:
            pl.when(self.valid(rep))(fn)

    def copy(self, src, rep_of, k, target):
        return rcopy(src, self.piece(rep_of), self.ssem.at[k], self.rsem.at[rep_of], self.pc.exp, target)

    def moves(self):
        pc = self.pc
        far = pc.rep_at(2)
        own, part = pc.rep, pc.partner
        return [
            (self.src, own, 0, pc.fwd),
            (self.src, own, 1, pc.bwd),
            (self.src, own, 2, part),
            (self.src, own, 3, far),
            (self.piece(pc.bwd), pc.bwd, 4, part),
            (self.piece(pc.fwd), pc.fwd, 5, part),
            (self.piece(far), far, 6, part),
        ]

    def start(self):
        def go():
            mv = self.moves()
            for k in (3, 0, 1, 2):
                self.copy(*mv[k]).start()

        self.guard(self.pc.rep, go)

    def arrive(self, rep):
        self.copy(self.piece(rep), rep, 0, self.pc.partner).wait_recv()

    def relay(self):
        mv = self.moves()

        def near():
            self.arrive(self.pc.bwd)
            self.copy(*mv[4]).start()

        self.guard(self.pc.bwd, near)

        def other():
            self.arrive(self.pc.fwd)
            self.copy(*mv[5]).start()

        self.guard(self.pc.fwd, other)

    def relay_far(self):
        far = self.pc.rep_at(2)

        def go():
            self.arrive(far)
            self.copy(*self.moves()[6]).start()

        self.guard(far, go)

    def finish(self):
        for dy in range(4):
            rep = ((self.pc.y + dy) % 4) * 2 + 1 - self.pc.c
            self.guard(rep, lambda rep=rep: self.arrive(rep))
        for mv in self.moves():
            self.guard(mv[1], lambda mv=mv: self.copy(*mv).wait_send())


class Scatter:
    def __init__(self, pc, src, got, total, side, ssem, rsem):
        self.pc, self.src, self.got, self.total, self.side, self.ssem, self.rsem = pc, src, got, total, side, ssem, rsem

    def copy(self, k):
        pc = self.pc
        y, d = pc.y, pc.d
        at = lambda dy: self.total.at[(y + dy + 4) % 4]
        src, dst, rep = (
            (self.src.at[1 - pc.c], self.got, pc.partner),
            (at(2), self.side.at[0], pc.rep_at(2)),
            (at(-d), self.side.at[1], pc.bwd),
            (at(d), self.side.at[2], pc.fwd),
        )[k]
        return rcopy(src, dst, self.ssem.at[k], self.rsem.at[k], pc.exp, rep)

    def start(self):
        self.copy(0).start()

    def add(self):
        self.copy(0).wait_recv()

        def body(k, _):
            self.total[k] = (self.src[self.pc.c, k].astype(F32) + self.got[k].astype(F32)).astype(self.total.dtype)
            return 0

        lax.fori_loop(0, 4, body, 0)
        for k in (1, 2, 3):
            self.copy(k).start()

    def result(self):
        for k in (1, 2, 3):
            self.copy(k).wait_recv()
        return self.total[self.pc.y].astype(F32) + sum(self.side[k].astype(F32) for k in range(3))

    def finish(self):
        for k in range(4):
            self.copy(k).wait_send()


def scatter_scratch(block, dtype):
    return [
        pltpu.VMEM((4,) + block, dtype),
        pltpu.VMEM((4,) + block, dtype),
        pltpu.VMEM((3,) + block, dtype),
        pltpu.SemaphoreType.DMA((4,)),
        pltpu.SemaphoreType.DMA((4,)),
    ]


def gather_scratch():
    return [pltpu.SemaphoreType.DMA((7,)), pltpu.SemaphoreType.DMA((REP,))]


def layer_kernel(
    latent, s_ref, gain_ref, wr_ref, routes_ref, wg_ref, wu_ref, wd_ref, gm_ref,
    mixed_ref, glat_ref, ggate_ref, gup_ref, gdown_ref,
    send, send_side, recv, recv_side, wfull, gp, gmine, gfull,
    h_prev, h_next, lat4, ptx, stem_ref, sg_hi, sg_lo,
    row32, side32, gm_all, hg_ref, dpre_ref,
    part, acc_l, acc_r, sums, ret32, send_back, back_in, bsum, back_all, slots, dp, tp, tmine, tfull, a_out, a_prev, a_next,
    *sems
):
    (g_got, g_tot, g_side, g_ss, g_rs, d_got, d_tot, d_side, d_ss, d_rs, t_got, t_tot, t_side, t_ss, t_rs,
     ag_ss, ag_rs, wg_ss, wg_rs, tg_ss, tg_rs, bg_ss, bg_rs, s0_ss, s0_rs, s1_ss, s1_rs,
     st_ss, st_rs, sd_ss, sd_rs, ln_ss, ln_rs, ca_ss, cl_rs, cr_rs, ct_ss, ct_rs, bk_ss, bo_ss, bk_rs,
     ha_ss, ha_rs, hb_ss, hb_rs, loc) = sems
    pc = Place()
    m = pc.m
    tok, dm = gm_ref.shape
    hid = wg_ref.shape[1]
    taps = s_ref.shape[0]
    wide = tok // 2
    top = routes_ref.shape[0]
    has_rows = pc.tile < TILES

    pc.greet()

    upper = (iota((tok, tok), 0) < iota((tok, tok), 1)).astype(BF)
    r_row = [routes_ref[k : k + 1, :] for k in range(top)]
    sel_row = [(iota((EXP, tok), 0) == r).astype(F32) for r in r_row]
    before_row = dot32((sel_row[0] + sel_row[1]).astype(BF), upper)
    pos_row = [jnp.sum(s * before_row, axis=0, keepdims=True).astype(I32) for s in sel_row]

    def here_id(pos, r):
        q = pos - ROWS * pc.tile
        return jnp.where((q >= 0) & (q < ROWS), r * ROWS + q, -1)

    def full_id(pos, r):
        t = lax.shift_right_logical(pos, 3)
        place = (r & 1) * (EXP // 2) + lax.shift_right_logical(r, 1)
        return t * (EXP * ROWS) + place * ROWS + (pos - t * ROWS)

    hot_here = [(iota((EXP * ROWS, tok), 0) == here_id(p, r)).astype(F32) for p, r in zip(pos_row, r_row)]
    hot_here_b = [h.astype(BF) for h in hot_here]
    picked_rows = dot32(hot_here_b[0] + hot_here_b[1], gm_ref[...])
    for e in range(EXP):
        send[e] = picked_rows[e * ROWS : (e + 1) * ROWS].astype(BF)

    gain = gain_ref[...].reshape(1, dm)
    dsl = wg_ref.shape[0]
    sg = s_ref[...].astype(F32) * gain
    hi, lo = split(sg)
    pick = (iota((dm, dsl), 0) == iota((dm, dsl), 1) + pc.rep * dsl).astype(BF)
    s_hi = dot32(hi, pick).astype(BF)
    s_lo = dot32(lo, pick).astype(BF)
    sg_hi[...] = s_hi
    sg_lo[...] = s_lo
    zero_taps = jnp.zeros((TAPS - taps, 2 * hid), F32)
    share = jnp.concatenate(
        [dot32(s_hi, w[...]) + dot32(s_lo, w[...]) for w in (wg_ref, wu_ref)], axis=1
    )
    share = jnp.concatenate([share, zero_taps], axis=0)
    for k in range(REP):
        gp[k // 4, k % 4] = share[k * TP : (k + 1) * TP]
    rproj = dot32(hi, wr_ref[...], NT) + dot32(lo, wr_ref[...], NT)

    pc.enter()

    ha = (
        rcopy(latent.at[1], h_prev, ha_ss.at[0], ha_rs.at[0], pc.exp + 1, pc.rep),
        rcopy(latent.at[0], h_next, ha_ss.at[1], ha_rs.at[1], pc.exp - 1, pc.rep),
    )
    first_row, last_row = pc.exp == 0, pc.exp == EXP * SH - 1
    pl.when(jnp.logical_not(last_row))(lambda: ha[0].start())
    pl.when(jnp.logical_not(first_row))(lambda: ha[1].start())

    def stage(k):
        peer = (pc.e + k) % EXP
        return rcopy(send.at[peer], recv.at[m, pc.tile], st_ss.at[k], st_rs.at[pc.tile], peer * SH + m, pc.rep)

    keep_gm = pltpu.make_async_copy(send.at[pc.e], recv.at[m, pc.tile], loc.at[0])

    @pl.when(has_rows)
    def _():
        for k in (1, 7, 2, 6, 3, 5, 4):
            stage(k).start()
        keep_gm.start()

    gather_w = Gather(pc, wd_ref, lambda rep: wfull.at[rep], wg_ss, wg_rs)
    own_w = pltpu.make_async_copy(wd_ref, wfull.at[pc.rep], loc.at[2])
    gather_w.start()
    own_w.start()

    scatter_g = Scatter(pc, gp, g_got, g_tot, g_side, g_ss, g_rs)
    scatter_g.start()

    @pl.when(jnp.logical_not(first_row))
    def _():
        rcopy(latent.at[1], h_prev, ha_ss.at[0], ha_rs.at[0], pc.exp, pc.partner).wait_recv()
        lat4[0] = h_prev[...].astype(F32)

    @pl.when(first_row)
    def _():
        lat4[0] = jnp.zeros(lat4.shape[1:], F32)

    @pl.when(jnp.logical_not(last_row))
    def _():
        rcopy(latent.at[0], h_next, ha_ss.at[1], ha_rs.at[1], pc.exp, pc.partner).wait_recv()
        lat4[3] = h_next[...].astype(F32)

    @pl.when(last_row)
    def _():
        lat4[3] = jnp.zeros(lat4.shape[1:], F32)

    lat4[1] = latent[0].astype(F32)
    lat4[2] = latent[1].astype(F32)
    chan = lat4.shape[1]
    col = iota((chan, tok), 1)
    col = jnp.where(col >= wide, col - wide, col)

    def shifted(v, by):
        if by == 0:
            return v
        rolled = pltpu.roll(v, (-by) % tok, 1)
        return jnp.where(col == (0 if by < 0 else wide - 1), 0.0, rolled)

    for i in range(3):
        two = jnp.concatenate([lat4[i], lat4[i + 1]], axis=1)
        for j in range(3):
            ptx[pl.ds((3 * i + j) * chan, chan), :] = shifted(two, j - 1)
    ptx[pl.ds(taps, SIDE - taps), :] = jnp.zeros((SIDE - taps, tok), F32)
    pt = ptx[pl.ds(0, taps), :]
    stem = dot32(pt.astype(BF), s_ref[...], TN).astype(BF)
    stem_ref[...] = stem
    sv = stem.astype(F32)
    rstd = lax.rsqrt(jnp.mean(sv * sv, axis=-1, keepdims=True) + 1e-06)
    rstd_row = jnp.transpose(jnp.broadcast_to(rstd, (tok, tok)))[0:1, :]
    normed = (sv * rstd * gain).astype(BF)
    logits = dot32(wr_ref[...], normed, NT)
    picked = [jnp.sum(s * logits, axis=0, keepdims=True) for s in sel_row]
    chosen = [jax.nn.sigmoid(p) for p in picked]
    total = chosen[0] + chosen[1]
    gates = [c / total for c in chosen]
    r_hi, r_lo = split(rstd_row)
    ptx[pl.ds(TAPS, 1), :] = r_hi.astype(F32)
    ptx[pl.ds(TAPS + 1, 1), :] = r_lo.astype(F32)
    side = jnp.zeros((EXP * ROWS, SIDE), F32)
    for k in range(top):
        k_hi, k_lo = split(gates[k])
        ptx[pl.ds(TAPS + 2, 1), :] = k_hi.astype(F32)
        ptx[pl.ds(TAPS + 3, 1), :] = k_lo.astype(F32)
        side = side + dot32(hot_here_b[k], ptx[...].astype(BF), NT)
    for e in range(EXP):
        send_side[e] = side[e * ROWS : (e + 1) * ROWS].astype(BF)

    scatter_g.add()

    def to_all(n):
        dest = (pc.exp + n) % (EXP * SH)
        e = dest // SH
        return rcopy(send_side.at[e], recv_side.at[m, pc.tile], sd_ss.at[e], sd_rs.at[m], dest, pc.rep)

    @pl.when(has_rows)
    def _():
        def body(n, _):
            to_all(n).start()
            return 0

        lax.fori_loop(1, EXP * SH, body, 0)
        pltpu.make_async_copy(send_side.at[pc.e], recv_side.at[m, pc.tile], sd_rs.at[m]).start()

    ends = (m < SH - 1, m > 0)

    def hop(way, p, c, s):
        at = pl.ds(CHUNKS[c][0], CHUNKS[c][1])
        ref = recv.at[p, at]
        return rcopy(ref, ref, ln_ss.at[way, s], ln_rs.at[p, c], pc.exp + 1 - 2 * way, pc.rep)

    def arrived(i):
        source = (5 * (pc.rep - i + 8)) % 8

        @pl.when(source != pc.e)
        def _():
            rcopy(recv.at[m, i], recv.at[m, i], st_ss.at[0], st_rs.at[i], pc.exp, pc.partner).wait_recv()

    def widen(p):
        for i in range(TILES):
            row32[pl.ds(pl.multiple_of(p * PIECE + i * ROWS, ROWS), ROWS), :] = recv[p, i].astype(F32)

    def step(s, _):
        for c in range(len(CHUNKS)):
            for way, p in ((0, m - s), (1, m + s)):
                ok = (p >= 0) if way == 0 else (p < SH)

                @pl.when(ok)
                def _():
                    hop(way, p, c, s).wait_recv()

                    @pl.when(ends[way])
                    def _():
                        hop(way, p, c, s).start()

        for way, p in ((0, m - s), (1, m + s)):
            pl.when((p >= 0) if way == 0 else (p < SH))(lambda p=p: widen(p))
        return 0

    @pl.when(has_rows)
    def _():
        keep_gm.wait()

    for c, (at, count) in enumerate(CHUNKS):
        for i in range(at, at + count):
            arrived(i)
        for way in range(2):
            pl.when(ends[way])(lambda way=way, c=c: hop(way, m, c, 0).start())
    gmine[...] = scatter_g.result()
    spot = lambda ref: lambda rep: ref.at[(rep % 2) * 4 + rep // 2]
    gather_g = Gather(pc, gmine, spot(gfull), ag_ss, ag_rs)
    own_g = pltpu.make_async_copy(gmine, spot(gfull)(pc.rep), loc.at[3])
    gather_g.start()
    own_g.start()
    widen(m)
    gather_w.relay()
    lax.fori_loop(1, 2, step, 0)
    gather_w.relay_far()
    gather_g.relay()
    gather_g.relay_far()
    lax.fori_loop(2, 3, step, 0)
    gather_g.finish()
    gather_w.finish()
    scatter_g.finish()
    own_w.wait()
    own_g.wait()

    def widen_side(p, _):
        pltpu.make_async_copy(recv_side.at[p], recv_side.at[p], sd_rs.at[p]).wait()
        for i in range(TILES):
            side32[pl.ds(pl.multiple_of(p * PIECE + i * ROWS, ROWS), ROWS), :] = recv_side[p, i].astype(F32)
        return 0

    lax.fori_loop(0, SH, widen_side, 0)
    more = side32[...]
    pr = more[:, :TAPS].astype(BF)
    rs = more[:, TAPS : TAPS + 1] + more[:, TAPS + 1 : TAPS + 2]
    gt = more[:, TAPS + 2 : TAPS + 3] + more[:, TAPS + 3 : TAPS + 4]
    g_hi, g_lo = split(gfull[...].reshape(TAPS, 2 * hid))
    pre = rs * (dot32(pr, g_hi) + dot32(pr, g_lo))
    pg, pu = pre[:, :hid], pre[:, hid:]
    sigma = jax.nn.sigmoid(pg)
    silu = pg * sigma
    hidden = silu * pu
    slope = pu * sigma * (1.0 + pg * (1.0 - sigma))
    hg = (gt * hidden).astype(BF)
    down_t = wfull[...].reshape(dm, hid)
    ret32[...] = dot32(hg, down_t, NT)
    hg_ref[...] = hg

    def give(way, p, c):
        at = pl.ds(CHUNKS[c][0], CHUNKS[c][1])
        dst, rsem = ((acc_l, cl_rs), (acc_r, cr_rs))[way]
        return rcopy(
            part.at[p, at], dst.at[p, at], ca_ss.at[p], rsem.at[p, c], pc.exp + 1 - 2 * way, pc.rep
        )

    def mine(p, i):
        return ret32[pl.ds(pl.multiple_of(p * PIECE + i * ROWS, ROWS), ROWS), :]

    def step_sum(tau, _):
        for c, (at, count) in enumerate(CHUNKS):
            for way, p in ((0, 7 - tau + m), (1, tau - 7 + m)):
                ok = (tau >= m) if way == 0 else (p >= 0)
                acc = (acc_l, acc_r)[way]

                @pl.when(ok & ends[1 - way])
                def _():
                    give(way, p, c).wait_recv()
                    for i in range(at, at + count):
                        part[p, i] = (mine(p, i) + acc[p, i].astype(F32)).astype(BF)

                @pl.when(ok & jnp.logical_not(ends[1 - way]))
                def _():
                    for i in range(at, at + count):
                        part[p, i] = mine(p, i).astype(BF)

                pl.when(ok & ends[way])(lambda: give(way, p, c).start())

        return 0

    def steps(at, to):
        lax.fori_loop(at, to, step_sum, 0)

    for n in range(5):
        steps(n, n + 1)
        lax.fori_loop(3 + n, 4 + n, step, 0)

    gm_all[...] = row32[...].astype(BF)
    u = dot32(gm_all[...], down_t)
    gg = jnp.sum(hidden * u, axis=-1, keepdims=True)
    gu = (rs * gt) * u
    dpre = jnp.concatenate([gu * slope, gu * silu], axis=1).astype(BF)
    dpre_ref[...] = dpre
    steps(5, 6)
    back = dot32(dpre, g_hi, NT) + dot32(dpre, g_lo, NT)
    gg_hi = gg.astype(BF).astype(F32)
    lane = iota((SH * PIECE, SIDE - TAPS), 1)
    tail = jnp.where(lane == 0, gg_hi, jnp.where(lane == 1, gg - gg_hi, 0.0))
    side32[...] = jnp.concatenate([back, tail], axis=1)
    place = pc.half * (EXP // 2) + pc.x

    def source_of(i):
        return (5 * (pc.rep - i + 8)) % 8

    def reply(p, i, sem):
        return rcopy(send_back.at[p, i], back_in.at[m, place], sem, bk_rs.at[0], source_of(i) * SH + p, pc.rep)

    def narrow(n, _):
        p = (m + n) % SH
        for i in range(TILES):
            send_back[p, i] = side32[pl.ds(pl.multiple_of(p * PIECE + i * ROWS, ROWS), ROWS), :].astype(BF)
        for i in range(TILES):
            pl.when(p != m)(lambda i=i: reply(p, i, bk_ss.at[p]).start())

            @pl.when((p == m) & (source_of(i) != pc.e))
            def _():
                reply(p, i, bo_ss.at[i]).start()

            @pl.when((p == m) & (source_of(i) == pc.e))
            def _():
                pltpu.make_async_copy(send_back.at[p, i], back_in.at[m, place], bk_rs.at[0]).start()

        return 0

    lax.fori_loop(0, SH, narrow, 0)
    steps(6, 7)
    gather_t = Gather(pc, tmine, spot(tfull), tg_ss, tg_rs)
    own_t = pltpu.make_async_copy(tmine, spot(tfull)(pc.rep), loc.at[4])
    with_rows = lambda rep: pc.tile_of(rep) < TILES
    tile_at = lambda rep: pc.tile_of(rep) % TILES
    gather_b = Gather(pc, bsum, lambda rep: back_all.at[tile_at(rep)], bg_ss, bg_rs, with_rows)
    own_b = pltpu.make_async_copy(bsum, back_all.at[pc.tile % TILES], loc.at[1])

    def home(i):
        source = source_of(i)
        return source, rcopy(
            sums.at[i], slots.at[pc.half, i, pc.x], ct_ss.at[i], ct_rs.at[pc.half], source * SH + m, pc.rep
        )

    keep_out = lambda i: pltpu.make_async_copy(sums.at[i], slots.at[pc.half, i, pc.x], ct_rs.at[pc.half])
    for c, (at, count) in enumerate(CHUNKS):
        for way in range(2):
            pl.when(ends[1 - way])(lambda way=way, c=c: give(way, m, c).wait_recv())
        for i in range(at, at + count):
            @pl.when(m == 0)
            def _():
                sums[i] = (mine(m, i) + acc_r[m, i].astype(F32)).astype(BF)

            @pl.when(m == SH - 1)
            def _():
                sums[i] = (mine(m, i) + acc_l[m, i].astype(F32)).astype(BF)

            @pl.when(ends[0] & ends[1])
            def _():
                sums[i] = (mine(m, i) + acc_l[m, i].astype(F32) + acc_r[m, i].astype(F32)).astype(BF)

            source, copy = home(i)
            pl.when(source != pc.e)(lambda copy=copy: copy.start())
            pl.when(source == pc.e)(lambda i=i: keep_out(i).start())

    t_share = dot32(pr, dpre_ref[...], TN)
    for k in range(REP):
        tp[k // 4, k % 4] = t_share[k * TP : (k + 1) * TP]
    scatter_t = Scatter(pc, tp, t_got, t_tot, t_side, t_ss, t_rs)
    scatter_t.start()
    d_share = dot32(gm_all[...], hg_ref[...], TN)
    for k in range(REP):
        dp[k % 2, k // 2] = d_share[k * dsl : (k + 1) * dsl].astype(BF)
    scatter_d = Scatter(pc, dp, d_got, d_tot, d_side, d_ss, d_rs)
    scatter_d.start()

    def out_gather(h, ss, rs):
        half = (pc.half + h) % 2
        ready = slots.at[half, pc.tile % TILES]
        gather = Gather(pc, ready, lambda rep: slots.at[half, tile_at(rep)], ss, rs, with_rows)
        wait = pltpu.make_async_copy(ready, ready, ct_rs.at[half])
        return half, gather, wait

    near_half, near, near_wait = out_gather(0, s0_ss, s0_rs)
    away_half, away, away_wait = out_gather(1, s1_ss, s1_rs)

    @pl.when(has_rows)
    def _():
        pltpu.make_async_copy(back_in, back_in, bk_rs.at[0]).wait()
        for k in range(EXP):
            bsum[k] = sum(back_in[j, k].astype(F32) for j in range(SH)).astype(BF)
        own_b.start()

    gather_b.start()
    scatter_t.add()
    pl.when(has_rows)(near_wait.wait)
    near.start()
    scatter_d.add()
    gather_b.relay()
    gather_b.relay_far()
    tmine[...] = scatter_t.result()
    gather_t.start()
    own_t.start()
    near.relay()
    near.relay_far()
    pl.when(has_rows)(away_wait.wait)
    away.start()
    gather_t.relay()
    gather_t.relay_far()
    pl.when(has_rows)(own_b.wait)
    gather_b.finish()

    for t in range(TILES):
        for k in range(EXP):
            side32[pl.ds((t * EXP + k) * ROWS, ROWS), :] = back_all[t, k].astype(F32)
    count = TILES * EXP * ROWS
    full_row = [full_id(p, r) for p, r in zip(pos_row, r_row)]
    hot_row = [(iota((count, tok), 0) == f).astype(F32) for f in full_row]
    tail = side32[...]
    gg_slot = tail[:, TAPS : TAPS + 1] + tail[:, TAPS + 1 : TAPS + 2]
    gg_row = [jnp.sum(h * gg_slot, axis=0, keepdims=True) for h in hot_row]
    b = dot32(tail.astype(BF), (hot_row[0] + hot_row[1]).astype(BF), TN)[:taps]
    mean = gg_row[0] * gates[0] + gg_row[1] * gates[1]
    grad_picked = [(g - mean) / total * (c * (1.0 - c)) for g, c in zip(gg_row, chosen)]
    grad_logits = sel_row[0] * grad_picked[0] + sel_row[1] * grad_picked[1]
    b = b + rstd_row * jnp.dot(rproj, grad_logits, precision=lax.Precision.HIGHEST, preferred_element_type=F32)
    c_row = jnp.sum(pt * b, axis=0, keepdims=True) * (rstd_row * rstd_row * (1.0 / dm))
    proj0 = dot32(s_ref[...], gm_ref[...], NT)
    proj1 = dot32(s_ref[...], stem_ref[...], NT)
    proj = proj0 + b - c_row * proj1
    rows3 = []
    for i in range(3):
        rows3.append(
            sum(shifted(proj[(3 * i + j) * chan : (3 * i + j + 1) * chan], 1 - j) for j in range(3))
        )
    a_out[0] = rows3[0][:, :wide]
    a_out[1] = rows3[2][:, wide:]
    hb = (
        rcopy(a_out.at[0], a_next, hb_ss.at[0], hb_rs.at[0], pc.exp - 1, pc.rep),
        rcopy(a_out.at[1], a_prev, hb_ss.at[1], hb_rs.at[1], pc.exp + 1, pc.rep),
    )
    pl.when(jnp.logical_not(first_row))(lambda: hb[0].start())
    pl.when(jnp.logical_not(last_row))(lambda: hb[1].start())
    glat_ref[0] = rows3[0][:, wide:] + rows3[1][:, :wide]
    glat_ref[1] = rows3[1][:, wide:] + rows3[2][:, :wide]

    @pl.when(jnp.logical_not(last_row))
    def _():
        rcopy(a_out.at[0], a_next, hb_ss.at[0], hb_rs.at[0], pc.exp, pc.partner).wait_recv()
        glat_ref[1] = glat_ref[1] + a_next[...]

    @pl.when(jnp.logical_not(first_row))
    def _():
        rcopy(a_out.at[1], a_prev, hb_ss.at[1], hb_rs.at[1], pc.exp, pc.partner).wait_recv()
        glat_ref[0] = glat_ref[0] + a_prev[...]

    away.relay()
    away.relay_far()
    gdown_ref[...] = scatter_d.result()
    gather_t.finish()
    own_t.wait()
    t_hi, t_lo = split(tfull[...].reshape(TAPS, 2 * hid)[:taps])
    gw = dot32(sg_hi[...], t_hi, TN) + dot32(sg_hi[...], t_lo, TN) + dot32(sg_lo[...], t_hi, TN)
    ggate_ref[...] = gw[:, :hid]
    gup_ref[...] = gw[:, hid:]
    square = [jnp.transpose(jnp.broadcast_to(f.astype(F32), (tok, tok)))[:, :1].astype(I32) for f in full_row]
    span = count // 2

    def out_of(half, gather):
        hot = jnp.zeros((tok, span), F32)
        for f in square:
            t = lax.shift_right_logical(f, 6)
            own = (lax.shift_right_logical(f, 5) & 1) == half
            at = jnp.where(own, t * (EXP // 2 * ROWS) + (f & 31), -1)
            hot = hot + (iota((tok, span), 1) == at).astype(F32)
        gather.finish()
        for t in range(TILES):
            for x in range(EXP // 2):
                ret32[pl.ds((t * (EXP // 2) + x) * ROWS, ROWS), :] = slots[half, t, x].astype(F32)
        return dot32(hot.astype(BF), ret32[pl.ds(0, span), :].astype(BF))

    sv_out = stem_ref[...].astype(F32) + out_of(near_half, near)

    for copy in (ha[1], hb[0]):
        pl.when(jnp.logical_not(first_row))(copy.wait_send)
    for copy in (ha[0], hb[1]):
        pl.when(jnp.logical_not(last_row))(copy.wait_send)
    scatter_t.finish()
    scatter_d.finish()

    @pl.when(has_rows)
    def _():
        for k in range(1, EXP):
            stage(k).wait_send()

        def body(k, _):
            rcopy(send_side, send_side, sd_ss.at[(pc.e + k) % EXP], sd_rs.at[0], pc.exp, pc.partner).wait_send()
            return 0

        lax.fori_loop(1, EXP, body, 0)
        seven = send_side.at[pl.ds(0, EXP - 1)]
        rcopy(seven, seven, sd_ss.at[pc.e], sd_rs.at[0], pc.exp, pc.partner).wait_send()

    def drain(s, _):
        for way, p in ((0, m - s), (1, m + s)):

            @pl.when(((p >= 0) if way == 0 else (p < SH)) & ends[way])
            def _():
                rcopy(recv.at[p], recv.at[p], ln_ss.at[way, s], ln_rs.at[p, 0], pc.exp, pc.partner).wait_send()

        for way, ok in ((0, s > m), (1, s < m)):

            @pl.when(ok & ends[way])
            def _():
                rcopy(part.at[s], acc_l.at[s], ca_ss.at[s], cl_rs.at[s, 0], pc.exp, pc.partner).wait_send()

        @pl.when(s != m)
        def _():
            rcopy(send_back.at[s], send_back.at[s], bk_ss.at[s], bk_rs.at[0], pc.exp, pc.partner).wait_send()

        return 0

    lax.fori_loop(0, SH, drain, 0)
    for i in range(TILES):

        @pl.when(source_of(i) != pc.e)
        def _():
            home(i)[1].wait_send()
            reply(m, i, bo_ss.at[i]).wait_send()

    mixed_ref[...] = (sv_out + out_of(away_half, away)).astype(BF)


def hand_over_kernel(*refs):
    half = len(refs) // 2
    for src, dst in zip(refs[:half], refs[half:]):
        dst[...] = src[...]


def local(latent, stem_weight, norm_gain, router_weight, routes, gate_weight, up_weight, down_weight, grad_mixed):
    tok, dm = grad_mixed.shape
    dsl, hid = gate_weight.shape
    rows_here, chan, wide = latent.shape
    taps = stem_weight.shape[0]
    dma = pltpu.SemaphoreType.DMA
    chunks = len(CHUNKS)
    v = pltpu.VMEM
    outs = pl.pallas_call(
        layer_kernel,
        out_shape=(
            jax.ShapeDtypeStruct((tok, dm), BF),
            jax.ShapeDtypeStruct((rows_here, chan, wide), F32),
            jax.ShapeDtypeStruct((dsl, hid), F32),
            jax.ShapeDtypeStruct((dsl, hid), F32),
            jax.ShapeDtypeStruct((dsl, hid), F32),
        ),
        in_specs=[VM] * 9,
        out_specs=(VM,) * 5,
        scratch_shapes=[
            v((EXP, ROWS, dm), BF),
            v((EXP, ROWS, SIDE), BF),
            v((SH, TILES, ROWS, dm), BF),
            v((SH, TILES, ROWS, SIDE), BF),
            v((REP, dsl, hid), BF),
            v((2, 4, TP, 2 * hid), F32),
            v((TP, 2 * hid), F32),
            v((REP, TP, 2 * hid), F32),
            v((chan, wide), BF),
            v((chan, wide), BF),
            v((4, chan, wide), F32),
            v((SIDE, tok), F32),
            v((tok, dm), BF),
            v((taps, dsl), BF),
            v((taps, dsl), BF),
            v((SH * PIECE, dm), F32),
            v((SH * PIECE, SIDE), F32),
            v((SH * PIECE, dm), BF),
            v((SH * PIECE, hid), BF),
            v((SH * PIECE, 2 * hid), BF),
            v((SH, TILES, ROWS, dm), BF),
            v((SH, TILES, ROWS, dm), BF),
            v((SH, TILES, ROWS, dm), BF),
            v((TILES, ROWS, dm), BF),
            v((SH * PIECE, dm), F32),
            v((SH, TILES, ROWS, SIDE), BF),
            v((SH, EXP, ROWS, SIDE), BF),
            v((EXP, ROWS, SIDE), BF),
            v((TILES, EXP, ROWS, SIDE), BF),
            v((2, TILES, EXP // 2, ROWS, dm), BF),
            v((2, 4, dsl, hid), BF),
            v((2, 4, TP, 2 * hid), F32),
            v((TP, 2 * hid), F32),
            v((REP, TP, 2 * hid), F32),
            v((2, chan, wide), F32),
            v((chan, wide), F32),
            v((chan, wide), F32),
        ]
        + scatter_scratch((TP, 2 * hid), F32)
        + scatter_scratch((dsl, hid), BF)
        + scatter_scratch((TP, 2 * hid), F32)
        + gather_scratch() * 6
        + [
            dma((EXP,)),
            dma((TILES,)),
            dma((EXP,)),
            dma((SH,)),
            dma((2, SH)),
            dma((SH, chunks)),
            dma((SH,)),
            dma((SH, chunks)),
            dma((SH, chunks)),
            dma((TILES,)),
            dma((2,)),
            dma((SH,)),
            dma((TILES,)),
            dma((1,)),
            dma((2,)),
            dma((2,)),
            dma((2,)),
            dma((2,)),
            dma((6,)),
        ],
        compiler_params=pltpu.CompilerParams(collective_id=0, has_side_effects=True),
        name="layer",
    )(
        latent, stem_weight, norm_gain, router_weight.T, routes.T,
        gate_weight, up_weight, down_weight.T, grad_mixed,
    )
    outs = pl.pallas_call(
        hand_over_kernel,
        out_shape=tuple(jax.ShapeDtypeStruct(o.shape, o.dtype) for o in outs),
        in_specs=[VM] * len(outs),
        out_specs=(VM,) * len(outs),
        name="hand_over",
    )(*outs)
    return tuple(outs[:4]) + (outs[4].T,)


def solution(mesh):
    return jax.shard_map(
        local,
        mesh=mesh,
        in_specs=(
            P("exp", None, None),
            P(),
            P(),
            P(),
            P("exp", None),
            P("rep", "exp"),
            P("rep", "exp"),
            P("exp", "rep"),
            P("exp", None),
        ),
        out_specs=(P("exp", None), P("exp", None, None), P("rep", "exp"), P("rep", "exp"), P("exp", "rep")),
        check_vma=False,
    )
```

```python
import jax
import jax.numpy as jnp
from jax import lax
from jax.experimental import pallas as pl
from jax.experimental.pallas import tpu as pltpu
from jax.sharding import PartitionSpec as P

F32 = jnp.float32
BF = jnp.bfloat16
I32 = jnp.int32
EXP = 8
SH = 8
REP = 8
TILES = 5
ROWS = 8
PIECE = TILES * ROWS
CHUNKS = ((0, 2), (2, 2), (4, 1))
TAPS = 192
TP = TAPS // REP
SIDE = 256
MESH = pl.DeviceIdType.MESH
VM = pl.BlockSpec(memory_space=pltpu.VMEM)


def dot32(a, b, dims=None):
    if dims is None:
        return jnp.dot(a, b, preferred_element_type=F32)
    return lax.dot_general(a, b, (dims, ((), ())), preferred_element_type=F32)


NT = ((1,), (1,))
TN = ((0,), (0,))


def split(v):
    hi = v.astype(BF)
    return hi, (v - hi.astype(F32)).astype(BF)


def iota(shape, dim):
    return lax.broadcasted_iota(I32, shape, dim)


def rcopy(src, dst, ssem, rsem, exp, rep):
    return pltpu.make_async_remote_copy(
        src_ref=src, dst_ref=dst, send_sem=ssem, recv_sem=rsem, device_id={"exp": exp, "rep": rep}, device_id_type=MESH
    )


class Place:
    def __init__(self):
        self.exp = lax.axis_index("exp")
        self.rep = lax.axis_index("rep")
        self.e = self.exp // SH
        self.half = self.e % 2
        self.x = self.e // 2
        self.m = self.exp % SH
        self.y = self.rep // 2
        self.c = self.rep % 2
        self.tile = self.tile_of(self.rep)
        self.d = 1 - 2 * self.c
        self.fwd = self.rep_at(self.d)
        self.bwd = self.rep_at(-self.d)
        self.partner = self.y * 2 + 1 - self.c

    def rep_at(self, dy):
        return ((self.y + dy + 4) % 4) * 2 + self.c

    def tile_of(self, rep):
        return (rep + 3 * self.e) % 8

    def greet(self):
        bar = pltpu.get_barrier_semaphore()

        def hello(exp, rep):
            pl.semaphore_signal(bar, inc=1, device_id={"exp": exp, "rep": rep}, device_id_type=MESH)

        for rep in (self.fwd, self.bwd, self.rep_at(2), self.partner):
            hello(self.exp, rep)

        def body(n, _):
            hello((self.exp + n) % (EXP * SH), self.rep)
            return 0

        lax.fori_loop(1, EXP * SH, body, 0)

    def enter(self):
        pl.semaphore_wait(pltpu.get_barrier_semaphore(), EXP * SH + 3)


class Gather:
    def __init__(self, pc, src, piece, ssem, rsem, valid=None):
        self.pc, self.src, self.piece, self.ssem, self.rsem = pc, src, piece, ssem, rsem
        self.valid = valid

    def guard(self, rep, fn):
        if self.valid is None:
            fn()
        else:
            pl.when(self.valid(rep))(fn)

    def copy(self, src, rep_of, k, target):
        return rcopy(src, self.piece(rep_of), self.ssem.at[k], self.rsem.at[rep_of], self.pc.exp, target)

    def moves(self):
        pc = self.pc
        far = pc.rep_at(2)
        own, part = pc.rep, pc.partner
        return [
            (self.src, own, 0, pc.fwd),
            (self.src, own, 1, pc.bwd),
            (self.src, own, 2, part),
            (self.src, own, 3, far),
            (self.piece(pc.bwd), pc.bwd, 4, part),
            (self.piece(pc.fwd), pc.fwd, 5, part),
            (self.piece(far), far, 6, part),
        ]

    def start(self):
        def go():
            mv = self.moves()
            for k in (3, 0, 1, 2):
                self.copy(*mv[k]).start()

        self.guard(self.pc.rep, go)

    def arrive(self, rep):
        self.copy(self.piece(rep), rep, 0, self.pc.partner).wait_recv()

    def relay(self):
        mv = self.moves()

        def near():
            self.arrive(self.pc.bwd)
            self.copy(*mv[4]).start()

        self.guard(self.pc.bwd, near)

        def other():
            self.arrive(self.pc.fwd)
            self.copy(*mv[5]).start()

        self.guard(self.pc.fwd, other)

    def relay_far(self):
        far = self.pc.rep_at(2)

        def go():
            self.arrive(far)
            self.copy(*self.moves()[6]).start()

        self.guard(far, go)

    def finish(self):
        for dy in range(4):
            rep = ((self.pc.y + dy) % 4) * 2 + 1 - self.pc.c
            self.guard(rep, lambda rep=rep: self.arrive(rep))
        for mv in self.moves():
            self.guard(mv[1], lambda mv=mv: self.copy(*mv).wait_send())


class Scatter:
    def __init__(self, pc, src, got, total, side, ssem, rsem):
        self.pc, self.src, self.got, self.total, self.side, self.ssem, self.rsem = pc, src, got, total, side, ssem, rsem

    def copy(self, k):
        pc = self.pc
        y, d = pc.y, pc.d
        at = lambda dy: self.total.at[(y + dy + 4) % 4]
        src, dst, rep = (
            (self.src.at[1 - pc.c], self.got, pc.partner),
            (at(2), self.side.at[0], pc.rep_at(2)),
            (at(-d), self.side.at[1], pc.bwd),
            (at(d), self.side.at[2], pc.fwd),
        )[k]
        return rcopy(src, dst, self.ssem.at[k], self.rsem.at[k], pc.exp, rep)

    def start(self):
        self.copy(0).start()

    def add(self):
        self.copy(0).wait_recv()

        def body(k, _):
            self.total[k] = (self.src[self.pc.c, k].astype(F32) + self.got[k].astype(F32)).astype(self.total.dtype)
            return 0

        lax.fori_loop(0, 4, body, 0)
        for k in (1, 2, 3):
            self.copy(k).start()

    def result(self):
        for k in (1, 2, 3):
            self.copy(k).wait_recv()
        return self.total[self.pc.y].astype(F32) + sum(self.side[k].astype(F32) for k in range(3))

    def finish(self):
        for k in range(4):
            self.copy(k).wait_send()


def scatter_scratch(block, dtype):
    return [
        pltpu.VMEM((4,) + block, dtype),
        pltpu.VMEM((4,) + block, dtype),
        pltpu.VMEM((3,) + block, dtype),
        pltpu.SemaphoreType.DMA((4,)),
        pltpu.SemaphoreType.DMA((4,)),
    ]


def gather_scratch():
    return [pltpu.SemaphoreType.DMA((7,)), pltpu.SemaphoreType.DMA((REP,))]


def layer_kernel(
    latent, s_ref, gain_ref, wr_ref, routes_ref, wg_ref, wu_ref, wd_ref, gm_ref,
    mixed_ref, glat_ref, ggate_ref, gup_ref, gdown_ref,
    send, send_side, recv, recv_side, wfull, gp, gmine, gfull,
    h_prev, h_next, lat4, ptx, stem_ref, sg_hi, sg_lo,
    row32, side32, gm_all, hg_ref, dpre_ref,
    part, acc_l, acc_r, sums, ret32, send_back, back_in, bsum, back_all, slots, dp, tp, tmine, tfull, a_out, a_prev, a_next,
    *sems
):
    (g_got, g_tot, g_side, g_ss, g_rs, d_got, d_tot, d_side, d_ss, d_rs, t_got, t_tot, t_side, t_ss, t_rs,
     ag_ss, ag_rs, wg_ss, wg_rs, tg_ss, tg_rs, bg_ss, bg_rs, s0_ss, s0_rs, s1_ss, s1_rs,
     st_ss, st_rs, sd_ss, sd_rs, ln_ss, ln_rs, ca_ss, cl_rs, cr_rs, ct_ss, ct_rs, bk_ss, bo_ss, bk_rs,
     ha_ss, ha_rs, hb_ss, hb_rs, loc) = sems
    pc = Place()
    m = pc.m
    tok, dm = gm_ref.shape
    hid = wg_ref.shape[1]
    taps = s_ref.shape[0]
    wide = tok // 2
    top = routes_ref.shape[0]
    has_rows = pc.tile < TILES

    pc.greet()

    upper = (iota((tok, tok), 0) < iota((tok, tok), 1)).astype(BF)
    r_row = [routes_ref[k : k + 1, :] for k in range(top)]
    sel_row = [(iota((EXP, tok), 0) == r).astype(F32) for r in r_row]
    before_row = dot32((sel_row[0] + sel_row[1]).astype(BF), upper)
    pos_row = [jnp.sum(s * before_row, axis=0, keepdims=True).astype(I32) for s in sel_row]

    def here_id(pos, r):
        q = pos - ROWS * pc.tile
        return jnp.where((q >= 0) & (q < ROWS), r * ROWS + q, -1)

    def full_id(pos, r):
        t = lax.shift_right_logical(pos, 3)
        place = (r & 1) * (EXP // 2) + lax.shift_right_logical(r, 1)
        return t * (EXP * ROWS) + place * ROWS + (pos - t * ROWS)

    hot_here = [(iota((EXP * ROWS, tok), 0) == here_id(p, r)).astype(F32) for p, r in zip(pos_row, r_row)]
    hot_here_b = [h.astype(BF) for h in hot_here]
    picked_rows = dot32(hot_here_b[0] + hot_here_b[1], gm_ref[...])
    for e in range(EXP):
        send[e] = picked_rows[e * ROWS : (e + 1) * ROWS].astype(BF)

    gain = gain_ref[...].reshape(1, dm)
    dsl = wg_ref.shape[0]
    sg = s_ref[...].astype(F32) * gain
    hi, lo = split(sg)
    pick = (iota((dm, dsl), 0) == iota((dm, dsl), 1) + pc.rep * dsl).astype(BF)
    s_hi = dot32(hi, pick).astype(BF)
    s_lo = dot32(lo, pick).astype(BF)
    sg_hi[...] = s_hi
    sg_lo[...] = s_lo
    zero_taps = jnp.zeros((TAPS - taps, 2 * hid), F32)
    share = jnp.concatenate(
        [dot32(s_hi, w[...]) + dot32(s_lo, w[...]) for w in (wg_ref, wu_ref)], axis=1
    )
    share = jnp.concatenate([share, zero_taps], axis=0)
    for k in range(REP):
        gp[k // 4, k % 4] = share[k * TP : (k + 1) * TP]
    rproj = dot32(hi, wr_ref[...], NT) + dot32(lo, wr_ref[...], NT)

    pc.enter()

    ha = (
        rcopy(latent.at[1], h_prev, ha_ss.at[0], ha_rs.at[0], pc.exp + 1, pc.rep),
        rcopy(latent.at[0], h_next, ha_ss.at[1], ha_rs.at[1], pc.exp - 1, pc.rep),
    )
    first_row, last_row = pc.exp == 0, pc.exp == EXP * SH - 1
    pl.when(jnp.logical_not(last_row))(lambda: ha[0].start())
    pl.when(jnp.logical_not(first_row))(lambda: ha[1].start())

    def stage(k):
        peer = (pc.e + k) % EXP
        return rcopy(send.at[peer], recv.at[m, pc.tile], st_ss.at[k], st_rs.at[pc.tile], peer * SH + m, pc.rep)

    keep_gm = pltpu.make_async_copy(send.at[pc.e], recv.at[m, pc.tile], loc.at[0])

    @pl.when(has_rows)
    def _():
        for k in (1, 7, 2, 6, 3, 5, 4):
            stage(k).start()
        keep_gm.start()

    gather_w = Gather(pc, wd_ref, lambda rep: wfull.at[rep], wg_ss, wg_rs)
    own_w = pltpu.make_async_copy(wd_ref, wfull.at[pc.rep], loc.at[2])
    gather_w.start()
    own_w.start()

    scatter_g = Scatter(pc, gp, g_got, g_tot, g_side, g_ss, g_rs)
    scatter_g.start()

    @pl.when(jnp.logical_not(first_row))
    def _():
        rcopy(latent.at[1], h_prev, ha_ss.at[0], ha_rs.at[0], pc.exp, pc.partner).wait_recv()
        lat4[0] = h_prev[...].astype(F32)

    @pl.when(first_row)
    def _():
        lat4[0] = jnp.zeros(lat4.shape[1:], F32)

    @pl.when(jnp.logical_not(last_row))
    def _():
        rcopy(latent.at[0], h_next, ha_ss.at[1], ha_rs.at[1], pc.exp, pc.partner).wait_recv()
        lat4[3] = h_next[...].astype(F32)

    @pl.when(last_row)
    def _():
        lat4[3] = jnp.zeros(lat4.shape[1:], F32)

    lat4[1] = latent[0].astype(F32)
    lat4[2] = latent[1].astype(F32)
    chan = lat4.shape[1]
    col = iota((chan, tok), 1)
    col = jnp.where(col >= wide, col - wide, col)

    def shifted(v, by):
        if by == 0:
            return v
        rolled = pltpu.roll(v, (-by) % tok, 1)
        return jnp.where(col == (0 if by < 0 else wide - 1), 0.0, rolled)

    for i in range(3):
        two = jnp.concatenate([lat4[i], lat4[i + 1]], axis=1)
        for j in range(3):
            ptx[pl.ds((3 * i + j) * chan, chan), :] = shifted(two, j - 1)
    ptx[pl.ds(taps, SIDE - taps), :] = jnp.zeros((SIDE - taps, tok), F32)
    pt = ptx[pl.ds(0, taps), :]
    stem = dot32(pt.astype(BF), s_ref[...], TN).astype(BF)
    stem_ref[...] = stem
    sv = stem.astype(F32)
    rstd = lax.rsqrt(jnp.mean(sv * sv, axis=-1, keepdims=True) + 1e-06)
    rstd_row = jnp.transpose(jnp.broadcast_to(rstd, (tok, tok)))[0:1, :]
    normed = (sv * rstd * gain).astype(BF)
    logits = dot32(wr_ref[...], normed, NT)
    picked = [jnp.sum(s * logits, axis=0, keepdims=True) for s in sel_row]
    chosen = [jax.nn.sigmoid(p) for p in picked]
    total = chosen[0] + chosen[1]
    gates = [c / total for c in chosen]
    r_hi, r_lo = split(rstd_row)
    ptx[pl.ds(TAPS, 1), :] = r_hi.astype(F32)
    ptx[pl.ds(TAPS + 1, 1), :] = r_lo.astype(F32)
    side = jnp.zeros((EXP * ROWS, SIDE), F32)
    for k in range(top):
        k_hi, k_lo = split(gates[k])
        ptx[pl.ds(TAPS + 2, 1), :] = k_hi.astype(F32)
        ptx[pl.ds(TAPS + 3, 1), :] = k_lo.astype(F32)
        side = side + dot32(hot_here_b[k], ptx[...].astype(BF), NT)
    for e in range(EXP):
        send_side[e] = side[e * ROWS : (e + 1) * ROWS].astype(BF)

    scatter_g.add()

    def to_all(n):
        dest = (pc.exp + n) % (EXP * SH)
        e = dest // SH
        return rcopy(send_side.at[e], recv_side.at[m, pc.tile], sd_ss.at[e], sd_rs.at[m], dest, pc.rep)

    @pl.when(has_rows)
    def _():
        def body(n, _):
            to_all(n).start()
            return 0

        lax.fori_loop(1, EXP * SH, body, 0)
        pltpu.make_async_copy(send_side.at[pc.e], recv_side.at[m, pc.tile], sd_rs.at[m]).start()

    ends = (m < SH - 1, m > 0)

    def hop(way, p, c, s):
        at = pl.ds(CHUNKS[c][0], CHUNKS[c][1])
        ref = recv.at[p, at]
        return rcopy(ref, ref, ln_ss.at[way, s], ln_rs.at[p, c], pc.exp + 1 - 2 * way, pc.rep)

    def arrived(i):
        source = (5 * (pc.rep - i + 8)) % 8

        @pl.when(source != pc.e)
        def _():
            rcopy(recv.at[m, i], recv.at[m, i], st_ss.at[0], st_rs.at[i], pc.exp, pc.partner).wait_recv()

    def widen(p):
        for i in range(TILES):
            row32[pl.ds(pl.multiple_of(p * PIECE + i * ROWS, ROWS), ROWS), :] = recv[p, i].astype(F32)

    def step(s, _):
        for c in range(len(CHUNKS)):
            for way, p in ((0, m - s), (1, m + s)):
                ok = (p >= 0) if way == 0 else (p < SH)

                @pl.when(ok)
                def _():
                    hop(way, p, c, s).wait_recv()

                    @pl.when(ends[way])
                    def _():
                        hop(way, p, c, s).start()

        for way, p in ((0, m - s), (1, m + s)):
            pl.when((p >= 0) if way == 0 else (p < SH))(lambda p=p: widen(p))
        return 0

    @pl.when(has_rows)
    def _():
        keep_gm.wait()

    for c, (at, count) in enumerate(CHUNKS):
        for i in range(at, at + count):
            arrived(i)
        for way in range(2):
            pl.when(ends[way])(lambda way=way, c=c: hop(way, m, c, 0).start())
    gmine[...] = scatter_g.result()
    spot = lambda ref: lambda rep: ref.at[(rep % 2) * 4 + rep // 2]
    gather_g = Gather(pc, gmine, spot(gfull), ag_ss, ag_rs)
    own_g = pltpu.make_async_copy(gmine, spot(gfull)(pc.rep), loc.at[3])
    gather_g.start()
    own_g.start()
    widen(m)
    gather_w.relay()
    lax.fori_loop(1, 2, step, 0)
    gather_w.relay_far()
    gather_g.relay()
    lax.fori_loop(2, 3, step, 0)
    gather_g.relay_far()
    lax.fori_loop(3, 4, step, 0)
    gather_g.finish()
    gather_w.finish()
    scatter_g.finish()
    own_w.wait()
    own_g.wait()

    def widen_side(p, _):
        pltpu.make_async_copy(recv_side.at[p], recv_side.at[p], sd_rs.at[p]).wait()
        for i in range(TILES):
            side32[pl.ds(pl.multiple_of(p * PIECE + i * ROWS, ROWS), ROWS), :] = recv_side[p, i].astype(F32)
        return 0

    lax.fori_loop(0, SH, widen_side, 0)
    more = side32[...]
    pr = more[:, :TAPS].astype(BF)
    rs = more[:, TAPS : TAPS + 1] + more[:, TAPS + 1 : TAPS + 2]
    gt = more[:, TAPS + 2 : TAPS + 3] + more[:, TAPS + 3 : TAPS + 4]
    g_hi, g_lo = split(gfull[...].reshape(TAPS, 2 * hid))
    pre = rs * (dot32(pr, g_hi) + dot32(pr, g_lo))
    pg, pu = pre[:, :hid], pre[:, hid:]
    sigma = jax.nn.sigmoid(pg)
    silu = pg * sigma
    hidden = silu * pu
    slope = pu * sigma * (1.0 + pg * (1.0 - sigma))
    hg = (gt * hidden).astype(BF)
    down_t = wfull[...].reshape(dm, hid)
    ret32[...] = dot32(hg, down_t, NT)
    hg_ref[...] = hg

    def give(way, p, c):
        at = pl.ds(CHUNKS[c][0], CHUNKS[c][1])
        dst, rsem = ((acc_l, cl_rs), (acc_r, cr_rs))[way]
        return rcopy(
            part.at[p, at], dst.at[p, at], ca_ss.at[p], rsem.at[p, c], pc.exp + 1 - 2 * way, pc.rep
        )

    def mine(p, i):
        return ret32[pl.ds(pl.multiple_of(p * PIECE + i * ROWS, ROWS), ROWS), :]

    def step_sum(tau, _):
        for c, (at, count) in enumerate(CHUNKS):
            for way, p in ((0, 7 - tau + m), (1, tau - 7 + m)):
                ok = (tau >= m) if way == 0 else (p >= 0)
                acc = (acc_l, acc_r)[way]

                @pl.when(ok & ends[1 - way])
                def _():
                    give(way, p, c).wait_recv()
                    for i in range(at, at + count):
                        part[p, i] = (mine(p, i) + acc[p, i].astype(F32)).astype(BF)

                @pl.when(ok & jnp.logical_not(ends[1 - way]))
                def _():
                    for i in range(at, at + count):
                        part[p, i] = mine(p, i).astype(BF)

                pl.when(ok & ends[way])(lambda: give(way, p, c).start())

        return 0

    def steps(at, to):
        lax.fori_loop(at, to, step_sum, 0)

    for n in range(4):
        steps(n, n + 1)
        lax.fori_loop(4 + n, 5 + n, step, 0)

    gm_all[...] = row32[...].astype(BF)
    u = dot32(gm_all[...], down_t)
    gg = jnp.sum(hidden * u, axis=-1, keepdims=True)
    gu = (rs * gt) * u
    dpre = jnp.concatenate([gu * slope, gu * silu], axis=1).astype(BF)
    dpre_ref[...] = dpre
    back = dot32(dpre, g_hi, NT) + dot32(dpre, g_lo, NT)
    gg_hi = gg.astype(BF).astype(F32)
    lane = iota((SH * PIECE, SIDE - TAPS), 1)
    tail = jnp.where(lane == 0, gg_hi, jnp.where(lane == 1, gg - gg_hi, 0.0))
    side32[...] = jnp.concatenate([back, tail], axis=1)
    place = pc.half * (EXP // 2) + pc.x

    def source_of(i):
        return (5 * (pc.rep - i + 8)) % 8

    def reply(p, i, sem):
        return rcopy(send_back.at[p, i], back_in.at[m, place], sem, bk_rs.at[0], source_of(i) * SH + p, pc.rep)

    def narrow(n, _):
        p = (m + n) % SH
        for i in range(TILES):
            send_back[p, i] = side32[pl.ds(pl.multiple_of(p * PIECE + i * ROWS, ROWS), ROWS), :].astype(BF)
        for i in range(TILES):
            pl.when(p != m)(lambda i=i: reply(p, i, bk_ss.at[p]).start())

            @pl.when((p == m) & (source_of(i) != pc.e))
            def _():
                reply(p, i, bo_ss.at[i]).start()

            @pl.when((p == m) & (source_of(i) == pc.e))
            def _():
                pltpu.make_async_copy(send_back.at[p, i], back_in.at[m, place], bk_rs.at[0]).start()

        return 0

    lax.fori_loop(0, SH, narrow, 0)
    steps(4, 5)
    t_share = dot32(pr, dpre_ref[...], TN)
    for k in range(REP):
        tp[k // 4, k % 4] = t_share[k * TP : (k + 1) * TP]
    scatter_t = Scatter(pc, tp, t_got, t_tot, t_side, t_ss, t_rs)
    scatter_t.start()
    d_share = dot32(gm_all[...], hg_ref[...], TN)
    for k in range(REP):
        dp[k % 2, k // 2] = d_share[k * dsl : (k + 1) * dsl].astype(BF)
    scatter_d = Scatter(pc, dp, d_got, d_tot, d_side, d_ss, d_rs)
    scatter_d.start()
    steps(5, 6)
    scatter_t.add()
    scatter_d.add()
    steps(6, 7)
    gather_t = Gather(pc, tmine, spot(tfull), tg_ss, tg_rs)
    own_t = pltpu.make_async_copy(tmine, spot(tfull)(pc.rep), loc.at[4])
    with_rows = lambda rep: pc.tile_of(rep) < TILES
    tile_at = lambda rep: pc.tile_of(rep) % TILES
    gather_b = Gather(pc, bsum, lambda rep: back_all.at[tile_at(rep)], bg_ss, bg_rs, with_rows)
    own_b = pltpu.make_async_copy(bsum, back_all.at[pc.tile % TILES], loc.at[1])

    def home(i):
        source = source_of(i)
        return source, rcopy(
            sums.at[i], slots.at[pc.half, i, pc.x], ct_ss.at[i], ct_rs.at[pc.half], source * SH + m, pc.rep
        )

    keep_out = lambda i: pltpu.make_async_copy(sums.at[i], slots.at[pc.half, i, pc.x], ct_rs.at[pc.half])
    for c, (at, count) in enumerate(CHUNKS):
        for way in range(2):
            pl.when(ends[1 - way])(lambda way=way, c=c: give(way, m, c).wait_recv())
        for i in range(at, at + count):
            @pl.when(m == 0)
            def _():
                sums[i] = (mine(m, i) + acc_r[m, i].astype(F32)).astype(BF)

            @pl.when(m == SH - 1)
            def _():
                sums[i] = (mine(m, i) + acc_l[m, i].astype(F32)).astype(BF)

            @pl.when(ends[0] & ends[1])
            def _():
                sums[i] = (mine(m, i) + acc_l[m, i].astype(F32) + acc_r[m, i].astype(F32)).astype(BF)

            source, copy = home(i)
            pl.when(source != pc.e)(lambda copy=copy: copy.start())
            pl.when(source == pc.e)(lambda i=i: keep_out(i).start())

    def out_gather(h, ss, rs):
        half = (pc.half + h) % 2
        ready = slots.at[half, pc.tile % TILES]
        gather = Gather(pc, ready, lambda rep: slots.at[half, tile_at(rep)], ss, rs, with_rows)
        wait = pltpu.make_async_copy(ready, ready, ct_rs.at[half])
        return half, gather, wait

    near_half, near, near_wait = out_gather(0, s0_ss, s0_rs)
    away_half, away, away_wait = out_gather(1, s1_ss, s1_rs)

    @pl.when(has_rows)
    def _():
        pltpu.make_async_copy(back_in, back_in, bk_rs.at[0]).wait()
        for k in range(EXP):
            bsum[k] = sum(back_in[j, k].astype(F32) for j in range(SH)).astype(BF)
        own_b.start()

    gather_b.start()
    tmine[...] = scatter_t.result()
    gather_t.start()
    own_t.start()
    pl.when(has_rows)(near_wait.wait)
    near.start()
    gather_b.relay()
    gather_t.relay()
    gather_b.relay_far()
    near.relay()
    gather_t.relay_far()
    near.relay_far()
    pl.when(has_rows)(away_wait.wait)
    away.start()
    gdown_ref[...] = scatter_d.result()
    pl.when(has_rows)(own_b.wait)
    gather_b.finish()

    for t in range(TILES):
        for k in range(EXP):
            side32[pl.ds((t * EXP + k) * ROWS, ROWS), :] = back_all[t, k].astype(F32)
    count = TILES * EXP * ROWS
    full_row = [full_id(p, r) for p, r in zip(pos_row, r_row)]
    hot_row = [(iota((count, tok), 0) == f).astype(F32) for f in full_row]
    tail = side32[...]
    gg_slot = tail[:, TAPS : TAPS + 1] + tail[:, TAPS + 1 : TAPS + 2]
    gg_row = [jnp.sum(h * gg_slot, axis=0, keepdims=True) for h in hot_row]
    b = dot32(tail.astype(BF), (hot_row[0] + hot_row[1]).astype(BF), TN)[:taps]
    mean = gg_row[0] * gates[0] + gg_row[1] * gates[1]
    grad_picked = [(g - mean) / total * (c * (1.0 - c)) for g, c in zip(gg_row, chosen)]
    grad_logits = sel_row[0] * grad_picked[0] + sel_row[1] * grad_picked[1]
    b = b + rstd_row * jnp.dot(rproj, grad_logits, precision=lax.Precision.HIGHEST, preferred_element_type=F32)
    c_row = jnp.sum(pt * b, axis=0, keepdims=True) * (rstd_row * rstd_row * (1.0 / dm))
    proj0 = dot32(s_ref[...], gm_ref[...], NT)
    proj1 = dot32(s_ref[...], stem_ref[...], NT)
    proj = proj0 + b - c_row * proj1
    rows3 = []
    for i in range(3):
        rows3.append(
            sum(shifted(proj[(3 * i + j) * chan : (3 * i + j + 1) * chan], 1 - j) for j in range(3))
        )
    a_out[0] = rows3[0][:, :wide]
    a_out[1] = rows3[2][:, wide:]
    hb = (
        rcopy(a_out.at[0], a_next, hb_ss.at[0], hb_rs.at[0], pc.exp - 1, pc.rep),
        rcopy(a_out.at[1], a_prev, hb_ss.at[1], hb_rs.at[1], pc.exp + 1, pc.rep),
    )
    pl.when(jnp.logical_not(first_row))(lambda: hb[0].start())
    pl.when(jnp.logical_not(last_row))(lambda: hb[1].start())
    glat_ref[0] = rows3[0][:, wide:] + rows3[1][:, :wide]
    glat_ref[1] = rows3[1][:, wide:] + rows3[2][:, :wide]

    @pl.when(jnp.logical_not(last_row))
    def _():
        rcopy(a_out.at[0], a_next, hb_ss.at[0], hb_rs.at[0], pc.exp, pc.partner).wait_recv()
        glat_ref[1] = glat_ref[1] + a_next[...]

    @pl.when(jnp.logical_not(first_row))
    def _():
        rcopy(a_out.at[1], a_prev, hb_ss.at[1], hb_rs.at[1], pc.exp, pc.partner).wait_recv()
        glat_ref[0] = glat_ref[0] + a_prev[...]

    away.relay()
    away.relay_far()
    gather_t.finish()
    own_t.wait()
    t_hi, t_lo = split(tfull[...].reshape(TAPS, 2 * hid)[:taps])
    gw = dot32(sg_hi[...], t_hi, TN) + dot32(sg_hi[...], t_lo, TN) + dot32(sg_lo[...], t_hi, TN)
    ggate_ref[...] = gw[:, :hid]
    gup_ref[...] = gw[:, hid:]
    square = [jnp.transpose(jnp.broadcast_to(f.astype(F32), (tok, tok)))[:, :1].astype(I32) for f in full_row]
    span = count // 2

    def out_of(half, gather):
        hot = jnp.zeros((tok, span), F32)
        for f in square:
            t = lax.shift_right_logical(f, 6)
            own = (lax.shift_right_logical(f, 5) & 1) == half
            at = jnp.where(own, t * (EXP // 2 * ROWS) + (f & 31), -1)
            hot = hot + (iota((tok, span), 1) == at).astype(F32)
        gather.finish()
        for t in range(TILES):
            for x in range(EXP // 2):
                ret32[pl.ds((t * (EXP // 2) + x) * ROWS, ROWS), :] = slots[half, t, x].astype(F32)
        return dot32(hot.astype(BF), ret32[pl.ds(0, span), :].astype(BF))

    sv_out = stem_ref[...].astype(F32) + out_of(near_half, near)

    for copy in (ha[1], hb[0]):
        pl.when(jnp.logical_not(first_row))(copy.wait_send)
    for copy in (ha[0], hb[1]):
        pl.when(jnp.logical_not(last_row))(copy.wait_send)
    scatter_t.finish()
    scatter_d.finish()

    @pl.when(has_rows)
    def _():
        for k in range(1, EXP):
            stage(k).wait_send()

        def body(k, _):
            rcopy(send_side, send_side, sd_ss.at[(pc.e + k) % EXP], sd_rs.at[0], pc.exp, pc.partner).wait_send()
            return 0

        lax.fori_loop(1, EXP, body, 0)
        seven = send_side.at[pl.ds(0, EXP - 1)]
        rcopy(seven, seven, sd_ss.at[pc.e], sd_rs.at[0], pc.exp, pc.partner).wait_send()

    def drain(s, _):
        for way, p in ((0, m - s), (1, m + s)):

            @pl.when(((p >= 0) if way == 0 else (p < SH)) & ends[way])
            def _():
                rcopy(recv.at[p], recv.at[p], ln_ss.at[way, s], ln_rs.at[p, 0], pc.exp, pc.partner).wait_send()

        for way, ok in ((0, s > m), (1, s < m)):

            @pl.when(ok & ends[way])
            def _():
                rcopy(part.at[s], acc_l.at[s], ca_ss.at[s], cl_rs.at[s, 0], pc.exp, pc.partner).wait_send()

        @pl.when(s != m)
        def _():
            rcopy(send_back.at[s], send_back.at[s], bk_ss.at[s], bk_rs.at[0], pc.exp, pc.partner).wait_send()

        return 0

    lax.fori_loop(0, SH, drain, 0)
    for i in range(TILES):

        @pl.when(source_of(i) != pc.e)
        def _():
            home(i)[1].wait_send()
            reply(m, i, bo_ss.at[i]).wait_send()

    mixed_ref[...] = (sv_out + out_of(away_half, away)).astype(BF)


def hand_over_kernel(*refs):
    half = len(refs) // 2
    for src, dst in zip(refs[:half], refs[half:]):
        dst[...] = src[...]


def local(latent, stem_weight, norm_gain, router_weight, routes, gate_weight, up_weight, down_weight, grad_mixed):
    tok, dm = grad_mixed.shape
    dsl, hid = gate_weight.shape
    rows_here, chan, wide = latent.shape
    taps = stem_weight.shape[0]
    dma = pltpu.SemaphoreType.DMA
    chunks = len(CHUNKS)
    v = pltpu.VMEM
    outs = pl.pallas_call(
        layer_kernel,
        out_shape=(
            jax.ShapeDtypeStruct((tok, dm), BF),
            jax.ShapeDtypeStruct((rows_here, chan, wide), F32),
            jax.ShapeDtypeStruct((dsl, hid), F32),
            jax.ShapeDtypeStruct((dsl, hid), F32),
            jax.ShapeDtypeStruct((dsl, hid), F32),
        ),
        in_specs=[VM] * 9,
        out_specs=(VM,) * 5,
        scratch_shapes=[
            v((EXP, ROWS, dm), BF),
            v((EXP, ROWS, SIDE), BF),
            v((SH, TILES, ROWS, dm), BF),
            v((SH, TILES, ROWS, SIDE), BF),
            v((REP, dsl, hid), BF),
            v((2, 4, TP, 2 * hid), F32),
            v((TP, 2 * hid), F32),
            v((REP, TP, 2 * hid), F32),
            v((chan, wide), BF),
            v((chan, wide), BF),
            v((4, chan, wide), F32),
            v((SIDE, tok), F32),
            v((tok, dm), BF),
            v((taps, dsl), BF),
            v((taps, dsl), BF),
            v((SH * PIECE, dm), F32),
            v((SH * PIECE, SIDE), F32),
            v((SH * PIECE, dm), BF),
            v((SH * PIECE, hid), BF),
            v((SH * PIECE, 2 * hid), BF),
            v((SH, TILES, ROWS, dm), BF),
            v((SH, TILES, ROWS, dm), BF),
            v((SH, TILES, ROWS, dm), BF),
            v((TILES, ROWS, dm), BF),
            v((SH * PIECE, dm), F32),
            v((SH, TILES, ROWS, SIDE), BF),
            v((SH, EXP, ROWS, SIDE), BF),
            v((EXP, ROWS, SIDE), BF),
            v((TILES, EXP, ROWS, SIDE), BF),
            v((2, TILES, EXP // 2, ROWS, dm), BF),
            v((2, 4, dsl, hid), BF),
            v((2, 4, TP, 2 * hid), F32),
            v((TP, 2 * hid), F32),
            v((REP, TP, 2 * hid), F32),
            v((2, chan, wide), F32),
            v((chan, wide), F32),
            v((chan, wide), F32),
        ]
        + scatter_scratch((TP, 2 * hid), F32)
        + scatter_scratch((dsl, hid), BF)
        + scatter_scratch((TP, 2 * hid), F32)
        + gather_scratch() * 6
        + [
            dma((EXP,)),
            dma((TILES,)),
            dma((EXP,)),
            dma((SH,)),
            dma((2, SH)),
            dma((SH, chunks)),
            dma((SH,)),
            dma((SH, chunks)),
            dma((SH, chunks)),
            dma((TILES,)),
            dma((2,)),
            dma((SH,)),
            dma((TILES,)),
            dma((1,)),
            dma((2,)),
            dma((2,)),
            dma((2,)),
            dma((2,)),
            dma((6,)),
        ],
        compiler_params=pltpu.CompilerParams(collective_id=0, has_side_effects=True),
        name="layer",
    )(
        latent, stem_weight, norm_gain, router_weight.T, routes.T,
        gate_weight, up_weight, down_weight.T, grad_mixed,
    )
    outs = pl.pallas_call(
        hand_over_kernel,
        out_shape=tuple(jax.ShapeDtypeStruct(o.shape, o.dtype) for o in outs),
        in_specs=[VM] * len(outs),
        out_specs=(VM,) * len(outs),
        name="hand_over",
    )(*outs)
    return tuple(outs[:4]) + (outs[4].T,)


def solution(mesh):
    return jax.shard_map(
        local,
        mesh=mesh,
        in_specs=(
            P("exp", None, None),
            P(),
            P(),
            P(),
            P("exp", None),
            P("rep", "exp"),
            P("rep", "exp"),
            P("exp", "rep"),
            P("exp", None),
        ),
        out_specs=(P("exp", None), P("exp", None, None), P("rep", "exp"), P("rep", "exp"), P("exp", "rep")),
        check_vma=False,
    )
```

```python
import jax
import jax.numpy as jnp
from jax import lax
from jax.experimental import pallas as pl
from jax.experimental.pallas import tpu as pltpu
from jax.sharding import PartitionSpec as P

F32 = jnp.float32
BF = jnp.bfloat16
I32 = jnp.int32
EXP = 8
SH = 8
REP = 8
TILES = 5
ROWS = 8
PIECE = TILES * ROWS
CHUNKS = ((0, 2), (2, 2), (4, 1))
TAPS = 192
TP = TAPS // REP
SIDE = 256
MESH = pl.DeviceIdType.MESH
VM = pl.BlockSpec(memory_space=pltpu.VMEM)


def dot32(a, b, dims=None):
    if dims is None:
        return jnp.dot(a, b, preferred_element_type=F32)
    return lax.dot_general(a, b, (dims, ((), ())), preferred_element_type=F32)


NT = ((1,), (1,))
TN = ((0,), (0,))


def split(v):
    hi = v.astype(BF)
    return hi, (v - hi.astype(F32)).astype(BF)


def iota(shape, dim):
    return lax.broadcasted_iota(I32, shape, dim)


def rcopy(src, dst, ssem, rsem, exp, rep):
    return pltpu.make_async_remote_copy(
        src_ref=src, dst_ref=dst, send_sem=ssem, recv_sem=rsem, device_id={"exp": exp, "rep": rep}, device_id_type=MESH
    )


class Place:
    def __init__(self):
        self.exp = lax.axis_index("exp")
        self.rep = lax.axis_index("rep")
        self.e = self.exp // SH
        self.half = self.e % 2
        self.x = self.e // 2
        self.m = self.exp % SH
        self.y = self.rep // 2
        self.c = self.rep % 2
        self.tile = self.tile_of(self.rep)
        self.d = 1 - 2 * self.c
        self.fwd = self.rep_at(self.d)
        self.bwd = self.rep_at(-self.d)
        self.partner = self.y * 2 + 1 - self.c

    def rep_at(self, dy):
        return ((self.y + dy + 4) % 4) * 2 + self.c

    def tile_of(self, rep):
        return (rep + 3 * self.e) % 8

    def greet(self):
        bar = pltpu.get_barrier_semaphore()

        def hello(exp, rep):
            pl.semaphore_signal(bar, inc=1, device_id={"exp": exp, "rep": rep}, device_id_type=MESH)

        for rep in (self.fwd, self.bwd, self.rep_at(2), self.partner):
            hello(self.exp, rep)

        def body(n, _):
            hello((self.exp + n) % (EXP * SH), self.rep)
            return 0

        lax.fori_loop(1, EXP * SH, body, 0)

    def enter(self):
        pl.semaphore_wait(pltpu.get_barrier_semaphore(), EXP * SH + 3)


class Gather:
    def __init__(self, pc, src, piece, ssem, rsem, valid=None):
        self.pc, self.src, self.piece, self.ssem, self.rsem = pc, src, piece, ssem, rsem
        self.valid = valid

    def guard(self, rep, fn):
        if self.valid is None:
            fn()
        else:
            pl.when(self.valid(rep))(fn)

    def copy(self, src, rep_of, k, target):
        return rcopy(src, self.piece(rep_of), self.ssem.at[k], self.rsem.at[rep_of], self.pc.exp, target)

    def moves(self):
        pc = self.pc
        far = pc.rep_at(2)
        own, part = pc.rep, pc.partner
        return [
            (self.src, own, 0, pc.fwd),
            (self.src, own, 1, pc.bwd),
            (self.src, own, 2, part),
            (self.src, own, 3, far),
            (self.piece(pc.bwd), pc.bwd, 4, part),
            (self.piece(pc.fwd), pc.fwd, 5, part),
            (self.piece(far), far, 6, part),
        ]

    def start(self):
        def go():
            mv = self.moves()
            for k in (3, 0, 1, 2):
                self.copy(*mv[k]).start()

        self.guard(self.pc.rep, go)

    def arrive(self, rep):
        self.copy(self.piece(rep), rep, 0, self.pc.partner).wait_recv()

    def relay(self):
        mv = self.moves()

        def near():
            self.arrive(self.pc.bwd)
            self.copy(*mv[4]).start()

        self.guard(self.pc.bwd, near)

        def other():
            self.arrive(self.pc.fwd)
            self.copy(*mv[5]).start()

        self.guard(self.pc.fwd, other)

    def relay_far(self):
        far = self.pc.rep_at(2)

        def go():
            self.arrive(far)
            self.copy(*self.moves()[6]).start()

        self.guard(far, go)

    def finish(self):
        for dy in range(4):
            rep = ((self.pc.y + dy) % 4) * 2 + 1 - self.pc.c
            self.guard(rep, lambda rep=rep: self.arrive(rep))
        for mv in self.moves():
            self.guard(mv[1], lambda mv=mv: self.copy(*mv).wait_send())


class Scatter:
    def __init__(self, pc, src, got, total, side, ssem, rsem):
        self.pc, self.src, self.got, self.total, self.side, self.ssem, self.rsem = pc, src, got, total, side, ssem, rsem

    def copy(self, k):
        pc = self.pc
        y, d = pc.y, pc.d
        at = lambda dy: self.total.at[(y + dy + 4) % 4]
        src, dst, rep = (
            (self.src.at[1 - pc.c], self.got, pc.partner),
            (at(2), self.side.at[0], pc.rep_at(2)),
            (at(-d), self.side.at[1], pc.bwd),
            (at(d), self.side.at[2], pc.fwd),
        )[k]
        return rcopy(src, dst, self.ssem.at[k], self.rsem.at[k], pc.exp, rep)

    def start(self):
        self.copy(0).start()

    def add(self):
        self.copy(0).wait_recv()

        def body(k, _):
            self.total[k] = (self.src[self.pc.c, k].astype(F32) + self.got[k].astype(F32)).astype(self.total.dtype)
            return 0

        lax.fori_loop(0, 4, body, 0)
        for k in (1, 2, 3):
            self.copy(k).start()

    def result(self):
        for k in (1, 2, 3):
            self.copy(k).wait_recv()
        return self.total[self.pc.y].astype(F32) + sum(self.side[k].astype(F32) for k in range(3))

    def finish(self):
        for k in range(4):
            self.copy(k).wait_send()


def scatter_scratch(block, dtype):
    return [
        pltpu.VMEM((4,) + block, dtype),
        pltpu.VMEM((4,) + block, dtype),
        pltpu.VMEM((3,) + block, dtype),
        pltpu.SemaphoreType.DMA((4,)),
        pltpu.SemaphoreType.DMA((4,)),
    ]


def gather_scratch():
    return [pltpu.SemaphoreType.DMA((7,)), pltpu.SemaphoreType.DMA((REP,))]


def layer_kernel(
    latent, s_ref, gain_ref, wr_ref, routes_ref, wg_ref, wu_ref, wd_ref, gm_ref,
    mixed_ref, glat_ref, ggate_ref, gup_ref, gdown_ref,
    send, send_side, recv, recv_side, wfull, gp, gmine, gfull,
    h_prev, h_next, lat4, ptx, stem_ref, sg_hi, sg_lo,
    row32, side32, gm_all, hg_ref, dpre_ref,
    part, acc_l, acc_r, sums, ret32, send_back, back_in, bsum, back_all, slots, dp, tp, tmine, tfull, a_out, a_prev, a_next,
    *sems
):
    (g_got, g_tot, g_side, g_ss, g_rs, d_got, d_tot, d_side, d_ss, d_rs, t_got, t_tot, t_side, t_ss, t_rs,
     ag_ss, ag_rs, wg_ss, wg_rs, tg_ss, tg_rs, bg_ss, bg_rs, s0_ss, s0_rs, s1_ss, s1_rs,
     st_ss, st_rs, sd_ss, sd_rs, ln_ss, ln_rs, ca_ss, cl_rs, cr_rs, ct_ss, ct_rs, bk_ss, bo_ss, bk_rs,
     ha_ss, ha_rs, hb_ss, hb_rs, loc) = sems
    pc = Place()
    m = pc.m
    tok, dm = gm_ref.shape
    hid = wg_ref.shape[1]
    taps = s_ref.shape[0]
    wide = tok // 2
    top = routes_ref.shape[0]
    has_rows = pc.tile < TILES

    pc.greet()

    upper = (iota((tok, tok), 0) < iota((tok, tok), 1)).astype(BF)
    r_row = [routes_ref[k : k + 1, :] for k in range(top)]
    sel_row = [(iota((EXP, tok), 0) == r).astype(F32) for r in r_row]
    before_row = dot32((sel_row[0] + sel_row[1]).astype(BF), upper)
    pos_row = [jnp.sum(s * before_row, axis=0, keepdims=True).astype(I32) for s in sel_row]

    def here_id(pos, r):
        q = pos - ROWS * pc.tile
        return jnp.where((q >= 0) & (q < ROWS), r * ROWS + q, -1)

    def full_id(pos, r):
        t = lax.shift_right_logical(pos, 3)
        place = (r & 1) * (EXP // 2) + lax.shift_right_logical(r, 1)
        return t * (EXP * ROWS) + place * ROWS + (pos - t * ROWS)

    hot_here = [(iota((EXP * ROWS, tok), 0) == here_id(p, r)).astype(F32) for p, r in zip(pos_row, r_row)]
    hot_here_b = [h.astype(BF) for h in hot_here]
    picked_rows = dot32(hot_here_b[0] + hot_here_b[1], gm_ref[...])
    for e in range(EXP):
        send[e] = picked_rows[e * ROWS : (e + 1) * ROWS].astype(BF)

    gain = gain_ref[...].reshape(1, dm)
    dsl = wg_ref.shape[0]
    sg = s_ref[...].astype(F32) * gain
    hi, lo = split(sg)
    pick = (iota((dm, dsl), 0) == iota((dm, dsl), 1) + pc.rep * dsl).astype(BF)
    s_hi = dot32(hi, pick).astype(BF)
    s_lo = dot32(lo, pick).astype(BF)
    sg_hi[...] = s_hi
    sg_lo[...] = s_lo
    zero_taps = jnp.zeros((TAPS - taps, 2 * hid), F32)
    share = jnp.concatenate(
        [dot32(s_hi, w[...]) + dot32(s_lo, w[...]) for w in (wg_ref, wu_ref)], axis=1
    )
    share = jnp.concatenate([share, zero_taps], axis=0)
    for k in range(REP):
        gp[k // 4, k % 4] = share[k * TP : (k + 1) * TP]
    rproj = dot32(hi, wr_ref[...], NT) + dot32(lo, wr_ref[...], NT)

    pc.enter()

    ha = (
        rcopy(latent.at[1], h_prev, ha_ss.at[0], ha_rs.at[0], pc.exp + 1, pc.rep),
        rcopy(latent.at[0], h_next, ha_ss.at[1], ha_rs.at[1], pc.exp - 1, pc.rep),
    )
    first_row, last_row = pc.exp == 0, pc.exp == EXP * SH - 1
    pl.when(jnp.logical_not(last_row))(lambda: ha[0].start())
    pl.when(jnp.logical_not(first_row))(lambda: ha[1].start())

    def stage(k):
        peer = (pc.e + k) % EXP
        return rcopy(send.at[peer], recv.at[m, pc.tile], st_ss.at[k], st_rs.at[pc.tile], peer * SH + m, pc.rep)

    keep_gm = pltpu.make_async_copy(send.at[pc.e], recv.at[m, pc.tile], loc.at[0])

    @pl.when(has_rows)
    def _():
        for k in (1, 7, 2, 6, 3, 5, 4):
            stage(k).start()
        keep_gm.start()

    gather_w = Gather(pc, wd_ref, lambda rep: wfull.at[rep], wg_ss, wg_rs)
    own_w = pltpu.make_async_copy(wd_ref, wfull.at[pc.rep], loc.at[2])
    gather_w.start()
    own_w.start()

    scatter_g = Scatter(pc, gp, g_got, g_tot, g_side, g_ss, g_rs)
    scatter_g.start()

    @pl.when(jnp.logical_not(first_row))
    def _():
        rcopy(latent.at[1], h_prev, ha_ss.at[0], ha_rs.at[0], pc.exp, pc.partner).wait_recv()
        lat4[0] = h_prev[...].astype(F32)

    @pl.when(first_row)
    def _():
        lat4[0] = jnp.zeros(lat4.shape[1:], F32)

    @pl.when(jnp.logical_not(last_row))
    def _():
        rcopy(latent.at[0], h_next, ha_ss.at[1], ha_rs.at[1], pc.exp, pc.partner).wait_recv()
        lat4[3] = h_next[...].astype(F32)

    @pl.when(last_row)
    def _():
        lat4[3] = jnp.zeros(lat4.shape[1:], F32)

    lat4[1] = latent[0].astype(F32)
    lat4[2] = latent[1].astype(F32)
    chan = lat4.shape[1]
    col = iota((chan, tok), 1)
    col = jnp.where(col >= wide, col - wide, col)

    def shifted(v, by):
        if by == 0:
            return v
        rolled = pltpu.roll(v, (-by) % tok, 1)
        return jnp.where(col == (0 if by < 0 else wide - 1), 0.0, rolled)

    for i in range(3):
        two = jnp.concatenate([lat4[i], lat4[i + 1]], axis=1)
        for j in range(3):
            ptx[pl.ds((3 * i + j) * chan, chan), :] = shifted(two, j - 1)
    ptx[pl.ds(taps, SIDE - taps), :] = jnp.zeros((SIDE - taps, tok), F32)
    pt = ptx[pl.ds(0, taps), :]
    stem = dot32(pt.astype(BF), s_ref[...], TN).astype(BF)
    stem_ref[...] = stem
    sv = stem.astype(F32)
    rstd = lax.rsqrt(jnp.mean(sv * sv, axis=-1, keepdims=True) + 1e-06)
    rstd_row = jnp.transpose(jnp.broadcast_to(rstd, (tok, tok)))[0:1, :]
    normed = (sv * rstd * gain).astype(BF)
    logits = dot32(wr_ref[...], normed, NT)
    picked = [jnp.sum(s * logits, axis=0, keepdims=True) for s in sel_row]
    chosen = [jax.nn.sigmoid(p) for p in picked]
    total = chosen[0] + chosen[1]
    gates = [c / total for c in chosen]
    r_hi, r_lo = split(rstd_row)
    ptx[pl.ds(TAPS, 1), :] = r_hi.astype(F32)
    ptx[pl.ds(TAPS + 1, 1), :] = r_lo.astype(F32)
    side = jnp.zeros((EXP * ROWS, SIDE), F32)
    for k in range(top):
        k_hi, k_lo = split(gates[k])
        ptx[pl.ds(TAPS + 2, 1), :] = k_hi.astype(F32)
        ptx[pl.ds(TAPS + 3, 1), :] = k_lo.astype(F32)
        side = side + dot32(hot_here_b[k], ptx[...].astype(BF), NT)
    for e in range(EXP):
        send_side[e] = side[e * ROWS : (e + 1) * ROWS].astype(BF)

    scatter_g.add()

    def to_all(n):
        dest = (pc.exp + n) % (EXP * SH)
        e = dest // SH
        return rcopy(send_side.at[e], recv_side.at[m, pc.tile], sd_ss.at[e], sd_rs.at[m], dest, pc.rep)

    @pl.when(has_rows)
    def _():
        def body(n, _):
            to_all(n).start()
            return 0

        lax.fori_loop(1, EXP * SH, body, 0)
        pltpu.make_async_copy(send_side.at[pc.e], recv_side.at[m, pc.tile], sd_rs.at[m]).start()

    ends = (m < SH - 1, m > 0)

    def hop(way, p, c, s):
        at = pl.ds(CHUNKS[c][0], CHUNKS[c][1])
        ref = recv.at[p, at]
        return rcopy(ref, ref, ln_ss.at[way, s], ln_rs.at[p, c], pc.exp + 1 - 2 * way, pc.rep)

    def arrived(i):
        source = (5 * (pc.rep - i + 8)) % 8

        @pl.when(source != pc.e)
        def _():
            rcopy(recv.at[m, i], recv.at[m, i], st_ss.at[0], st_rs.at[i], pc.exp, pc.partner).wait_recv()

    def widen(p):
        for i in range(TILES):
            row32[pl.ds(pl.multiple_of(p * PIECE + i * ROWS, ROWS), ROWS), :] = recv[p, i].astype(F32)

    def step(s, _):
        for c in range(len(CHUNKS)):
            for way, p in ((0, m - s), (1, m + s)):
                ok = (p >= 0) if way == 0 else (p < SH)

                @pl.when(ok)
                def _():
                    hop(way, p, c, s).wait_recv()

                    @pl.when(ends[way])
                    def _():
                        hop(way, p, c, s).start()

        for way, p in ((0, m - s), (1, m + s)):
            pl.when((p >= 0) if way == 0 else (p < SH))(lambda p=p: widen(p))
        return 0

    @pl.when(has_rows)
    def _():
        keep_gm.wait()

    for c, (at, count) in enumerate(CHUNKS):
        for i in range(at, at + count):
            arrived(i)
        for way in range(2):
            pl.when(ends[way])(lambda way=way, c=c: hop(way, m, c, 0).start())
    gmine[...] = scatter_g.result()
    spot = lambda ref: lambda rep: ref.at[(rep % 2) * 4 + rep // 2]
    gather_g = Gather(pc, gmine, spot(gfull), ag_ss, ag_rs)
    own_g = pltpu.make_async_copy(gmine, spot(gfull)(pc.rep), loc.at[3])
    gather_g.start()
    own_g.start()
    widen(m)
    gather_w.relay()
    lax.fori_loop(1, 2, step, 0)
    gather_w.relay_far()
    gather_g.relay()
    gather_g.relay_far()
    lax.fori_loop(2, 3, step, 0)
    gather_g.finish()
    gather_w.finish()
    scatter_g.finish()
    own_w.wait()
    own_g.wait()

    def widen_side(p, _):
        pltpu.make_async_copy(recv_side.at[p], recv_side.at[p], sd_rs.at[p]).wait()
        for i in range(TILES):
            side32[pl.ds(pl.multiple_of(p * PIECE + i * ROWS, ROWS), ROWS), :] = recv_side[p, i].astype(F32)
        return 0

    lax.fori_loop(0, SH, widen_side, 0)
    more = side32[...]
    pr = more[:, :TAPS].astype(BF)
    rs = more[:, TAPS : TAPS + 1] + more[:, TAPS + 1 : TAPS + 2]
    gt = more[:, TAPS + 2 : TAPS + 3] + more[:, TAPS + 3 : TAPS + 4]
    g_hi, g_lo = split(gfull[...].reshape(TAPS, 2 * hid))
    pre = rs * (dot32(pr, g_hi) + dot32(pr, g_lo))
    pg, pu = pre[:, :hid], pre[:, hid:]
    sigma = jax.nn.sigmoid(pg)
    silu = pg * sigma
    hidden = silu * pu
    slope = pu * sigma * (1.0 + pg * (1.0 - sigma))
    hg = (gt * hidden).astype(BF)
    down_t = wfull[...].reshape(dm, hid)
    ret32[...] = dot32(hg, down_t, NT)
    hg_ref[...] = hg

    def give(way, p, c):
        at = pl.ds(CHUNKS[c][0], CHUNKS[c][1])
        dst, rsem = ((acc_l, cl_rs), (acc_r, cr_rs))[way]
        return rcopy(
            part.at[p, at], dst.at[p, at], ca_ss.at[p], rsem.at[p, c], pc.exp + 1 - 2 * way, pc.rep
        )

    def mine(p, i):
        return ret32[pl.ds(pl.multiple_of(p * PIECE + i * ROWS, ROWS), ROWS), :]

    def step_sum(tau, _):
        for c, (at, count) in enumerate(CHUNKS):
            for way, p in ((0, 7 - tau + m), (1, tau - 7 + m)):
                ok = (tau >= m) if way == 0 else (p >= 0)
                acc = (acc_l, acc_r)[way]

                @pl.when(ok & ends[1 - way])
                def _():
                    give(way, p, c).wait_recv()
                    for i in range(at, at + count):
                        part[p, i] = (mine(p, i) + acc[p, i].astype(F32)).astype(BF)

                @pl.when(ok & jnp.logical_not(ends[1 - way]))
                def _():
                    for i in range(at, at + count):
                        part[p, i] = mine(p, i).astype(BF)

                pl.when(ok & ends[way])(lambda: give(way, p, c).start())

        return 0

    def steps(at, to):
        lax.fori_loop(at, to, step_sum, 0)

    for n in range(5):
        steps(n, n + 1)
        lax.fori_loop(3 + n, 4 + n, step, 0)

    gm_all[...] = row32[...].astype(BF)
    u = dot32(gm_all[...], down_t)
    gg = jnp.sum(hidden * u, axis=-1, keepdims=True)
    gu = (rs * gt) * u
    dpre = jnp.concatenate([gu * slope, gu * silu], axis=1).astype(BF)
    dpre_ref[...] = dpre
    steps(5, 6)
    t_share = dot32(pr, dpre_ref[...], TN)
    for k in range(REP):
        tp[k // 4, k % 4] = t_share[k * TP : (k + 1) * TP]
    scatter_t = Scatter(pc, tp, t_got, t_tot, t_side, t_ss, t_rs)
    scatter_t.start()
    d_share = dot32(gm_all[...], hg_ref[...], TN)
    for k in range(REP):
        dp[k % 2, k // 2] = d_share[k * dsl : (k + 1) * dsl].astype(BF)
    scatter_d = Scatter(pc, dp, d_got, d_tot, d_side, d_ss, d_rs)
    scatter_d.start()
    back = dot32(dpre, g_hi, NT) + dot32(dpre, g_lo, NT)
    gg_hi = gg.astype(BF).astype(F32)
    lane = iota((SH * PIECE, SIDE - TAPS), 1)
    tail = jnp.where(lane == 0, gg_hi, jnp.where(lane == 1, gg - gg_hi, 0.0))
    side32[...] = jnp.concatenate([back, tail], axis=1)
    place = pc.half * (EXP // 2) + pc.x

    def source_of(i):
        return (5 * (pc.rep - i + 8)) % 8

    def reply(p, i, sem):
        return rcopy(send_back.at[p, i], back_in.at[m, place], sem, bk_rs.at[0], source_of(i) * SH + p, pc.rep)

    def narrow(n, _):
        p = (m + n) % SH
        for i in range(TILES):
            send_back[p, i] = side32[pl.ds(pl.multiple_of(p * PIECE + i * ROWS, ROWS), ROWS), :].astype(BF)
        for i in range(TILES):
            pl.when(p != m)(lambda i=i: reply(p, i, bk_ss.at[p]).start())

            @pl.when((p == m) & (source_of(i) != pc.e))
            def _():
                reply(p, i, bo_ss.at[i]).start()

            @pl.when((p == m) & (source_of(i) == pc.e))
            def _():
                pltpu.make_async_copy(send_back.at[p, i], back_in.at[m, place], bk_rs.at[0]).start()

        return 0

    lax.fori_loop(0, SH, narrow, 0)
    scatter_t.add()
    scatter_d.add()
    steps(6, 7)
    gather_t = Gather(pc, tmine, spot(tfull), tg_ss, tg_rs)
    own_t = pltpu.make_async_copy(tmine, spot(tfull)(pc.rep), loc.at[4])
    with_rows = lambda rep: pc.tile_of(rep) < TILES
    tile_at = lambda rep: pc.tile_of(rep) % TILES
    gather_b = Gather(pc, bsum, lambda rep: back_all.at[tile_at(rep)], bg_ss, bg_rs, with_rows)
    own_b = pltpu.make_async_copy(bsum, back_all.at[pc.tile % TILES], loc.at[1])

    def home(i):
        source = source_of(i)
        return source, rcopy(
            sums.at[i], slots.at[pc.half, i, pc.x], ct_ss.at[i], ct_rs.at[pc.half], source * SH + m, pc.rep
        )

    keep_out = lambda i: pltpu.make_async_copy(sums.at[i], slots.at[pc.half, i, pc.x], ct_rs.at[pc.half])
    for c, (at, count) in enumerate(CHUNKS):
        for way in range(2):
            pl.when(ends[1 - way])(lambda way=way, c=c: give(way, m, c).wait_recv())
        for i in range(at, at + count):
            @pl.when(m == 0)
            def _():
                sums[i] = (mine(m, i) + acc_r[m, i].astype(F32)).astype(BF)

            @pl.when(m == SH - 1)
            def _():
                sums[i] = (mine(m, i) + acc_l[m, i].astype(F32)).astype(BF)

            @pl.when(ends[0] & ends[1])
            def _():
                sums[i] = (mine(m, i) + acc_l[m, i].astype(F32) + acc_r[m, i].astype(F32)).astype(BF)

            source, copy = home(i)
            pl.when(source != pc.e)(lambda copy=copy: copy.start())
            pl.when(source == pc.e)(lambda i=i: keep_out(i).start())

    def out_gather(h, ss, rs):
        half = (pc.half + h) % 2
        ready = slots.at[half, pc.tile % TILES]
        gather = Gather(pc, ready, lambda rep: slots.at[half, tile_at(rep)], ss, rs, with_rows)
        wait = pltpu.make_async_copy(ready, ready, ct_rs.at[half])
        return half, gather, wait

    near_half, near, near_wait = out_gather(0, s0_ss, s0_rs)
    away_half, away, away_wait = out_gather(1, s1_ss, s1_rs)

    @pl.when(has_rows)
    def _():
        pltpu.make_async_copy(back_in, back_in, bk_rs.at[0]).wait()
        for k in range(EXP):
            bsum[k] = sum(back_in[j, k].astype(F32) for j in range(SH)).astype(BF)
        own_b.start()

    gather_b.start()
    tmine[...] = scatter_t.result()
    gather_t.start()
    own_t.start()
    pl.when(has_rows)(near_wait.wait)
    near.start()
    gather_b.relay()
    gather_t.relay()
    gather_b.relay_far()
    near.relay()
    gather_t.relay_far()
    near.relay_far()
    pl.when(has_rows)(away_wait.wait)
    away.start()
    gdown_ref[...] = scatter_d.result()
    pl.when(has_rows)(own_b.wait)
    gather_b.finish()

    for t in range(TILES):
        for k in range(EXP):
            side32[pl.ds((t * EXP + k) * ROWS, ROWS), :] = back_all[t, k].astype(F32)
    count = TILES * EXP * ROWS
    full_row = [full_id(p, r) for p, r in zip(pos_row, r_row)]
    hot_row = [(iota((count, tok), 0) == f).astype(F32) for f in full_row]
    tail = side32[...]
    gg_slot = tail[:, TAPS : TAPS + 1] + tail[:, TAPS + 1 : TAPS + 2]
    gg_row = [jnp.sum(h * gg_slot, axis=0, keepdims=True) for h in hot_row]
    b = dot32(tail.astype(BF), (hot_row[0] + hot_row[1]).astype(BF), TN)[:taps]
    mean = gg_row[0] * gates[0] + gg_row[1] * gates[1]
    grad_picked = [(g - mean) / total * (c * (1.0 - c)) for g, c in zip(gg_row, chosen)]
    grad_logits = sel_row[0] * grad_picked[0] + sel_row[1] * grad_picked[1]
    b = b + rstd_row * jnp.dot(rproj, grad_logits, precision=lax.Precision.HIGHEST, preferred_element_type=F32)
    c_row = jnp.sum(pt * b, axis=0, keepdims=True) * (rstd_row * rstd_row * (1.0 / dm))
    proj0 = dot32(s_ref[...], gm_ref[...], NT)
    proj1 = dot32(s_ref[...], stem_ref[...], NT)
    proj = proj0 + b - c_row * proj1
    rows3 = []
    for i in range(3):
        rows3.append(
            sum(shifted(proj[(3 * i + j) * chan : (3 * i + j + 1) * chan], 1 - j) for j in range(3))
        )
    a_out[0] = rows3[0][:, :wide]
    a_out[1] = rows3[2][:, wide:]
    hb = (
        rcopy(a_out.at[0], a_next, hb_ss.at[0], hb_rs.at[0], pc.exp - 1, pc.rep),
        rcopy(a_out.at[1], a_prev, hb_ss.at[1], hb_rs.at[1], pc.exp + 1, pc.rep),
    )
    pl.when(jnp.logical_not(first_row))(lambda: hb[0].start())
    pl.when(jnp.logical_not(last_row))(lambda: hb[1].start())
    glat_ref[0] = rows3[0][:, wide:] + rows3[1][:, :wide]
    glat_ref[1] = rows3[1][:, wide:] + rows3[2][:, :wide]

    @pl.when(jnp.logical_not(last_row))
    def _():
        rcopy(a_out.at[0], a_next, hb_ss.at[0], hb_rs.at[0], pc.exp, pc.partner).wait_recv()
        glat_ref[1] = glat_ref[1] + a_next[...]

    @pl.when(jnp.logical_not(first_row))
    def _():
        rcopy(a_out.at[1], a_prev, hb_ss.at[1], hb_rs.at[1], pc.exp, pc.partner).wait_recv()
        glat_ref[0] = glat_ref[0] + a_prev[...]

    away.relay()
    away.relay_far()
    gather_t.finish()
    own_t.wait()
    t_hi, t_lo = split(tfull[...].reshape(TAPS, 2 * hid)[:taps])
    gw = dot32(sg_hi[...], t_hi, TN) + dot32(sg_hi[...], t_lo, TN) + dot32(sg_lo[...], t_hi, TN)
    ggate_ref[...] = gw[:, :hid]
    gup_ref[...] = gw[:, hid:]
    square = [jnp.transpose(jnp.broadcast_to(f.astype(F32), (tok, tok)))[:, :1].astype(I32) for f in full_row]
    span = count // 2

    def out_of(half, gather):
        hot = jnp.zeros((tok, span), F32)
        for f in square:
            t = lax.shift_right_logical(f, 6)
            own = (lax.shift_right_logical(f, 5) & 1) == half
            at = jnp.where(own, t * (EXP // 2 * ROWS) + (f & 31), -1)
            hot = hot + (iota((tok, span), 1) == at).astype(F32)
        gather.finish()
        for t in range(TILES):
            for x in range(EXP // 2):
                ret32[pl.ds((t * (EXP // 2) + x) * ROWS, ROWS), :] = slots[half, t, x].astype(F32)
        return dot32(hot.astype(BF), ret32[pl.ds(0, span), :].astype(BF))

    sv_out = stem_ref[...].astype(F32) + out_of(near_half, near)

    for copy in (ha[1], hb[0]):
        pl.when(jnp.logical_not(first_row))(copy.wait_send)
    for copy in (ha[0], hb[1]):
        pl.when(jnp.logical_not(last_row))(copy.wait_send)
    scatter_t.finish()
    scatter_d.finish()

    @pl.when(has_rows)
    def _():
        for k in range(1, EXP):
            stage(k).wait_send()

        def body(k, _):
            rcopy(send_side, send_side, sd_ss.at[(pc.e + k) % EXP], sd_rs.at[0], pc.exp, pc.partner).wait_send()
            return 0

        lax.fori_loop(1, EXP, body, 0)
        seven = send_side.at[pl.ds(0, EXP - 1)]
        rcopy(seven, seven, sd_ss.at[pc.e], sd_rs.at[0], pc.exp, pc.partner).wait_send()

    def drain(s, _):
        for way, p in ((0, m - s), (1, m + s)):

            @pl.when(((p >= 0) if way == 0 else (p < SH)) & ends[way])
            def _():
                rcopy(recv.at[p], recv.at[p], ln_ss.at[way, s], ln_rs.at[p, 0], pc.exp, pc.partner).wait_send()

        for way, ok in ((0, s > m), (1, s < m)):

            @pl.when(ok & ends[way])
            def _():
                rcopy(part.at[s], acc_l.at[s], ca_ss.at[s], cl_rs.at[s, 0], pc.exp, pc.partner).wait_send()

        @pl.when(s != m)
        def _():
            rcopy(send_back.at[s], send_back.at[s], bk_ss.at[s], bk_rs.at[0], pc.exp, pc.partner).wait_send()

        return 0

    lax.fori_loop(0, SH, drain, 0)
    for i in range(TILES):

        @pl.when(source_of(i) != pc.e)
        def _():
            home(i)[1].wait_send()
            reply(m, i, bo_ss.at[i]).wait_send()

    mixed_ref[...] = (sv_out + out_of(away_half, away)).astype(BF)


def hand_over_kernel(*refs):
    half = len(refs) // 2
    for src, dst in zip(refs[:half], refs[half:]):
        dst[...] = src[...]


def local(latent, stem_weight, norm_gain, router_weight, routes, gate_weight, up_weight, down_weight, grad_mixed):
    tok, dm = grad_mixed.shape
    dsl, hid = gate_weight.shape
    rows_here, chan, wide = latent.shape
    taps = stem_weight.shape[0]
    dma = pltpu.SemaphoreType.DMA
    chunks = len(CHUNKS)
    v = pltpu.VMEM
    outs = pl.pallas_call(
        layer_kernel,
        out_shape=(
            jax.ShapeDtypeStruct((tok, dm), BF),
            jax.ShapeDtypeStruct((rows_here, chan, wide), F32),
            jax.ShapeDtypeStruct((dsl, hid), F32),
            jax.ShapeDtypeStruct((dsl, hid), F32),
            jax.ShapeDtypeStruct((dsl, hid), F32),
        ),
        in_specs=[VM] * 9,
        out_specs=(VM,) * 5,
        scratch_shapes=[
            v((EXP, ROWS, dm), BF),
            v((EXP, ROWS, SIDE), BF),
            v((SH, TILES, ROWS, dm), BF),
            v((SH, TILES, ROWS, SIDE), BF),
            v((REP, dsl, hid), BF),
            v((2, 4, TP, 2 * hid), F32),
            v((TP, 2 * hid), F32),
            v((REP, TP, 2 * hid), F32),
            v((chan, wide), BF),
            v((chan, wide), BF),
            v((4, chan, wide), F32),
            v((SIDE, tok), F32),
            v((tok, dm), BF),
            v((taps, dsl), BF),
            v((taps, dsl), BF),
            v((SH * PIECE, dm), F32),
            v((SH * PIECE, SIDE), F32),
            v((SH * PIECE, dm), BF),
            v((SH * PIECE, hid), BF),
            v((SH * PIECE, 2 * hid), BF),
            v((SH, TILES, ROWS, dm), BF),
            v((SH, TILES, ROWS, dm), BF),
            v((SH, TILES, ROWS, dm), BF),
            v((TILES, ROWS, dm), BF),
            v((SH * PIECE, dm), F32),
            v((SH, TILES, ROWS, SIDE), BF),
            v((SH, EXP, ROWS, SIDE), BF),
            v((EXP, ROWS, SIDE), BF),
            v((TILES, EXP, ROWS, SIDE), BF),
            v((2, TILES, EXP // 2, ROWS, dm), BF),
            v((2, 4, dsl, hid), BF),
            v((2, 4, TP, 2 * hid), F32),
            v((TP, 2 * hid), F32),
            v((REP, TP, 2 * hid), F32),
            v((2, chan, wide), F32),
            v((chan, wide), F32),
            v((chan, wide), F32),
        ]
        + scatter_scratch((TP, 2 * hid), F32)
        + scatter_scratch((dsl, hid), BF)
        + scatter_scratch((TP, 2 * hid), F32)
        + gather_scratch() * 6
        + [
            dma((EXP,)),
            dma((TILES,)),
            dma((EXP,)),
            dma((SH,)),
            dma((2, SH)),
            dma((SH, chunks)),
            dma((SH,)),
            dma((SH, chunks)),
            dma((SH, chunks)),
            dma((TILES,)),
            dma((2,)),
            dma((SH,)),
            dma((TILES,)),
            dma((1,)),
            dma((2,)),
            dma((2,)),
            dma((2,)),
            dma((2,)),
            dma((6,)),
        ],
        compiler_params=pltpu.CompilerParams(collective_id=0, has_side_effects=True),
        name="layer",
    )(
        latent, stem_weight, norm_gain, router_weight.T, routes.T,
        gate_weight, up_weight, down_weight.T, grad_mixed,
    )
    outs = pl.pallas_call(
        hand_over_kernel,
        out_shape=tuple(jax.ShapeDtypeStruct(o.shape, o.dtype) for o in outs),
        in_specs=[VM] * len(outs),
        out_specs=(VM,) * len(outs),
        name="hand_over",
    )(*outs)
    return tuple(outs[:4]) + (outs[4].T,)


def solution(mesh):
    return jax.shard_map(
        local,
        mesh=mesh,
        in_specs=(
            P("exp", None, None),
            P(),
            P(),
            P(),
            P("exp", None),
            P("rep", "exp"),
            P("rep", "exp"),
            P("exp", "rep"),
            P("exp", None),
        ),
        out_specs=(P("exp", None), P("exp", None, None), P("rep", "exp"), P("rep", "exp"), P("exp", "rep")),
        check_vma=False,
    )
```
